128 devices in a mesh: row: 16 (over z, y), col: 8 (over x, core).
Axes of the slice: x: 4, y: 4, z: 4, core: 2. Of those that a mesh axis runs over, the one named last changes fastest.
Arguments:
- delta: float32 [512, 8192], P('row', 'col'), may hold values from -4 to 4
- counts: int32 [8, 512, 8192], P(None, 'row', 'col'), may hold values from 0 to 32
- nbar: float32 [8], replicated, may hold values from 0.2 to 1
- bias: float32 [8], replicated, may hold values from 0.05 to 0.15
- owner: int32 [32768, 1], P(('row', 'col')), may hold values from 0 to 127; in each aligned block of 256 rows (0 to 255, 256 to 511, ...) at most 4 rows name the same one
- anchor_x: int32 [32768], P(('row', 'col')), may hold values from 0 to 29
- anchor_y: int32 [32768], P(('row', 'col')), may hold values from 0 to 59
- anchor_z: int32 [32768], P(('row', 'col')), may hold values from 0 to 15
Outputs:
- gradient: float32 [512, 8192], P('row', 'col')
- density: float32 [512, 8192], P('row', 'col')
The draws below stay inside these ranges and needn't reach their ends.
Inputs may be any that keep to these rules, and one draw needn't show every extreme that they name: Within the blocks of one device no owner is named more than 4 times, a bound that some block reaches.
All inputs are finite; a program needn't handle non-finite values.
Results may differ from the reference program's by a relative error of at most 0.0003.
Values sent between devices are 32-bit elements; how exact they have to be, the bound alone decides.
A program may use at most 192 MiB of HBM per device.

```python
import math
import jax
import jax.numpy as jnp
import numpy as np

GRID = 512
NBIN = 8
NZ = 16
BX = 2
BY = 4
BZ = 16
CX = 32
CY = 64
PB = 128
BLOCKS_DEV = 256
BLOCKS = 32768
CAP = 4
N_ROW = 16
N_COL = 8
DEVICES = 128


def draw_delta(key, part):
    draw_keys = jax.random.split(jax.random.fold_in(key, 11), 4)
    across = jnp.arange(GRID, dtype=jnp.int32)
    height = jnp.arange(NZ, dtype=jnp.int32)
    parity = (across[:, None] + across[None, :]) % 2
    checker = (1 - 2 * parity).astype(jnp.float32)
    offsets = jax.random.uniform(draw_keys[0], (3,), jnp.float32, 0.0, 2.0 * math.pi)
    circle = across.astype(jnp.float32) * (2.0 * math.pi / GRID)
    phase_xy = offsets[0] + 1.5 * jnp.cos(circle + offsets[1])[:, None] + 1.5 * jnp.cos(circle + offsets[2])[None, :]
    phase_z = (height % 16).astype(jnp.float32) * (2.0 * math.pi / 16.0)
    argument = phase_xy[:, :, None] + phase_z[None, None, :]
    plateau = jax.random.uniform(draw_keys[1], (), jnp.float32, 2.8, 3.2)
    jitter = 0.3 * jax.random.normal(draw_keys[2], (GRID, GRID, NZ), jnp.float32)
    wobble = jax.random.uniform(draw_keys[3], (), jnp.float32, 0.4, 0.6)
    sample = checker[:, :, None] * (plateau + wobble * jnp.cos(argument)) + jitter
    return jnp.clip(sample, -4.0, 4.0).reshape(GRID, GRID * NZ)


def touch_ends(entries, key, smallest, top_value):
    longest = entries.shape.index(max(entries.shape))
    spots = []
    for shift in (0, 1):
        where = [jax.random.randint(jax.random.fold_in(key, axis), (), 0, length) for axis, length in enumerate(entries.shape)]
        where[longest] = (where[longest] + shift) % entries.shape[longest]
        spots.append(tuple(where))
    return entries.at[spots[0]].set(smallest).at[spots[1]].set(top_value)


def deal_out(key, own, number, rows, amount, top, limit, lean):
    ranking = jax.random.permutation(key, amount)
    packed, common = portions_of(amount, rows * top, limit, lean, True), portions_of(amount, rows * top, limit, lean, False)
    places = jnp.arange(amount)

    def named(lengths, turn):
        used = int((lengths > 0).sum())
        fixed = max(1, used // 4)
        passed = fixed + (places - fixed + turn * (used - fixed)) % max(1, amount - fixed)
        return jnp.zeros((amount,), jnp.int32).at[ranking[jnp.where(places < fixed, places, passed)]].set(jnp.asarray(lengths, jnp.int32))

    lengths = jnp.where(number % 4 == 0, named(packed, number // 4), named(common, number - number // 4 - 1))
    mixed = jax.random.permutation(jax.random.fold_in(own, 3), amount)
    source_of, taker = mixed[0:amount // 2 * 2:2], mixed[1:amount // 2 * 2:2]
    margin = jnp.minimum(lengths[source_of] - 1, limit - lengths[taker]) // 2
    margin = jnp.where((source_of == ranking[0]) | (taker == ranking[0]) | (lengths[taker] == 0), 0, jnp.maximum(margin, 0))
    passed = jax.random.randint(jax.random.fold_in(own, 4), (amount // 2,), 0, 1 << 20) % (margin + 1)
    lengths = lengths.at[source_of].add(-passed).at[taker].add(passed)
    members = jnp.searchsorted(jnp.cumsum(lengths), jnp.arange(rows * top), side="right").astype(jnp.int32)
    grid = members.reshape(top, rows).T
    grid = grid[jax.random.permutation(jax.random.fold_in(own, 1), rows)]
    turn = jax.random.randint(jax.random.fold_in(own, 2), (rows, 1), 0, top)
    return jnp.take_along_axis(grid, (jnp.arange(top)[None, :] + turn) % top, axis=1)


def portions_of(count, total, bound, lean, full):
    portions = [(1 << 20) // math.isqrt(rank ** lean) + 1 for rank in range(1, count + 1)]
    largest = bound if full else min(bound, max(-(-total // count), total * portions[0] // sum(portions)))
    least = 1 if total - largest >= count - 1 else 0
    given, rest = [largest] + [least] * (count - 1), total - largest - least * (count - 1)
    while rest > 0:
        candidates = [i for i in range(1, count) if given[i] < largest] or [i for i in range(1, count) if given[i] < bound]
        mass, remaining = sum([portions[i] for i in candidates]), rest
        for i in candidates:
            extra = min(bound - given[i], max(1, remaining * portions[i] // mass), rest)
            given[i] = given[i] + extra
            rest = rest - extra
    return np.array(given)


def setup_inputs(seed: int = 0) -> dict:
    key_list = jax.random.split(jax.random.key(seed), 9)
    delta = draw_delta(jax.random.fold_in(key_list[8], 71), 0)
    counts = touch_ends(jax.random.randint(key_list[1], (NBIN, GRID, GRID * NZ), 0, 33), jax.random.fold_in(key_list[1], 1), 0, 32).astype(jnp.int32)
    nbar = jnp.clip(jnp.exp(jax.random.uniform(key_list[2], (NBIN,), jnp.float32, math.log(0.2), math.log(1.0))), 0.2, 1.0)
    bias = jnp.clip(jax.random.uniform(key_list[3], (NBIN,), jnp.float32, 0.05, 0.15), 0.05, 0.15)
    owner_keys = jax.random.split(jax.random.fold_in(key_list[4], 1), BLOCKS // BLOCKS_DEV)
    owner_turns = jax.random.permutation(jax.random.fold_in(key_list[4], 3), BLOCKS // BLOCKS_DEV)
    owner = jax.vmap(lambda own, number: deal_out(jax.random.fold_in(key_list[4], 2), own, number, BLOCKS_DEV, DEVICES, 1, CAP, 2))(owner_keys, owner_turns).reshape((BLOCKS, 1))
    anchor_x = touch_ends(jax.random.randint(key_list[5], (BLOCKS,), 0, CX - BX), jax.random.fold_in(key_list[5], 1), 0, (CX - BX) - 1).astype(jnp.int32)
    anchor_y = touch_ends(jax.random.randint(key_list[6], (BLOCKS,), 0, CY - BY), jax.random.fold_in(key_list[6], 1), 0, (CY - BY) - 1).astype(jnp.int32)
    anchor_z = touch_ends(jax.random.randint(key_list[7], (BLOCKS,), 0, NZ), jax.random.fold_in(key_list[7], 1), 0, NZ - 1).astype(jnp.int32)
    return dict(delta=delta, counts=counts, nbar=nbar, bias=bias, owner=owner, anchor_x=anchor_x, anchor_y=anchor_y, anchor_z=anchor_z)


SECOND_ORDER = 3.0 / 7.0

def wave_square(length):
    number = jnp.fft.fftfreq(length).astype(jnp.float32) * (2.0 * math.pi)
    return number * number

def poisson(source):
    wave_x = wave_square(GRID)
    wave_z = wave_square(NZ)
    total = wave_x[:, None, None] + wave_x[None, :, None] + wave_z[None, None, :]
    safe = jnp.where(total > 0, total, jnp.ones_like(total))
    factor = jnp.where(total > 0, -1.0 / safe, jnp.zeros_like(total))
    return jnp.fft.ifftn(jnp.fft.fftn(source) * factor).real.astype(source.dtype)

def ahead(array, axis):
    return jnp.roll(array, -1, axis=axis)

def behind(array, axis):
    return jnp.roll(array, 1, axis=axis)

def slope(array, axis):
    return (ahead(array, axis) - behind(array, axis)) * 0.5

def bend(array, axis):
    return ahead(array, axis) - 2.0 * array + behind(array, axis)

def twist(array, first_axis, other_axis):
    differ = ahead(array, first_axis) - behind(array, first_axis)
    return (ahead(differ, other_axis) - behind(differ, other_axis)) * 0.25

def paint(delta, owner, anchor_x, anchor_y, anchor_z):
    field = delta.reshape(GRID, GRID, NZ)
    first = poisson(field)
    along_xx = bend(first, 0)
    along_yy = bend(first, 1)
    along_zz = bend(first, 2)
    along_xy = twist(first, 0, 1)
    along_xz = twist(first, 0, 2)
    along_yz = twist(first, 1, 2)
    source = along_xx * along_yy + along_xx * along_zz + along_yy * along_zz - along_xy * along_xy - along_xz * along_xz - along_yz * along_yz
    total = first + SECOND_ORDER * poisson(source)
    shift = jnp.stack([0.5 - slope(total, 0), 0.5 - slope(total, 1), 0.5 - slope(total, 2)])
    blocks = shift.reshape(3, N_ROW, CX // BX, BX, N_COL, CY // BY, BY, NZ // BZ, BZ)
    blocks = blocks.transpose(1, 4, 2, 5, 7, 0, 3, 6, 8).reshape(BLOCKS, 3, PB)
    target = owner[:, 0]
    particle = jnp.arange(PB, dtype=jnp.int32)
    step_x = particle // (BY * BZ)
    step_y = particle // BZ % BY
    step_z = particle % BZ
    base_x = (target // N_COL * CX + anchor_x)[:, None] + step_x[None, :]
    base_y = (target % N_COL * CY + anchor_y)[:, None] + step_y[None, :]
    base_z = anchor_z[:, None] + step_z[None, :]
    pairs_x = (1.0 - blocks[:, 0], blocks[:, 0])
    pairs_y = (1.0 - blocks[:, 1], blocks[:, 1])
    pairs_z = (1.0 - blocks[:, 2], blocks[:, 2])
    cells = []
    shares = []
    for corner in range(8):
        up_x = corner // 4
        up_y = corner // 2 % 2
        up_z = corner % 2
        cells.append(((base_x + up_x) * GRID + base_y + up_y) * NZ + (base_z + up_z) % NZ)
        shares.append(pairs_x[up_x] * pairs_y[up_y] * pairs_z[up_z])
    flat = jnp.zeros((GRID * GRID * NZ,), blocks.dtype)
    flat = flat.at[jnp.stack(cells).reshape(-1)].add(jnp.stack(shares).reshape(-1))
    return flat.reshape(GRID, GRID * NZ)

def reference(delta, counts, nbar, bias, owner, anchor_x, anchor_y, anchor_z):
    number = counts.astype(jnp.float32)

    def loglike(field):
        density = paint(field, owner, anchor_x, anchor_y, anchor_z)
        contrast = density - 1.0
        rate = nbar[:, None, None] * jnp.exp(bias[:, None, None] * contrast[None])
        return (jnp.sum(number * bias[:, None, None] * contrast[None] - rate), density)
    value, pullback, density = jax.vjp(loglike, delta, has_aux=True)
    gradient = pullback(jnp.ones_like(value))[0]
    return (gradient, density)
```

```python
import functools
import math

import jax
import jax.numpy as jnp
import numpy as np
from jax import lax
from jax.experimental import pallas as pl
from jax.experimental.pallas import tpu as pltpu
from jax.sharding import PartitionSpec as P

GRID, NZ = 512, 16
NROW, NCOL = 16, 8
CX, CY = 32, 64
NBIN = 8
XH = 40
SECOND_ORDER = 3.0 / 7.0
F32, BF16 = jnp.float32, jnp.bfloat16
MESH = pl.DeviceIdType.MESH


def real_basis(n):
    k = np.arange(n)
    rows = []
    for m in range(n):
        if m == 0:
            rows.append(np.full(n, 1.0 / math.sqrt(n)))
        elif m < n // 2:
            rows.append(math.sqrt(2.0 / n) * np.cos(2 * np.pi * (m * k % n) / n))
        elif m == n // 2:
            rows.append((1.0 - 2.0 * (k % 2)) / math.sqrt(n))
        else:
            rows.append(math.sqrt(2.0 / n) * np.sin(2 * np.pi * ((m - n // 2) * k % n) / n))
    return np.stack(rows)


def two_terms(table):
    table = table.astype(np.float32)
    high = table.astype(jnp.bfloat16)
    low = (table - high.astype(np.float32)).astype(jnp.bfloat16)
    return high, low


def make_tables():
    basis = real_basis(GRID)
    r, i = np.divmod(np.arange(256), 16)
    first, second = 32 * r + i, 32 * r + 16 + i
    c, k = np.divmod(np.arange(256), 32)
    low, high = 64 * c + k, 64 * c + 32 + k
    fx = np.concatenate(
        [
            basis[low][:, first],
            basis[high][:, second],
            basis[high][:, first],
            basis[low][:, second],
        ]
    )
    fy = basis.T
    gy = np.zeros((GRID, NCOL, 128))
    for c in range(NCOL):
        gy[:, c, :68] = basis[:, (CY * c - 2 + np.arange(68)) % GRID]
    gx = np.zeros((NROW, XH, GRID))
    for r in range(NROW):
        gx[r, :36] = basis[:, (CX * r - 2 + np.arange(36)) % GRID].T
    tables = []
    for t in (fx, fy, gy.reshape(GRID, NCOL * 128), gx.reshape(NROW * XH, GRID)):
        tables.extend(two_terms(t))
    return tables


ZB = real_basis(NZ)


def box_lane(a, b, z):
    if a == 0:
        return b * 16 + z
    if a == 2:
        return 128 + b * 16 + z
    return 80 + b * 16 + z if b < 3 else 208 + (b - 3) * 16 + z


def make_spread():
    e = np.zeros((4, 128, 256), np.float32)
    for dx in range(2):
        for dy in range(2):
            for v in range(4):
                for u in range(2):
                    for z in range(16):
                        e[dx * 2 + dy, 32 * v + 16 * u + z, box_lane(u + dx, v + dy, z)] = 1.0
    return e.reshape(512, 256)


def dot(a, b):
    return lax.dot_general(a, b, (((1,), (0,)), ((), ())), preferred_element_type=F32)


def split(x):
    high = x.astype(BF16)
    return high, (x - high.astype(F32)).astype(BF16)


def split_3(x):
    high = x.astype(BF16)
    rest = x - high.astype(F32)
    middle = rest.astype(BF16)
    return high, middle, (rest - middle.astype(F32)).astype(BF16)


def left_product(high, low, b):
    n = b.shape[1]
    b0, b1, b2 = split_3(b)
    pair = jnp.concatenate([b0, b1], axis=1)
    t = dot(high, pair)
    s = dot(low, pair)
    return t[:, :n] + ((t[:, n:] + s[:, :n]) + (s[:, n:] + dot(high, b2)))


def right_product(a, high, low):
    m = a.shape[0]
    a0, a1, a2 = split_3(a)
    pair = jnp.concatenate([a0, a1], axis=0)
    t = dot(jnp.concatenate([pair, a2], axis=0), high)
    s = dot(pair, low)
    return t[:m] + ((t[m : 2 * m] + s[:m]) + (s[m:] + t[2 * m :]))


def exact_left(zero_one, b):
    n = b.shape[1]
    t = dot(zero_one, jnp.concatenate(split(b), axis=1))
    return t[:, :n] + t[:, n:]


def exact_right(a, zero_one):
    m = a.shape[0]
    t = dot(jnp.concatenate(split(a), axis=0), zero_one)
    return t[:m] + t[m:]


def lanes(shape, axis=1):
    return lax.broadcasted_iota(jnp.int32, shape, axis)


def roll(x, shift, axis):
    shift = shift % x.shape[axis]
    return x if shift == 0 else pltpu.roll(x, shift, axis)


def up(x, axis):
    return roll(x, -1, axis)


def down(x, axis):
    return roll(x, 1, axis)


def forward_z(v):
    even = [v[0]] + [v[z] + v[16 - z] for z in range(1, 8)] + [v[8]]
    odd = [None] + [v[z] - v[16 - z] for z in range(1, 8)]
    out = []
    for m in range(9):
        s = even[0] * float(ZB[m, 0])
        for z in range(1, 9):
            s = s + even[z] * float(ZB[m, z])
        out.append(s)
    for m in range(9, 16):
        s = odd[1] * float(ZB[m, 1])
        for z in range(2, 8):
            s = s + odd[z] * float(ZB[m, z])
        out.append(s)
    return out


def inverse_z(v):
    out = [None] * 16
    for z in range(9):
        even = v[0] * float(ZB[0, z])
        for m in range(1, 9):
            even = even + v[m] * float(ZB[m, z])
        if z in (0, 8):
            out[z] = even
            continue
        odd = v[9] * float(ZB[9, z])
        for m in range(10, 16):
            odd = odd + v[m] * float(ZB[m, z])
        out[z] = even + odd
        out[16 - z] = even - odd
    return out


def exchange(n, me, axis, src, dst, send, recv, own):
    sends, recvs = [], []
    for k in range(1, n):
        peer = lax.rem(me + k, n)
        origin = lax.rem(me + n - k, n)
        copy = pltpu.make_async_remote_copy(
            src_ref=src.at[peer],
            dst_ref=dst.at[me],
            send_sem=send.at[k],
            recv_sem=recv.at[k],
            device_id={axis: peer},
            device_id_type=MESH,
        )
        copy.start()
        sends.append(copy)
        recvs.append(
            pltpu.make_async_remote_copy(
                src_ref=src.at[peer],
                dst_ref=dst.at[origin],
                send_sem=send.at[k],
                recv_sem=recv.at[k],
                device_id={axis: peer},
                device_id_type=MESH,
            )
        )
    copy = pltpu.make_async_copy(src.at[me], dst.at[me], own)
    copy.start()
    return sends, recvs, copy


def arrive(state):
    state[2].wait()
    for copy in state[1]:
        copy.wait_recv()


def poisson_kernel(
    src, *refs
):
    tables = refs[:8]
    out = refs[8]
    mo, r1, pk, r2, zb, r3, xb, r4 = refs[9:17]
    held = refs[17:25]
    tsem, s1, q1, s2, q2, s3, q3, s4, q4, own = refs[25:]
    row, col = lax.axis_index("row"), lax.axis_index("col")

    barrier = pltpu.get_barrier_semaphore()
    for k in range(1, NROW):
        pl.semaphore_signal(
            barrier, inc=1, device_id={"row": lax.rem(row + k, NROW)}, device_id_type=MESH
        )
    for k in range(1, NCOL):
        pl.semaphore_signal(
            barrier, inc=1, device_id={"col": lax.rem(col + k, NCOL)}, device_id_type=MESH
        )
    loads = [
        pltpu.make_async_copy(t, h, tsem.at[i]) for i, (t, h) in enumerate(zip(tables, held))
    ]
    for load in loads:
        load.start()
    for s in range(2):
        rows = pl.ds(8 * s, 8)
        for m, value in enumerate(forward_z([src[z, rows, :] for z in range(16)])):
            mo[m, rows, :] = value
    pl.semaphore_wait(barrier, NROW + NCOL - 2)

    low_half = lanes((256, 128)) < 64
    state1 = exchange(NROW, row, "row", mo, r1, s1, q1, own.at[0])
    for load in loads:
        load.wait()
    fxh, fxl, fyh, fyl, gyh, gyl, gxh, gxl = held

    kx = lanes((64, GRID), 0) + col * 64
    ky = lanes((64, GRID), 1)
    kx = jnp.where(kx <= GRID // 2, kx, kx - GRID // 2).astype(F32) * (2.0 * math.pi / GRID)
    ky = jnp.where(ky <= GRID // 2, ky, ky - GRID // 2).astype(F32) * (2.0 * math.pi / GRID)
    kz = jnp.where(row <= NZ // 2, row, row - NZ // 2)
    kz = jnp.full((64, GRID), kz, jnp.int32).astype(F32) * (2.0 * math.pi / NZ)
    square = kx * kx + ky * ky + kz * kz
    factor = jnp.where(square > 0, -1.0 / jnp.where(square > 0, square, 1.0), 0.0)

    arrive(state1)
    t = left_product(fxh[...], fxl[...], r1[...].reshape(256, 128))
    packed = jnp.where(low_half, t[:256], t[256:512]) + roll(
        jnp.where(low_half, t[512:768], t[768:]), 64, 1
    )
    pk[...] = packed.reshape(NCOL, 32, 128)
    state2 = exchange(NCOL, col, "col", pk, r2, s2, q2, own.at[1])
    arrive(state2)
    half = lanes((32, 128)) < 64
    top, bottom = [], []
    for p in range(4):
        a, b = r2[2 * p], r2[2 * p + 1]
        top.append(jnp.where(half, a, roll(b, 64, 1)))
        bottom.append(jnp.where(half, roll(a, 64, 1), b))
    full = jnp.concatenate(
        [jnp.concatenate(top, axis=1), jnp.concatenate(bottom, axis=1)], axis=0
    )
    modes = right_product(full, fyh[...], fyl[...]) * factor
    back = right_product(modes, gyh[...], gyl[...])
    for c in range(NCOL):
        zb[c] = back[:, 128 * c : 128 * (c + 1)]
    state3 = exchange(NCOL, col, "col", zb, r3, s3, q3, own.at[2])
    arrive(state3)
    xb[...] = left_product(gxh[...], gxl[...], r3[...].reshape(GRID, 128)).reshape(NROW, XH, 128)
    state4 = exchange(NROW, row, "row", xb, r4, s4, q4, own.at[3])
    arrive(state4)
    for s in range(5):
        rows = pl.ds(8 * s, 8)
        for z, value in enumerate(inverse_z([r4[m, rows, :] for m in range(16)])):
            out[z, rows, :] = value
    for state in (state1, state2, state3, state4):
        for copy in state[0]:
            copy.wait_send()


VM = pl.BlockSpec(memory_space=pltpu.VMEM)
ANY = pl.BlockSpec(memory_space=pl.ANY)


def poisson(src, tables):
    buffers = [(NROW, 16, 128), (NCOL, 32, 128), (NCOL, 64, 128), (NROW, XH, 128)]
    scratch = []
    for shape in buffers:
        scratch += [pltpu.VMEM(shape, F32), pltpu.VMEM(shape, F32)]
    scratch += [pltpu.VMEM(t.shape, BF16) for t in tables]
    scratch += [pltpu.SemaphoreType.DMA((8,))]
    for n in (NROW, NCOL, NCOL, NROW):
        scratch += [pltpu.SemaphoreType.DMA((n,)), pltpu.SemaphoreType.DMA((n,))]
    scratch += [pltpu.SemaphoreType.DMA((4,))]
    return pl.pallas_call(
        poisson_kernel,
        out_shape=jax.ShapeDtypeStruct((NZ, XH, 128), F32),
        in_specs=[VM] + [ANY] * 8,
        out_specs=VM,
        scratch_shapes=scratch,
        compiler_params=pltpu.CompilerParams(
            collective_id=0, has_side_effects=True, vmem_limit_bytes=40 << 20
        ),
        name="poisson",
    )(src, *tables)


def pack(f):
    f = roll(f, -2, 0)
    low = roll(f[0:16], -2, 1)
    high = roll(f[16:32], 62, 1)
    return jnp.where(lanes((16, 128)) < 64, low, high)


def curvatures(below, here, above):
    xx = up(here, 0) - 2.0 * here + down(here, 0)
    yy = up(here, 1) - 2.0 * here + down(here, 1)
    zz = above - 2.0 * here + below
    dx = up(here, 0) - down(here, 0)
    dz = above - below
    xy = (up(dx, 1) - down(dx, 1)) * 0.25
    xz = (up(dz, 0) - down(dz, 0)) * 0.25
    yz = (up(dz, 1) - down(dz, 1)) * 0.25
    return xx, yy, zz, xy, xz, yz


def source_kernel(first, out):
    @pl.loop(0, NZ)
    def _(z):
        xx, yy, zz, xy, xz, yz = curvatures(
            first[(z + 15) % 16], first[z], first[(z + 1) % 16]
        )
        out[z] = pack(xx * yy + xx * zz + yy * zz - xy * xy - xz * xz - yz * yz)


def group_roll(x, s):
    z = lanes(x.shape) % 16
    return jnp.where(z >= s, roll(x, s, 1), roll(x, s - 16, 1))


def barrel(x, amount):
    for bit in (1, 2, 4, 8):
        x = jnp.where((amount & bit) > 0, group_roll(x, bit), x)
    return x


def barrel_16(x, amount):
    for bit in (1, 2, 4):
        x = jnp.where((amount & bit) > 0, roll(x, 16 * bit, 1), x)
    return x


def slots(owner_row, owner_col):
    device = lanes((128, 256), 0)
    chosen_t = jnp.where(device == owner_row, 1.0, 0.0)
    order = jnp.where(lanes((256, 256), 0) < lanes((256, 256), 1), 1.0, 0.0)
    earlier_t = dot(chosen_t.astype(BF16), order.astype(BF16))
    along = jnp.sum(earlier_t * chosen_t, axis=0, keepdims=True)
    along = owner_row * 8 + along.astype(jnp.int32)
    chosen = jnp.where(lanes((256, 128)) == owner_col, 1.0, 0.0)
    order = jnp.where(lanes((256, 256), 0) > lanes((256, 256), 1), 1.0, 0.0)
    earlier = dot(order.astype(BF16), chosen.astype(BF16))
    down_ = jnp.sum(earlier * chosen, axis=1, keepdims=True)
    down_ = owner_col * 8 + down_.astype(jnp.int32)
    return along, down_


def paint_kernel(first, second, owner_row, owner_col, ax, ay, az, spread, out, fracs, tz, tt):
    zrows = [None, None, None]
    piece = lanes((16, 128)) // 32
    for axis in range(3):

        @pl.loop(0, NZ)
        def _(z, axis=axis):
            def total(k):
                return first[k] + SECOND_ORDER * second[k]

            if axis == 2:
                slope = total((z + 1) % 16) - total((z + 15) % 16)
            else:
                here = total(z)
                slope = up(here, axis) - down(here, axis)
            value = 0.5 - 0.5 * slope
            value = roll(roll(value, -2, 0)[0:32], -2, 1)
            tz[pl.ds(z, 32, stride=16), :] = value

        for q in range(4):
            tt[q] = jnp.transpose(tz[pl.ds(128 * q, 128), :])[0:64]
        for q in range(4):
            quarter = [tt[q, pl.ds(v, 16, stride=4), :] for v in range(4)]
            for k in range(4):
                block = roll(quarter[0], -32 * k, 1)
                for v in range(1, 4):
                    block = jnp.where(piece == v, roll(quarter[v], 32 * (v - k), 1), block)
                fracs[axis, pl.ds(16 * (4 * q + k), 16), :] = block
    amount = az[...]
    for axis in range(3):
        fracs[axis] = barrel(fracs[axis], amount)
    fx, fy, fz = fracs[0], fracs[1], fracs[2]
    fields = []
    for wx in (1.0 - fx, fx):
        for wy in (1.0 - fy, fy):
            q = wx * wy
            upper = q * fz
            fields.append(q - upper + group_roll(upper, 1))
    box = exact_right(jnp.concatenate(fields, axis=1), spread[...])
    lane = lanes((256, 256))
    box = jnp.where(lane == 240, ax[...].astype(F32), box)
    box = jnp.where(lane == 241, ay[...].astype(F32), box)
    along, _ = slots(owner_row[...], owner_col[...])
    target = jnp.concatenate([along, along + 4], axis=1)
    table = jnp.where(lanes((1024, 512), 0) == target, 1.0, 0.0).astype(BF16)
    stacked = jnp.concatenate([box[:, :128], box[:, 128:]], axis=0)
    out[...] = exact_left(table, stacked)


def owner_kernel(nbar, bias, arrived, counts, density, back, dens, pulls):
    data = arrived[...]
    second = lanes((1024, 128), 0) // 4 % 2
    is_second = second == 1

    def both(lane):
        column = jnp.broadcast_to(data[:, lane : lane + 1], (1024, 128))
        return jnp.where(is_second, column, roll(column, -4, 0)).astype(jnp.int32)

    ax, ay = both(112), both(113)
    flipped = jnp.concatenate(
        [jnp.transpose(data[128 * i : 128 * (i + 1)]) for i in range(8)], axis=1
    )
    second_row = lanes((1, 1024)) // 4 % 2

    def both_row(lane):
        line = flipped[lane : lane + 1]
        line = jnp.where(second_row == 1, line, roll(line, -4, 1))
        return line.astype(jnp.int32)

    ax_row, ay_row = both_row(112), both_row(113)
    base_row = (ay_row >> 3) * 32 + ax_row
    base = (ay >> 3) * 32 + ax
    lane = lanes((1024, 128))
    step = ay & 7
    side_step = (3 * second + 3 + ay) & 7
    stay = lane >= step * 16
    main = barrel_16(jnp.where(lane < 80, data, 0.0), step)
    side_mask = (lane >= 80) & (lane < 112 + 16 * (1 - second))
    side = barrel_16(jnp.where(side_mask, data, 0.0), side_step)
    total = None
    for part, offset in ((main, 2 * second_row), (side, 1)):
        table = jnp.where(lanes((256, 1024), 0) == base_row + offset, 1.0, 0.0).astype(BF16)
        near = split(jnp.where(stay, part, 0.0))
        far = split(jnp.where(stay, 0.0, part))
        t = dot(table, jnp.concatenate([*near, *far], axis=1))
        total = t if total is None else total + t
    near = total[:, :128] + total[:, 128:256]
    far = total[:, 256:384] + total[:, 384:]
    dens[...] = near + jnp.where(lanes((256, 128), 0) >= 32, roll(far, 32, 0), 0.0)
    for j in range(8):
        here = dens[pl.ds(32 * j, 32), :]
        density[:, pl.ds(128 * j, 128)] = here
        contrast = here - 1.0
        pull = jnp.zeros((32, 128), F32)
        for b in range(NBIN):
            rate = nbar[b] * jnp.exp(bias[b] * contrast)
            number = counts[b, :, pl.ds(128 * j, 128)].astype(F32)
            pull = pull + bias[b] * (number - rate)
        pulls[pl.ds(32 * j, 32), :] = pull
    pull = pulls[...]
    ahead = jnp.where(lanes((256, 128), 0) < 224, roll(pull, -32, 0), 0.0)
    both_pulls = jnp.concatenate([*split(pull), *split(ahead)], axis=1)

    def picked(offset, amount):
        wide = jnp.concatenate([base + offset, base + offset], axis=1)
        table = jnp.where(lanes((1024, 256)) == wide, 1.0, 0.0).astype(BF16)
        t = dot(table, both_pulls)
        value = jnp.where(stay, t[:, :128] + t[:, 128:256], t[:, 256:384] + t[:, 384:])
        return barrel_16(value, (8 - amount) & 7)

    back[...] = jnp.where(lane < 80, picked(2 * second, step), picked(1, side_step))


def force_kernel(returned, owner_row, owner_col, az, spread_t, fracs, fx_out, fy_out, fz_out):
    _, place = slots(owner_row[...], owner_col[...])
    target = jnp.concatenate([place, place + 4], axis=0)
    table = jnp.where(lanes((512, 1024)) == target, 1.0, 0.0).astype(BF16)
    t = exact_left(table, returned[...])
    box = jnp.concatenate([t[:256], t[256:]], axis=1)
    corner = exact_right(box, spread_t[...])
    fx, fy, fz = fracs[0], fracs[1], fracs[2]
    along, across = [], []
    for d in range(4):
        here = corner[:, 128 * d : 128 * (d + 1)]
        change = group_roll(here, 15) - here
        along.append(here + fz * change)
        across.append(change)
    amount = (16 - az[...]) & 15
    force_x = (1.0 - fy) * (along[2] - along[0]) + fy * (along[3] - along[1])
    force_y = (1.0 - fx) * (along[1] - along[0]) + fx * (along[3] - along[2])
    force_z = (1.0 - fx) * ((1.0 - fy) * across[0] + fy * across[1]) + fx * (
        (1.0 - fy) * across[2] + fy * across[3]
    )
    piece = lanes((16, 128)) // 32
    for force, out in ((force_x, fx_out), (force_y, fy_out), (force_z, fz_out)):
        force = barrel(force, amount)
        for q in range(4):
            group = [force[16 * (4 * q + k) : 16 * (4 * q + k) + 16] for k in range(4)]
            for v in range(4):
                value = roll(group[0], -32 * v, 1)
                for k in range(1, 4):
                    value = jnp.where(piece == k, roll(group[k], 32 * (k - v), 1), value)
                out[q, pl.ds(v, 16, stride=4), :] = value


def divergence_kernel(fx, fy, fz, x_low, x_high, y_low, y_high, out, tz):
    def wide(ref):
        return jnp.concatenate([ref[q] for q in range(4)], axis=1)

    f = wide(fx)
    lane = lanes((64, 512))
    before = jnp.where(lane < 16, x_low[...], roll(f, 16, 1))
    after = jnp.where(lane >= 496, x_high[...], roll(f, -16, 1))
    total = after - before
    g = wide(fy)
    line = lanes((64, 512), 0)
    before = jnp.where(line == 0, wide(y_low), roll(g, 1, 0))
    after = jnp.where(line == 63, wide(y_high), roll(g, -1, 0))
    total = total + (after - before)
    h = wide(fz)
    z = lane % 16
    after = jnp.where(z == 15, roll(h, 15, 1), roll(h, -1, 1))
    before = jnp.where(z == 0, roll(h, -15, 1), roll(h, 1, 1))
    total = (total + (after - before)) * (0.5 * SECOND_ORDER)
    total = jnp.concatenate([total, jnp.zeros_like(total)], axis=0)
    for q in range(4):
        tz[pl.ds(128 * q, 128), :] = jnp.transpose(total[:, 128 * q : 128 * (q + 1)])
    for z in range(NZ):
        value = tz[pl.ds(z, 32, stride=16), :]
        out[z] = jnp.where(
            lanes((16, 128)) < 64, value[0:16], roll(value[16:32], 64, 1)
        )


def weight_kernel(first, pulled, out, part, wzz, wxz, wyz):
    @pl.loop(0, NZ)
    def _(z):
        xx, yy, zz, xy, xz, yz = curvatures(
            first[(z + 15) % 16], first[z], first[(z + 1) % 16]
        )
        g = pulled[z]
        wx, wy = g * (yy + zz), g * (xx + zz)
        wxy = -2.0 * g * xy
        diff = up(wxy, 0) - down(wxy, 0)
        part[z] = (
            (up(wx, 0) - 2.0 * wx + down(wx, 0))
            + (up(wy, 1) - 2.0 * wy + down(wy, 1))
            + (up(diff, 1) - down(diff, 1)) * 0.25
        )
        wzz[z] = g * (xx + yy)
        wxz[z] = -2.0 * g * xz
        wyz[z] = -2.0 * g * yz

    @pl.loop(0, NZ)
    def _(z):
        a, b = (z + 1) % 16, (z + 15) % 16
        dx, dy = wxz[a] - wxz[b], wyz[a] - wyz[b]
        out[z] = pack(
            part[z]
            + (wzz[a] - 2.0 * wzz[z] + wzz[b])
            + (up(dx, 0) - down(dx, 0)) * 0.25
            + (up(dy, 1) - down(dy, 1)) * 0.25
        )


def local(kernel, outs, scratch=(), smem=0, n=0, name=None):
    many = isinstance(outs, (list, tuple))
    return pl.pallas_call(
        kernel,
        out_shape=outs,
        in_specs=[pl.BlockSpec(memory_space=pltpu.SMEM)] * smem + [VM] * (n - smem),
        out_specs=[VM] * len(outs) if many else VM,
        scratch_shapes=list(scratch),
        compiler_params=pltpu.CompilerParams(vmem_limit_bytes=40 << 20),
        name=name,
    )


def shape(*s):
    return jax.ShapeDtypeStruct(s, F32)


TABLES = make_tables()
SPREAD = make_spread()


def handover(payload):
    moved = lax.all_to_all(
        payload.reshape(128, 8, 128), ("row", "col"), split_axis=0, concat_axis=0, tiled=True
    )
    return moved.reshape(1024, 128)


def neighbours(low, high, axis, count):
    forward = [(i, (i + 1) % count) for i in range(count)]
    backward = [((i + 1) % count, i) for i in range(count)]
    return lax.ppermute(high, axis, forward), lax.ppermute(low, axis, backward)


def on_device(delta, counts, nbar, bias, owner, anchor_x, anchor_y, anchor_z):
    tables = [jnp.asarray(t) for t in TABLES]
    spread = jnp.asarray(SPREAD, BF16)
    spread_t = jnp.asarray(SPREAD.T, BF16)
    owner_row, owner_col = owner.reshape(1, 256), owner
    ax, ay, az = (a.reshape(256, 1) for a in (anchor_x, anchor_y, anchor_z))

    src = delta.reshape(2, 16, CY, NZ).transpose(3, 1, 0, 2).reshape(NZ, 16, 128)
    first = poisson(src, tables)
    src = local(source_kernel, shape(NZ, 16, 128), n=1, name="source")(first)
    second = poisson(src, tables)
    payload, fracs = local(
        paint_kernel,
        [shape(1024, 128), shape(3, 256, 128)],
        [pltpu.VMEM((512, 128), F32), pltpu.VMEM((4, 64, 128), F32)],
        n=8,
        name="paint",
    )(first, second, owner_row, owner_col, ax, ay, az, spread)
    arrived = handover(payload)
    density, back = local(
        owner_kernel,
        [shape(CX, CY * NZ), shape(1024, 128)],
        [pltpu.VMEM((256, 128), F32), pltpu.VMEM((256, 128), F32)],
        smem=2,
        n=4,
        name="owner",
    )(nbar, bias, arrived, counts)
    returned = handover(back)
    fx, fy, fz = local(force_kernel, [shape(4, CY, 128)] * 3, n=6, name="force")(
        returned, owner_row, owner_col, az, spread_t, fracs
    )
    x_low, x_high = neighbours(fx[0, :, :16], fx[3, :, 112:], "row", NROW)
    y_low, y_high = neighbours(fy[:, :1], fy[:, 63:], "col", NCOL)
    x_low = jnp.pad(x_low, ((0, 0), (0, 496)))
    x_high = jnp.pad(x_high, ((0, 0), (496, 0)))
    src = local(
        divergence_kernel,
        shape(NZ, 16, 128),
        [pltpu.VMEM((512, 128), F32)],
        n=7,
        name="divergence",
    )(fx, fy, fz, x_low, x_high, y_low, y_high)
    pulled = poisson(src, tables)
    src = local(
        weight_kernel,
        shape(NZ, 16, 128),
        [pltpu.VMEM((NZ, XH, 128), F32)] * 4,
        n=2,
        name="weights",
    )(first, pulled)
    last = poisson(src, tables)
    gradient = pulled[:, 2:34, 2:66] * (1.0 / SECOND_ORDER) + last[:, 2:34, 2:66]
    gradient = gradient.transpose(1, 2, 0).reshape(CX, CY * NZ)
    return gradient, density


def solution(mesh):
    return jax.shard_map(
        on_device,
        mesh=mesh,
        in_specs=(
            P("row", "col"),
            P(None, "row", "col"),
            P(),
            P(),
            P(("row", "col"), None),
            P(("row", "col")),
            P(("row", "col")),
            P(("row", "col")),
        ),
        out_specs=(P("row", "col"), P("row", "col")),
        check_vma=False,
    )
```

```python
import functools
import math

import jax
import jax.numpy as jnp
import numpy as np
from jax import lax
from jax.experimental import pallas as pl
from jax.experimental.pallas import tpu as pltpu
from jax.sharding import PartitionSpec as P

GRID, NZ = 512, 16
NROW, NCOL = 16, 8
CX, CY = 32, 64
NBIN = 8
XH = 40
SECOND_ORDER = 3.0 / 7.0
F32, BF16 = jnp.float32, jnp.bfloat16
MESH = pl.DeviceIdType.MESH


def real_basis(n):
    k = np.arange(n)
    rows = []
    for m in range(n):
        if m == 0:
            rows.append(np.full(n, 1.0 / math.sqrt(n)))
        elif m < n // 2:
            rows.append(math.sqrt(2.0 / n) * np.cos(2 * np.pi * (m * k % n) / n))
        elif m == n // 2:
            rows.append((1.0 - 2.0 * (k % 2)) / math.sqrt(n))
        else:
            rows.append(math.sqrt(2.0 / n) * np.sin(2 * np.pi * ((m - n // 2) * k % n) / n))
    return np.stack(rows)


def two_terms(table):
    table = table.astype(np.float32)
    high = table.astype(jnp.bfloat16)
    low = (table - high.astype(np.float32)).astype(jnp.bfloat16)
    return high, low


def make_tables():
    basis = real_basis(GRID)
    r, i = np.divmod(np.arange(256), 16)
    first, second = 32 * r + i, 32 * r + 16 + i
    c, k = np.divmod(np.arange(256), 32)
    low, high = 64 * c + k, 64 * c + 32 + k
    fx = np.concatenate(
        [
            basis[low][:, first],
            basis[high][:, second],
            basis[high][:, first],
            basis[low][:, second],
        ]
    )
    fy = basis.T
    gy = np.zeros((GRID, NCOL, 128))
    for c in range(NCOL):
        gy[:, c, :68] = basis[:, (CY * c - 2 + np.arange(68)) % GRID]
    gx = np.zeros((NROW, XH, GRID))
    for r in range(NROW):
        gx[r, :36] = basis[:, (CX * r - 2 + np.arange(36)) % GRID].T
    tables = []
    for t in (fx, fy, gy.reshape(GRID, NCOL * 128), gx.reshape(NROW * XH, GRID)):
        tables.extend(two_terms(t))
    return tables


ZB = real_basis(NZ)


def box_lane(a, b, z):
    if a == 0:
        return b * 16 + z
    if a == 2:
        return 128 + b * 16 + z
    return 80 + b * 16 + z if b < 3 else 208 + (b - 3) * 16 + z


def make_spread():
    e = np.zeros((4, 128, 256), np.float32)
    for dx in range(2):
        for dy in range(2):
            for v in range(4):
                for u in range(2):
                    for z in range(16):
                        e[dx * 2 + dy, 32 * v + 16 * u + z, box_lane(u + dx, v + dy, z)] = 1.0
    return e.reshape(512, 256)


def dot(a, b):
    return lax.dot_general(a, b, (((1,), (0,)), ((), ())), preferred_element_type=F32)


def split(x):
    high = x.astype(BF16)
    return high, (x - high.astype(F32)).astype(BF16)


def split_3(x):
    high = x.astype(BF16)
    rest = x - high.astype(F32)
    middle = rest.astype(BF16)
    return high, middle, (rest - middle.astype(F32)).astype(BF16)


def left_product(high, low, b):
    n = b.shape[1]
    b0, b1, b2 = split_3(b)
    pair = jnp.concatenate([b0, b1], axis=1)
    t = dot(high, pair)
    s = dot(low, pair)
    return t[:, :n] + ((t[:, n:] + s[:, :n]) + (s[:, n:] + dot(high, b2)))


def right_product(a, high, low):
    m = a.shape[0]
    a0, a1, a2 = split_3(a)
    pair = jnp.concatenate([a0, a1], axis=0)
    t = dot(jnp.concatenate([pair, a2], axis=0), high)
    s = dot(pair, low)
    return t[:m] + ((t[m : 2 * m] + s[:m]) + (s[m:] + t[2 * m :]))


def exact_left(zero_one, b):
    n = b.shape[1]
    t = dot(zero_one, jnp.concatenate(split(b), axis=1))
    return t[:, :n] + t[:, n:]


def exact_right(a, zero_one):
    m = a.shape[0]
    t = dot(jnp.concatenate(split(a), axis=0), zero_one)
    return t[:m] + t[m:]


def lanes(shape, axis=1):
    return lax.broadcasted_iota(jnp.int32, shape, axis)


def roll(x, shift, axis):
    shift = shift % x.shape[axis]
    return x if shift == 0 else pltpu.roll(x, shift, axis)


def up(x, axis):
    return roll(x, -1, axis)


def down(x, axis):
    return roll(x, 1, axis)


def forward_z(v):
    even = [v[0]] + [v[z] + v[16 - z] for z in range(1, 8)] + [v[8]]
    odd = [None] + [v[z] - v[16 - z] for z in range(1, 8)]
    out = []
    for m in range(9):
        s = even[0] * float(ZB[m, 0])
        for z in range(1, 9):
            s = s + even[z] * float(ZB[m, z])
        out.append(s)
    for m in range(9, 16):
        s = odd[1] * float(ZB[m, 1])
        for z in range(2, 8):
            s = s + odd[z] * float(ZB[m, z])
        out.append(s)
    return out


def inverse_z(v):
    out = [None] * 16
    for z in range(9):
        even = v[0] * float(ZB[0, z])
        for m in range(1, 9):
            even = even + v[m] * float(ZB[m, z])
        if z in (0, 8):
            out[z] = even
            continue
        odd = v[9] * float(ZB[9, z])
        for m in range(10, 16):
            odd = odd + v[m] * float(ZB[m, z])
        out[z] = even + odd
        out[16 - z] = even - odd
    return out


def exchange(n, me, axis, src, dst, send, recv, own):
    sends, recvs = [], []
    for k in range(1, n):
        peer = lax.rem(me + k, n)
        origin = lax.rem(me + n - k, n)
        copy = pltpu.make_async_remote_copy(
            src_ref=src.at[peer],
            dst_ref=dst.at[me],
            send_sem=send.at[k],
            recv_sem=recv.at[k],
            device_id={axis: peer},
            device_id_type=MESH,
        )
        copy.start()
        sends.append(copy)
        recvs.append(
            pltpu.make_async_remote_copy(
                src_ref=src.at[peer],
                dst_ref=dst.at[origin],
                send_sem=send.at[k],
                recv_sem=recv.at[k],
                device_id={axis: peer},
                device_id_type=MESH,
            )
        )
    copy = pltpu.make_async_copy(src.at[me], dst.at[me], own)
    copy.start()
    return sends, recvs, copy


def arrive(state):
    state[2].wait()
    for copy in state[1]:
        copy.wait_recv()


def modes_factor(row, col):
    kx = lanes((64, GRID), 0) + col * 64
    ky = lanes((64, GRID), 1)
    kx = jnp.where(kx <= GRID // 2, kx, kx - GRID // 2).astype(F32) * (2.0 * math.pi / GRID)
    ky = jnp.where(ky <= GRID // 2, ky, ky - GRID // 2).astype(F32) * (2.0 * math.pi / GRID)
    kz = jnp.where(row <= NZ // 2, row, row - NZ // 2)
    kz = jnp.full((64, GRID), kz, jnp.int32).astype(F32) * (2.0 * math.pi / NZ)
    square = kx * kx + ky * ky + kz * kz
    return jnp.where(square > 0, -1.0 / jnp.where(square > 0, square, 1.0), 0.0)


def solve(place, buffers, semaphores, held, factor, out, pending, ready=None):
    row, col = place
    mo, r1, pk, r2, zb, r3, xb, r4 = buffers
    s1, q1, s2, q2, s3, q3, s4, q4, own = semaphores
    fxh, fxl, fyh, fyl, gyh, gyl, gxh, gxl = held
    low_half = lanes((256, 128)) < 64
    state1 = exchange(NROW, row, "row", mo, r1, s1, q1, own.at[0])
    if ready is not None:
        ready()
    arrive(state1)
    t = left_product(fxh[...], fxl[...], r1[...].reshape(256, 128))
    packed = jnp.where(low_half, t[:256], t[256:512]) + roll(
        jnp.where(low_half, t[512:768], t[768:]), 64, 1
    )
    pk[...] = packed.reshape(NCOL, 32, 128)
    state2 = exchange(NCOL, col, "col", pk, r2, s2, q2, own.at[1])
    arrive(state2)
    half = lanes((32, 128)) < 64
    top, bottom = [], []
    for p in range(4):
        a, b = r2[2 * p], r2[2 * p + 1]
        top.append(jnp.where(half, a, roll(b, 64, 1)))
        bottom.append(jnp.where(half, roll(a, 64, 1), b))
    full = jnp.concatenate(
        [jnp.concatenate(top, axis=1), jnp.concatenate(bottom, axis=1)], axis=0
    )
    modes = right_product(full, fyh[...], fyl[...]) * factor[...]
    back = right_product(modes, gyh[...], gyl[...])
    for c in range(NCOL):
        zb[c] = back[:, 128 * c : 128 * (c + 1)]
    state3 = exchange(NCOL, col, "col", zb, r3, s3, q3, own.at[2])
    arrive(state3)
    xb[...] = left_product(gxh[...], gxl[...], r3[...].reshape(GRID, 128)).reshape(NROW, XH, 128)
    state4 = exchange(NROW, row, "row", xb, r4, s4, q4, own.at[3])
    arrive(state4)
    for s in range(5):
        rows = pl.ds(8 * s, 8)
        for z, value in enumerate(inverse_z([r4[m, rows, :] for m in range(16)])):
            out[z, rows, :] = value
    for state in (state1, state2, state3, state4):
        pending.extend(state[0])


def to_modes(src, mo):
    for s in range(2):
        rows = pl.ds(8 * s, 8)
        for m, value in enumerate(forward_z([src[z, rows, :] for z in range(16)])):
            mo[m, rows, :] = value


def delta_modes(delta, tzh, tzl, mo):
    d = delta[...]
    t = right_product(
        jnp.concatenate([d[:, 256 * q : 256 * (q + 1)] for q in range(4)], axis=0),
        tzh[...],
        tzl[...],
    )
    slot = lanes((16, 128)) // 16
    for m in range(16):
        part = 128 * (m // 8)
        value = None
        for h in range(2):
            for q in range(4):
                piece = t[32 * q + 16 * h : 32 * q + 16 * h + 16, part : part + 128]
                piece = roll(piece, 16 * (4 * h + q - m % 8), 1)
                value = piece if value is None else jnp.where(slot == 4 * h + q, piece, value)
        mo[m] = value


def handover(row, col, src, dst, send, recv, own):
    me = row * NCOL + col

    @pl.loop(1, 128)
    def _(k):
        peer = lax.rem(me + k, 128)
        pltpu.make_async_remote_copy(
            src_ref=src.at[peer],
            dst_ref=dst.at[me],
            send_sem=send,
            recv_sem=recv,
            device_id={"row": peer // NCOL, "col": lax.rem(peer, NCOL)},
            device_id_type=MESH,
        ).start()

    copy = pltpu.make_async_copy(src.at[me], dst.at[me], own)
    copy.start()
    copy.wait()
    all_of_them = pltpu.make_async_remote_copy(
        src_ref=src.at[pl.ds(0, 127)],
        dst_ref=dst.at[pl.ds(0, 127)],
        send_sem=send,
        recv_sem=recv,
        device_id={"col": lax.rem(col + 1, NCOL)},
        device_id_type=MESH,
    )
    all_of_them.wait_recv()
    return all_of_them


def neighbours(row, col, fx, fy, x_low, x_high, y_low, y_high, sems, pending):
    copies = []
    for i, (axis, peer, src, dst) in enumerate(
        (
            ("row", lax.rem(row + 1, NROW), fx.at[3], x_low),
            ("row", lax.rem(row + NROW - 1, NROW), fx.at[0], x_high),
            ("col", lax.rem(col + 1, NCOL), fy.at[:, pl.ds(56, 8)], y_low),
            ("col", lax.rem(col + NCOL - 1, NCOL), fy.at[:, pl.ds(0, 8)], y_high),
        )
    ):
        copies.append(
            pltpu.make_async_remote_copy(
                src_ref=src,
                dst_ref=dst,
                send_sem=sems.at[0, i],
                recv_sem=sems.at[1, i],
                device_id={axis: peer},
                device_id_type=MESH,
            )
        )
        copies[-1].start()
    for copy in copies:
        copy.wait_recv()
    pending.extend(copies)


VM = pl.BlockSpec(memory_space=pltpu.VMEM)
ANY = pl.BlockSpec(memory_space=pl.ANY)


def pack(f):
    f = roll(f, -2, 0)
    low = roll(f[0:16], -2, 1)
    high = roll(f[16:32], 62, 1)
    return jnp.where(lanes((16, 128)) < 64, low, high)


def curvatures(below, here, above):
    xx = up(here, 0) - 2.0 * here + down(here, 0)
    yy = up(here, 1) - 2.0 * here + down(here, 1)
    zz = above - 2.0 * here + below
    dx = up(here, 0) - down(here, 0)
    dz = above - below
    xy = (up(dx, 1) - down(dx, 1)) * 0.25
    xz = (up(dz, 0) - down(dz, 0)) * 0.25
    yz = (up(dz, 1) - down(dz, 1)) * 0.25
    return xx, yy, zz, xy, xz, yz


def source(first, out):
    @pl.loop(0, NZ)
    def _(z):
        xx, yy, zz, xy, xz, yz = curvatures(
            first[(z + 15) % 16], first[z], first[(z + 1) % 16]
        )
        out[z] = pack(xx * yy + xx * zz + yy * zz - xy * xy - xz * xz - yz * yz)


def group_roll(x, s):
    z = lanes(x.shape) % 16
    return jnp.where(z >= s, roll(x, s, 1), roll(x, s - 16, 1))


def barrel(x, amount):
    for bit in (1, 2, 4, 8):
        x = jnp.where((amount & bit) > 0, group_roll(x, bit), x)
    return x


def barrel_16(x, amount):
    for bit in (1, 2, 4):
        x = jnp.where((amount & bit) > 0, roll(x, 16 * bit, 1), x)
    return x


def slots(owner_row, owner_col):
    device = lanes((128, 256), 0)
    chosen_t = jnp.where(device == owner_row, 1.0, 0.0)
    order = jnp.where(lanes((256, 256), 0) < lanes((256, 256), 1), 1.0, 0.0)
    earlier_t = dot(chosen_t.astype(BF16), order.astype(BF16))
    along = jnp.sum(earlier_t * chosen_t, axis=0, keepdims=True)
    along = owner_row * 8 + along.astype(jnp.int32)
    chosen = jnp.where(lanes((256, 128)) == owner_col, 1.0, 0.0)
    order = jnp.where(lanes((256, 256), 0) > lanes((256, 256), 1), 1.0, 0.0)
    earlier = dot(order.astype(BF16), chosen.astype(BF16))
    down_ = jnp.sum(earlier * chosen, axis=1, keepdims=True)
    down_ = owner_col * 8 + down_.astype(jnp.int32)
    return along, down_


def paint(first, second, along, ax, ay, az, spread, out, fracs, tz, tt):
    piece = lanes((16, 128)) // 32
    for axis in range(3):

        @pl.loop(0, NZ)
        def _(z, axis=axis):
            def total(k):
                return first[k] + SECOND_ORDER * second[k]

            if axis == 2:
                slope = total((z + 1) % 16) - total((z + 15) % 16)
            else:
                here = total(z)
                slope = up(here, axis) - down(here, axis)
            value = 0.5 - 0.5 * slope
            value = roll(roll(value, -2, 0)[0:32], -2, 1)
            tz[pl.ds(z, 32, stride=16), :] = value

        for q in range(4):
            tt[q] = jnp.transpose(tz[pl.ds(128 * q, 128), :])[0:64]
        for q in range(4):
            quarter = [tt[q, pl.ds(v, 16, stride=4), :] for v in range(4)]
            for k in range(4):
                block = roll(quarter[0], -32 * k, 1)
                for v in range(1, 4):
                    block = jnp.where(piece == v, roll(quarter[v], 32 * (v - k), 1), block)
                fracs[axis, pl.ds(16 * (4 * q + k), 16), :] = block
    for axis in range(3):
        fracs[axis] = barrel(fracs[axis], az)
    fx, fy, fz = fracs[0], fracs[1], fracs[2]
    fields = []
    for wx in (1.0 - fx, fx):
        for wy in (1.0 - fy, fy):
            q = wx * wy
            upper = q * fz
            fields.append(q - upper + group_roll(upper, 1))
    box = exact_right(jnp.concatenate(fields, axis=1), spread[...])
    lane = lanes((256, 256))
    box = jnp.where(lane == 240, ax.astype(F32), box)
    box = jnp.where(lane == 241, ay.astype(F32), box)
    target = jnp.concatenate([along, along + 4], axis=1)
    table = jnp.where(lanes((1024, 512), 0) == target, 1.0, 0.0).astype(BF16)
    stacked = jnp.concatenate([box[:, :128], box[:, 128:]], axis=0)
    out[...] = exact_left(table, stacked).reshape(128, 8, 128)


def own_cells(nbar, bias, arrived, counts, density, back, dens, pulls):
    data = arrived[...].reshape(1024, 128)
    second = lanes((1024, 128), 0) // 4 % 2
    is_second = second == 1

    def both(lane):
        column = jnp.broadcast_to(data[:, lane : lane + 1], (1024, 128))
        return jnp.where(is_second, column, roll(column, -4, 0)).astype(jnp.int32)

    ax, ay = both(112), both(113)
    flipped = jnp.concatenate(
        [jnp.transpose(data[128 * i : 128 * (i + 1)]) for i in range(8)], axis=1
    )
    second_row = lanes((1, 1024)) // 4 % 2

    def both_row(lane):
        line = flipped[lane : lane + 1]
        line = jnp.where(second_row == 1, line, roll(line, -4, 1))
        return line.astype(jnp.int32)

    ax_row, ay_row = both_row(112), both_row(113)
    base_row = (ay_row >> 3) * 32 + ax_row
    base = (ay >> 3) * 32 + ax
    lane = lanes((1024, 128))
    step = ay & 7
    side_step = (3 * second + 3 + ay) & 7
    stay = lane >= step * 16
    main = barrel_16(jnp.where(lane < 80, data, 0.0), step)
    side_mask = (lane >= 80) & (lane < 112 + 16 * (1 - second))
    side = barrel_16(jnp.where(side_mask, data, 0.0), side_step)
    total = None
    for part, offset in ((main, 2 * second_row), (side, 1)):
        table = jnp.where(lanes((256, 1024), 0) == base_row + offset, 1.0, 0.0).astype(BF16)
        near = split(jnp.where(stay, part, 0.0))
        far = split(jnp.where(stay, 0.0, part))
        t = dot(table, jnp.concatenate([*near, *far], axis=1))
        total = t if total is None else total + t
    near = total[:, :128] + total[:, 128:256]
    far = total[:, 256:384] + total[:, 384:]
    dens[...] = near + jnp.where(lanes((256, 128), 0) >= 32, roll(far, 32, 0), 0.0)
    for j in range(8):
        here = dens[pl.ds(32 * j, 32), :]
        density[:, pl.ds(128 * j, 128)] = here
        contrast = here - 1.0
        pull = jnp.zeros((32, 128), F32)
        for b in range(NBIN):
            rate = nbar[b] * jnp.exp(bias[b] * contrast)
            number = counts[b, :, pl.ds(128 * j, 128)].astype(F32)
            pull = pull + bias[b] * (number - rate)
        pulls[pl.ds(32 * j, 32), :] = pull
    pull = pulls[...]
    ahead = jnp.where(lanes((256, 128), 0) < 224, roll(pull, -32, 0), 0.0)
    both_pulls = jnp.concatenate([*split(pull), *split(ahead)], axis=1)

    def picked(offset, amount):
        wide = jnp.concatenate([base + offset, base + offset], axis=1)
        table = jnp.where(lanes((1024, 256)) == wide, 1.0, 0.0).astype(BF16)
        t = dot(table, both_pulls)
        value = jnp.where(stay, t[:, :128] + t[:, 128:256], t[:, 256:384] + t[:, 384:])
        return barrel_16(value, (8 - amount) & 7)

    value = jnp.where(lane < 80, picked(2 * second, step), picked(1, side_step))
    back[...] = value.reshape(128, 8, 128)


def forces(returned, place, az, spread_t, fracs, fx_out, fy_out, fz_out):
    target = jnp.concatenate([place, place + 4], axis=0)
    table = jnp.where(lanes((512, 1024)) == target, 1.0, 0.0).astype(BF16)
    t = exact_left(table, returned[...].reshape(1024, 128))
    box = jnp.concatenate([t[:256], t[256:]], axis=1)
    corner = exact_right(box, spread_t[...])
    fx, fy, fz = fracs[0], fracs[1], fracs[2]
    along, across = [], []
    for d in range(4):
        here = corner[:, 128 * d : 128 * (d + 1)]
        change = group_roll(here, 15) - here
        along.append(here + fz * change)
        across.append(change)
    amount = (16 - az) & 15
    force_x = (1.0 - fy) * (along[2] - along[0]) + fy * (along[3] - along[1])
    force_y = (1.0 - fx) * (along[1] - along[0]) + fx * (along[3] - along[2])
    force_z = (1.0 - fx) * ((1.0 - fy) * across[0] + fy * across[1]) + fx * (
        (1.0 - fy) * across[2] + fy * across[3]
    )
    piece = lanes((16, 128)) // 32
    for force, out in ((force_x, fx_out), (force_y, fy_out), (force_z, fz_out)):
        force = barrel(force, amount)
        for q in range(4):
            group = [force[16 * (4 * q + k) : 16 * (4 * q + k) + 16] for k in range(4)]
            for v in range(4):
                value = roll(group[0], -32 * v, 1)
                for k in range(1, 4):
                    value = jnp.where(piece == k, roll(group[k], 32 * (k - v), 1), value)
                out[q, pl.ds(v, 16, stride=4), :] = value


def divergence(fx, fy, fz, x_low, x_high, y_low, y_high, out, tz):
    def wide(ref):
        return jnp.concatenate([ref[q] for q in range(4)], axis=1)

    def four(value):
        return jnp.concatenate([value] * 4, axis=1)

    def edge(ref, i):
        return jnp.concatenate([ref[q, i : i + 1, :] for q in range(4)], axis=1)

    f = wide(fx)
    lane = lanes((64, 512))
    before = jnp.where(lane < 16, four(roll(x_low[...], 16, 1)), roll(f, 16, 1))
    after = jnp.where(lane >= 496, four(roll(x_high[...], 112, 1)), roll(f, -16, 1))
    total = after - before
    g = wide(fy)
    line = lanes((64, 512), 0)
    before = jnp.where(line == 0, edge(y_low, 7), roll(g, 1, 0))
    after = jnp.where(line == 63, edge(y_high, 0), roll(g, -1, 0))
    total = total + (after - before)
    h = wide(fz)
    z = lane % 16
    after = jnp.where(z == 15, roll(h, 15, 1), roll(h, -1, 1))
    before = jnp.where(z == 0, roll(h, -15, 1), roll(h, 1, 1))
    total = (total + (after - before)) * (0.5 * SECOND_ORDER)
    total = jnp.concatenate([total, jnp.zeros_like(total)], axis=0)
    for q in range(4):
        tz[pl.ds(128 * q, 128), :] = jnp.transpose(total[:, 128 * q : 128 * (q + 1)])
    for z in range(NZ):
        value = tz[pl.ds(z, 32, stride=16), :]
        out[z] = jnp.where(
            lanes((16, 128)) < 64, value[0:16], roll(value[16:32], 64, 1)
        )


def weights(first, pulled, out, part, wzz, wxz, wyz):
    @pl.loop(0, NZ)
    def _(z):
        xx, yy, zz, xy, xz, yz = curvatures(
            first[(z + 15) % 16], first[z], first[(z + 1) % 16]
        )
        g = pulled[z]
        wx, wy = g * (yy + zz), g * (xx + zz)
        wxy = -2.0 * g * xy
        diff = up(wxy, 0) - down(wxy, 0)
        part[z] = (
            (up(wx, 0) - 2.0 * wx + down(wx, 0))
            + (up(wy, 1) - 2.0 * wy + down(wy, 1))
            + (up(diff, 1) - down(diff, 1)) * 0.25
        )
        wzz[z] = g * (xx + yy)
        wxz[z] = -2.0 * g * xz
        wyz[z] = -2.0 * g * yz

    @pl.loop(0, NZ)
    def _(z):
        a, b = (z + 1) % 16, (z + 15) % 16
        dx, dy = wxz[a] - wxz[b], wyz[a] - wyz[b]
        out[z] = pack(
            part[z]
            + (wzz[a] - 2.0 * wzz[z] + wzz[b])
            + (up(dx, 0) - down(dx, 0)) * 0.25
            + (up(dy, 1) - down(dy, 1)) * 0.25
        )


def columns(rows):
    stack = jnp.concatenate([r.astype(F32) for r in rows] + [jnp.zeros((124, 256), F32)], axis=0)
    turned = jnp.concatenate([jnp.transpose(stack[:, :128]), jnp.transpose(stack[:, 128:])], axis=0)
    return [turned[:, i : i + 1].astype(jnp.int32) for i in range(len(rows))]


N_TABLES = 12


def whole_kernel(nbar, bias, delta, owner, anchor_x, anchor_y, anchor_z, *refs):
    counts_far, tables = refs[0], refs[1 : 1 + N_TABLES]
    gradient, density = refs[1 + N_TABLES : 3 + N_TABLES]
    rest = list(refs[3 + N_TABLES :])

    def take(n):
        taken, rest[:] = rest[:n], rest[n:]
        return taken

    held, (counts,) = take(N_TABLES), take(1)
    buffers = [take(8) for _ in range(4)]
    first, second, pulled, last, part, wzz, wxz, wyz = take(8)
    src, factor, fracs, tz, tt = take(5)
    payload, arrived, back, returned, dens, pulls = take(6)
    fx, fy, fz, x_low, x_high, y_low, y_high = take(7)
    table_sem, *exchange_sems, own, hand_sem, edge_sem = rest
    row, col = lax.axis_index("row"), lax.axis_index("col")
    me = row * NCOL + col
    pending = []

    def semaphores(i):
        return [s.at[i] for s in exchange_sems] + [own.at[i]]

    barrier = pltpu.get_barrier_semaphore()

    @pl.loop(1, 128)
    def _(k):
        peer = lax.rem(me + k, 128)
        pl.semaphore_signal(
            barrier,
            inc=1,
            device_id={"row": peer // NCOL, "col": lax.rem(peer, NCOL)},
            device_id_type=MESH,
        )

    loads = [
        pltpu.make_async_copy(t, h, table_sem.at[i])
        for i, (t, h) in enumerate(zip((*tables, counts_far), (*held, counts)))
    ]
    for load in loads:
        load.start()
    tzh, tzl, *main, spread, spread_t = held
    loads[0].wait()
    loads[1].wait()
    delta_modes(delta, tzh, tzl, buffers[0][0])
    pl.semaphore_wait(barrier, 127)

    def ready():
        factor[...] = modes_factor(row, col)
        for load in loads[2:]:
            load.wait()

    place = (row, col)
    solve(place, buffers[0], semaphores(0), main, factor, first, pending, ready)
    source(first, src)
    to_modes(src, buffers[1][0])
    solve(place, buffers[1], semaphores(1), main, factor, second, pending)
    owner_row = owner[...]
    rows = (owner_row, anchor_x[...], anchor_y[...], anchor_z[...])
    owner_col, ax, ay, az = columns(rows)
    along, down_rows = slots(owner_row, owner_col)
    paint(first, second, along, ax, ay, az, spread, payload, fracs, tz, tt)
    pending.append(handover(row, col, payload, arrived, hand_sem.at[0], hand_sem.at[1], hand_sem.at[2]))
    own_cells(nbar, bias, arrived, counts, density, back, dens, pulls)
    pending.append(handover(row, col, back, returned, hand_sem.at[3], hand_sem.at[4], hand_sem.at[5]))
    forces(returned, down_rows, az, spread_t, fracs, fx, fy, fz)
    neighbours(row, col, fx, fy, x_low, x_high, y_low, y_high, edge_sem, pending)
    divergence(fx, fy, fz, x_low, x_high, y_low, y_high, src, tz)
    to_modes(src, buffers[2][0])
    solve(place, buffers[2], semaphores(2), main, factor, pulled, pending)
    weights(first, pulled, src, part, wzz, wxz, wyz)
    to_modes(src, buffers[3][0])
    solve(place, buffers[3], semaphores(3), main, factor, last, pending)

    @pl.loop(0, NZ)
    def _(z):
        value = pulled[z] * (1.0 / SECOND_ORDER) + last[z]
        gradient[z] = roll(roll(value, -2, 0)[0:32], -2, 1)

    for copy in pending:
        copy.wait_send()


def delta_table():
    t = np.zeros((16, 16, 16, 16))
    for y in range(16):
        t[y, :, :, y] = ZB.T
    return two_terms(t.reshape(256, 256))


def spread_tables():
    spread = make_spread()
    return [spread.astype(jnp.bfloat16), spread.T.copy().astype(jnp.bfloat16)]


TABLES = [*delta_table(), *make_tables(), *spread_tables()]


def on_device(delta, counts, nbar, bias, owner, anchor_x, anchor_y, anchor_z):
    tables = [jnp.asarray(t) for t in TABLES]
    flat = [a.reshape(1, 256) for a in (owner, anchor_x, anchor_y, anchor_z)]
    field = pltpu.VMEM((NZ, XH, 128), F32)
    hand = pltpu.VMEM((128, 8, 128), F32)
    scratch = [pltpu.VMEM(t.shape, BF16) for t in tables] + [pltpu.VMEM(counts.shape, jnp.int32)]
    for _ in range(4):
        for s in ((NROW, 16, 128), (NCOL, 32, 128), (NCOL, 64, 128), (NROW, XH, 128)):
            scratch += [pltpu.VMEM(s, F32), pltpu.VMEM(s, F32)]
    scratch += [field] * 8
    scratch += [pltpu.VMEM((NZ, 16, 128), F32), pltpu.VMEM((64, GRID), F32)]
    scratch += [pltpu.VMEM((3, 256, 128), F32), pltpu.VMEM((512, 128), F32)]
    scratch += [pltpu.VMEM((4, 64, 128), F32)]
    scratch += [hand] * 4 + [pltpu.VMEM((256, 128), F32)] * 2
    scratch += [pltpu.VMEM((4, 64, 128), F32)] * 3
    scratch += [pltpu.VMEM((64, 128), F32)] * 2 + [pltpu.VMEM((4, 8, 128), F32)] * 2
    scratch += [pltpu.SemaphoreType.DMA((len(tables) + 1,))]
    for n in (NROW, NCOL, NCOL, NROW):
        scratch += [pltpu.SemaphoreType.DMA((4, n)), pltpu.SemaphoreType.DMA((4, n))]
    scratch += [
        pltpu.SemaphoreType.DMA((4, 4)),
        pltpu.SemaphoreType.DMA((6,)),
        pltpu.SemaphoreType.DMA((2, 4)),
    ]
    smem = pl.BlockSpec(memory_space=pltpu.SMEM)
    gradient, density = pl.pallas_call(
        whole_kernel,
        out_shape=[
            jax.ShapeDtypeStruct((NZ, CX, 128), F32),
            jax.ShapeDtypeStruct((CX, CY * NZ), F32),
        ],
        in_specs=[smem] * 2 + [VM] * 5 + [ANY] * (1 + len(tables)),
        out_specs=[VM, VM],
        scratch_shapes=scratch,
        compiler_params=pltpu.CompilerParams(
            collective_id=0, has_side_effects=True, vmem_limit_bytes=60 << 20
        ),
        name="whole",
    )(nbar, bias, delta, *flat, counts, *tables)
    gradient = gradient[:, :, :CY].transpose(1, 2, 0).reshape(CX, CY * NZ)
    return gradient, density


def solution(mesh):
    return jax.shard_map(
        on_device,
        mesh=mesh,
        in_specs=(
            P("row", "col"),
            P(None, "row", "col"),
            P(),
            P(),
            P(("row", "col"), None),
            P(("row", "col")),
            P(("row", "col")),
            P(("row", "col")),
        ),
        out_specs=(P("row", "col"), P("row", "col")),
        check_vma=False,
    )
```

```python
import functools
import math

import jax
import jax.numpy as jnp
import numpy as np
from jax import lax
from jax.experimental import pallas as pl
from jax.experimental.pallas import tpu as pltpu
from jax.sharding import PartitionSpec as P

GRID, NZ = 512, 16
NROW, NCOL = 16, 8
CX, CY = 32, 64
NBIN = 8
XH = 40
SECOND_ORDER = 3.0 / 7.0
F32, BF16 = jnp.float32, jnp.bfloat16
MESH = pl.DeviceIdType.MESH


def real_basis(n):
    k = np.arange(n)
    rows = []
    for m in range(n):
        if m == 0:
            rows.append(np.full(n, 1.0 / math.sqrt(n)))
        elif m < n // 2:
            rows.append(math.sqrt(2.0 / n) * np.cos(2 * np.pi * (m * k % n) / n))
        elif m == n // 2:
            rows.append((1.0 - 2.0 * (k % 2)) / math.sqrt(n))
        else:
            rows.append(math.sqrt(2.0 / n) * np.sin(2 * np.pi * ((m - n // 2) * k % n) / n))
    return np.stack(rows)


def two_terms(table):
    table = table.astype(np.float32)
    high = table.astype(jnp.bfloat16)
    low = (table - high.astype(np.float32)).astype(jnp.bfloat16)
    return high, low


def make_tables():
    basis = real_basis(GRID)
    r, i = np.divmod(np.arange(256), 16)
    first, second = 32 * r + i, 32 * r + 16 + i
    c, k = np.divmod(np.arange(256), 32)
    low, high = 64 * c + k, 64 * c + 32 + k
    fx = np.concatenate(
        [
            basis[low][:, first],
            basis[high][:, second],
            basis[high][:, first],
            basis[low][:, second],
        ]
    )
    fy = basis.T
    gy = np.zeros((GRID, NCOL, 128))
    for c in range(NCOL):
        for y in range(-2, CY + 2):
            gy[:, c, y % 128] = basis[:, (CY * c + y) % GRID]
    gx = np.zeros((NROW, XH, GRID))
    for r in range(NROW):
        for x in range(-2, CX + 2):
            gx[r, x % XH] = basis[:, (CX * r + x) % GRID]
    tables = []
    for t in (fx, fy, gy.reshape(GRID, NCOL * 128), gx.reshape(NROW * XH, GRID)):
        tables.extend(two_terms(t))
    return tables


ZB = real_basis(NZ)


def box_lane(a, b, z):
    if a == 0:
        return b * 16 + z
    if a == 2:
        return 128 + b * 16 + z
    return 80 + b * 16 + z if b < 3 else 208 + (b - 3) * 16 + z


def make_spread():
    e = np.zeros((4, 128, 256), np.float32)
    for dx in range(2):
        for dy in range(2):
            for v in range(4):
                for u in range(2):
                    for z in range(16):
                        e[dx * 2 + dy, 32 * v + 16 * u + z, box_lane(u + dx, v + dy, z)] = 1.0
    return e.reshape(512, 256)


def dot(a, b):
    return lax.dot_general(a, b, (((1,), (0,)), ((), ())), preferred_element_type=F32)


def split(x):
    high = x.astype(BF16)
    return high, (x - high.astype(F32)).astype(BF16)


def split_3(x):
    high = x.astype(BF16)
    rest = x - high.astype(F32)
    middle = rest.astype(BF16)
    return high, middle, (rest - middle.astype(F32)).astype(BF16)


def left_product(high, low, b):
    n = b.shape[1]
    b0, b1, b2 = split_3(b)
    pair = jnp.concatenate([b0, b1], axis=1)
    t = dot(high, pair)
    s = dot(low, pair)
    return t[:, :n] + ((t[:, n:] + s[:, :n]) + (s[:, n:] + dot(high, b2)))


def right_product(a, high, low):
    m = a.shape[0]
    a0, a1, a2 = split_3(a)
    pair = jnp.concatenate([a0, a1], axis=0)
    t = dot(jnp.concatenate([pair, a2], axis=0), high)
    s = dot(pair, low)
    return t[:m] + ((t[m : 2 * m] + s[:m]) + (s[m:] + t[2 * m :]))


def exact_left(zero_one, b):
    n = b.shape[1]
    t = dot(zero_one, jnp.concatenate(split(b), axis=1))
    return t[:, :n] + t[:, n:]


def exact_right(a, zero_one):
    m = a.shape[0]
    t = dot(jnp.concatenate(split(a), axis=0), zero_one)
    return t[:m] + t[m:]


def lanes(shape, axis=1):
    return lax.broadcasted_iota(jnp.int32, shape, axis)


def roll(x, shift, axis):
    shift = shift % x.shape[axis]
    return x if shift == 0 else pltpu.roll(x, shift, axis)


def up(x, axis):
    return roll(x, -1, axis)


def down(x, axis):
    return roll(x, 1, axis)


def forward_z(v):
    even = [v[0]] + [v[z] + v[16 - z] for z in range(1, 8)] + [v[8]]
    odd = [None] + [v[z] - v[16 - z] for z in range(1, 8)]
    out = []
    for m in range(9):
        s = even[0] * float(ZB[m, 0])
        for z in range(1, 9):
            s = s + even[z] * float(ZB[m, z])
        out.append(s)
    for m in range(9, 16):
        s = odd[1] * float(ZB[m, 1])
        for z in range(2, 8):
            s = s + odd[z] * float(ZB[m, z])
        out.append(s)
    return out


def inverse_z(v):
    out = [None] * 16
    for z in range(9):
        even = v[0] * float(ZB[0, z])
        for m in range(1, 9):
            even = even + v[m] * float(ZB[m, z])
        if z in (0, 8):
            out[z] = even
            continue
        odd = v[9] * float(ZB[9, z])
        for m in range(10, 16):
            odd = odd + v[m] * float(ZB[m, z])
        out[z] = even + odd
        out[16 - z] = even - odd
    return out


def distance(n, k):
    around = lambda d: min(d, 4 - d)
    return around(k % 4) + around(k // 4) if n == NROW else around(k // 2)


def exchange(n, me, axis, src, dst, send, recv, own):
    sends, recvs = [], []
    for k in sorted(range(1, n), key=lambda k: -distance(n, k)):
        peer = lax.rem(me + k, n)
        origin = lax.rem(me + n - k, n)
        copy = pltpu.make_async_remote_copy(
            src_ref=src.at[peer],
            dst_ref=dst.at[me],
            send_sem=send.at[k],
            recv_sem=recv.at[k],
            device_id={axis: peer},
            device_id_type=MESH,
        )
        copy.start()
        sends.append(copy)
        recvs.append(
            pltpu.make_async_remote_copy(
                src_ref=src.at[peer],
                dst_ref=dst.at[origin],
                send_sem=send.at[k],
                recv_sem=recv.at[k],
                device_id={axis: peer},
                device_id_type=MESH,
            )
        )
    copy = pltpu.make_async_copy(src.at[me], dst.at[me], own)
    copy.start()
    return sends, recvs, copy


def arrive(state):
    state[2].wait()
    for copy in state[1]:
        copy.wait_recv()


def modes_factor(row, col):
    kx = lanes((64, GRID), 0) + col * 64
    ky = lanes((64, GRID), 1)
    kx = jnp.where(kx <= GRID // 2, kx, kx - GRID // 2).astype(F32) * (2.0 * math.pi / GRID)
    ky = jnp.where(ky <= GRID // 2, ky, ky - GRID // 2).astype(F32) * (2.0 * math.pi / GRID)
    kz = jnp.where(row <= NZ // 2, row, row - NZ // 2)
    kz = jnp.full((64, GRID), kz, jnp.int32).astype(F32) * (2.0 * math.pi / NZ)
    square = kx * kx + ky * ky + kz * kz
    return jnp.where(square > 0, -1.0 / jnp.where(square > 0, square, 1.0), 0.0)


def solve(place, buffers, semaphores, held, factor, out, pending, fill=(None,) * 4):
    row, col = place
    mo, r1, pk, r2, zb, r3, xb, r4 = buffers
    s1, q1, s2, q2, s3, q3, s4, q4, own = semaphores
    fxh, fxl, fyh, fyl, gyh, gyl, gxh, gxl = held
    low_half = lanes((256, 128)) < 64
    state1 = exchange(NROW, row, "row", mo, r1, s1, q1, own.at[0])
    if fill[0]:
        fill[0]()
    arrive(state1)
    t = left_product(fxh[...], fxl[...], r1[...].reshape(256, 128))
    packed = jnp.where(low_half, t[:256], t[256:512]) + roll(
        jnp.where(low_half, t[512:768], t[768:]), 64, 1
    )
    pk[...] = packed.reshape(NCOL, 32, 128)
    state2 = exchange(NCOL, col, "col", pk, r2, s2, q2, own.at[1])
    if fill[1]:
        fill[1]()
    arrive(state2)
    half = lanes((32, 128)) < 64
    top, bottom = [], []
    for p in range(4):
        a, b = r2[2 * p], r2[2 * p + 1]
        top.append(jnp.where(half, a, roll(b, 64, 1)))
        bottom.append(jnp.where(half, roll(a, 64, 1), b))
    full = jnp.concatenate(
        [jnp.concatenate(top, axis=1), jnp.concatenate(bottom, axis=1)], axis=0
    )
    modes = right_product(full, fyh[...], fyl[...]) * factor[...]
    back = right_product(modes, gyh[...], gyl[...])
    for c in range(NCOL):
        zb[c] = back[:, 128 * c : 128 * (c + 1)]
    state3 = exchange(NCOL, col, "col", zb, r3, s3, q3, own.at[2])
    if fill[2]:
        fill[2]()
    arrive(state3)
    xb[...] = left_product(gxh[...], gxl[...], r3[...].reshape(GRID, 128)).reshape(NROW, XH, 128)
    state4 = exchange(NROW, row, "row", xb, r4, s4, q4, own.at[3])
    if fill[3]:
        fill[3]()
    arrive(state4)
    for s in range(5 if out is not None else 0):
        rows = pl.ds(8 * s, 8)
        for z, value in enumerate(inverse_z([r4[m, rows, :] for m in range(16)])):
            out[z, rows, :] = value
    for state in (state1, state2, state3, state4):
        pending.extend(state[0])


def to_modes(src, mo):
    for s in range(2):
        rows = pl.ds(8 * s, 8)
        for m, value in enumerate(forward_z([src[z, rows, :] for z in range(16)])):
            mo[m, rows, :] = value


def delta_modes(delta, tzh, tzl, mo):
    d = delta[...]
    t = right_product(
        jnp.concatenate([d[:, 256 * q : 256 * (q + 1)] for q in range(4)], axis=0),
        tzh[...],
        tzl[...],
    )
    slot = lanes((16, 128)) // 16
    for m in range(16):
        part = 128 * (m // 8)
        value = None
        for h in range(2):
            for q in range(4):
                piece = t[32 * q + 16 * h : 32 * q + 16 * h + 16, part : part + 128]
                piece = roll(piece, 16 * (4 * h + q - m % 8), 1)
                value = piece if value is None else jnp.where(slot == 4 * h + q, piece, value)
        mo[m] = value


def handover(row, col, src, dst, send, recv, own):
    me = row * NCOL + col

    @pl.loop(1, 128)
    def _(k):
        peer = lax.rem(me + k, 128)
        pltpu.make_async_remote_copy(
            src_ref=src.at[peer],
            dst_ref=dst.at[me],
            send_sem=send,
            recv_sem=recv,
            device_id={"row": peer // NCOL, "col": lax.rem(peer, NCOL)},
            device_id_type=MESH,
        ).start()

    copy = pltpu.make_async_copy(src.at[me], dst.at[me], own)
    copy.start()
    copy.wait()
    all_of_them = pltpu.make_async_remote_copy(
        src_ref=src.at[pl.ds(0, 127)],
        dst_ref=dst.at[pl.ds(0, 127)],
        send_sem=send,
        recv_sem=recv,
        device_id={"col": lax.rem(col + 1, NCOL)},
        device_id_type=MESH,
    )
    all_of_them.wait_recv()
    return all_of_them


def neighbours(row, col, fx, fy, x_low, x_high, y_low, y_high, sems, pending):
    copies = []
    for i, (axis, peer, src, dst) in enumerate(
        (
            ("row", lax.rem(row + 1, NROW), fx.at[3], x_low),
            ("row", lax.rem(row + NROW - 1, NROW), fx.at[0], x_high),
            ("col", lax.rem(col + 1, NCOL), fy.at[:, pl.ds(56, 8)], y_low),
            ("col", lax.rem(col + NCOL - 1, NCOL), fy.at[:, pl.ds(0, 8)], y_high),
        )
    ):
        copies.append(
            pltpu.make_async_remote_copy(
                src_ref=src,
                dst_ref=dst,
                send_sem=sems.at[0, i],
                recv_sem=sems.at[1, i],
                device_id={axis: peer},
                device_id_type=MESH,
            )
        )
        copies[-1].start()
    for copy in copies:
        copy.wait_recv()
    pending.extend(copies)


VM = pl.BlockSpec(memory_space=pltpu.VMEM)
ANY = pl.BlockSpec(memory_space=pl.ANY)


def pack(f):
    return jnp.where(lanes((16, 128)) < 64, f[0:16], roll(f[16:32], 64, 1))


def curvatures(below, here, above):
    xx = up(here, 0) - 2.0 * here + down(here, 0)
    yy = up(here, 1) - 2.0 * here + down(here, 1)
    zz = above - 2.0 * here + below
    dx = up(here, 0) - down(here, 0)
    dz = above - below
    xy = (up(dx, 1) - down(dx, 1)) * 0.25
    xz = (up(dz, 0) - down(dz, 0)) * 0.25
    yz = (up(dz, 1) - down(dz, 1)) * 0.25
    return xx, yy, zz, xy, xz, yz


def source(first, out):
    for z in range(NZ):
        xx, yy, zz, xy, xz, yz = curvatures(
            first[(z + 15) % 16], first[z], first[(z + 1) % 16]
        )
        out[z] = pack(xx * (yy + zz) + yy * zz - (xy * xy + xz * xz + yz * yz))


def keep_curvatures(first, kept, zs):
    for z in zs:
        xx, yy, zz, xy, xz, yz = curvatures(
            first[(z + 15) % 16], first[z], first[(z + 1) % 16]
        )
        for i, value in enumerate((yy + zz, xx + zz, xx + yy, -2.0 * xy, -2.0 * xz, -2.0 * yz)):
            kept[i, z] = value


def group_roll(x, s):
    z = lanes(x.shape) % 16
    return jnp.where(z >= s, roll(x, s, 1), roll(x, s - 16, 1))


def barrel(x, amount):
    for bit in (1, 2, 4, 8):
        x = jnp.where((amount & bit) > 0, group_roll(x, bit), x)
    return x


def barrel_16(x, amount):
    for bit in (1, 2, 4):
        x = jnp.where((amount & bit) > 0, roll(x, 16 * bit, 1), x)
    return x


def slots(owner_row, owner_col):
    device = lanes((128, 256), 0)
    chosen_t = jnp.where(device == owner_row, 1.0, 0.0)
    order = jnp.where(lanes((256, 256), 0) < lanes((256, 256), 1), 1.0, 0.0)
    earlier_t = dot(chosen_t.astype(BF16), order.astype(BF16))
    along = jnp.sum(earlier_t * chosen_t, axis=0, keepdims=True)
    along = owner_row * 8 + along.astype(jnp.int32)
    chosen = jnp.where(lanes((256, 128)) == owner_col, 1.0, 0.0)
    order = jnp.where(lanes((256, 256), 0) > lanes((256, 256), 1), 1.0, 0.0)
    earlier = dot(order.astype(BF16), chosen.astype(BF16))
    down_ = jnp.sum(earlier * chosen, axis=1, keepdims=True)
    down_ = owner_col * 8 + down_.astype(jnp.int32)
    return along, down_


def place_tables(along, down_rows, to_slot, from_slot):
    target = jnp.concatenate([along, along + 4], axis=1)
    for i in range(4):
        rows = lanes((256, 512), 0) + 256 * i
        to_slot[pl.ds(256 * i, 256), :] = jnp.where(rows == target, 1.0, 0.0).astype(BF16)
    for i in range(2):
        table = jnp.where(lanes((256, 1024)) == down_rows + 4 * i, 1.0, 0.0)
        from_slot[pl.ds(256 * i, 256), :] = table.astype(BF16)


def paint(first, second, to_slot, ax, ay, az, spread, out, total, fracs, tz, tt):
    piece = lanes((16, 128)) // 32
    for z in range(NZ):
        total[z] = first[z] + SECOND_ORDER * second[z]
    for axis in range(3):
        for z in range(NZ):
            if axis == 2:
                slope = total[(z + 1) % 16, 0:32, :] - total[(z + 15) % 16, 0:32, :]
            elif axis == 1:
                here = total[z, 0:32, :]
                slope = up(here, 1) - down(here, 1)
            else:
                here = total[z]
                slope = (up(here, 0) - down(here, 0))[0:32]
            tz[pl.ds(z, 32, stride=16), :] = 0.5 - 0.5 * slope
        for q in range(4):
            tt[q] = jnp.transpose(tz[pl.ds(128 * q, 128), :])[0:64]
        for q in range(4):
            quarter = [tt[q, pl.ds(v, 16, stride=4), :] for v in range(4)]
            for k in range(4):
                block = roll(quarter[0], -32 * k, 1)
                for v in range(1, 4):
                    block = jnp.where(piece == v, roll(quarter[v], 32 * (v - k), 1), block)
                fracs[axis, pl.ds(16 * (4 * q + k), 16), :] = block
    fx, fy, fz = fracs[0], fracs[1], fracs[2]
    fields = []
    for wx in (1.0 - fx, fx):
        for wy in (1.0 - fy, fy):
            q = wx * wy
            upper = q * fz
            fields.append(q - upper + group_roll(upper, 1))
    box = exact_right(jnp.concatenate(fields, axis=1), spread[...])
    box_0, box_1 = barrel(box[:, :128], az), barrel(box[:, 128:], az)
    lane = lanes((256, 128))
    box_1 = jnp.where(lane == 112, ax.astype(F32), box_1)
    box_1 = jnp.where(lane == 113, ay.astype(F32), box_1)
    stacked = jnp.concatenate([box_0, box_1], axis=0)
    out[...] = exact_left(to_slot[...], stacked).reshape(128, 8, 128)


def weigh_counts(bias, counts, weighted):
    for j in range(8):
        value = None
        for b in range(NBIN):
            term = bias[b] * counts[b, :, pl.ds(128 * j, 128)].astype(F32)
            value = term if value is None else value + term
        weighted[pl.ds(32 * j, 32), :] = value


def own_cells(nbar, bias, arrived, weighted, density, back, dens, pulls):
    data = arrived[...].reshape(1024, 128)
    second = lanes((1024, 128), 0) // 4 % 2
    is_second = second == 1

    def both(lane):
        column = jnp.broadcast_to(data[:, lane : lane + 1], (1024, 128))
        return jnp.where(is_second, column, roll(column, -4, 0)).astype(jnp.int32)

    ax, ay = both(112), both(113)
    flipped = jnp.concatenate(
        [jnp.transpose(data[128 * i : 128 * (i + 1)]) for i in range(8)], axis=1
    )
    second_row = lanes((1, 1024)) // 4 % 2

    def both_row(lane):
        line = flipped[lane : lane + 1]
        line = jnp.where(second_row == 1, line, roll(line, -4, 1))
        return line.astype(jnp.int32)

    ax_row, ay_row = both_row(112), both_row(113)
    base_row = (ay_row >> 3) * 32 + ax_row
    base = (ay >> 3) * 32 + ax
    lane = lanes((1024, 128))
    step = ay & 7
    side_step = (3 * second + 3 + ay) & 7
    stay = lane >= step * 16
    main = barrel_16(jnp.where(lane < 80, data, 0.0), step)
    side_mask = (lane >= 80) & (lane < 112 + 16 * (1 - second))
    side = barrel_16(jnp.where(side_mask, data, 0.0), side_step)
    total = None
    for part, offset in ((main, 2 * second_row), (side, 1)):
        table = jnp.where(lanes((256, 1024), 0) == base_row + offset, 1.0, 0.0).astype(BF16)
        near = split(jnp.where(stay, part, 0.0))
        far = split(jnp.where(stay, 0.0, part))
        t = dot(table, jnp.concatenate([*near, *far], axis=1))
        total = t if total is None else total + t
    near = total[:, :128] + total[:, 128:256]
    far = total[:, 256:384] + total[:, 384:]
    dens[...] = near + jnp.where(lanes((256, 128), 0) >= 32, roll(far, 32, 0), 0.0)
    for j in range(8):
        here = dens[pl.ds(32 * j, 32), :]
        density[:, pl.ds(128 * j, 128)] = here
        contrast = here - 1.0
        pull = weighted[pl.ds(32 * j, 32), :]
        for b in range(NBIN):
            pull = pull - (bias[b] * nbar[b]) * jnp.exp(bias[b] * contrast)
        pulls[pl.ds(32 * j, 32), :] = pull
    pull = pulls[...]
    ahead = jnp.where(lanes((256, 128), 0) < 224, roll(pull, -32, 0), 0.0)
    both_pulls = jnp.concatenate([*split(pull), *split(ahead)], axis=1)

    def picked(offset, amount):
        wide = jnp.concatenate([base + offset, base + offset], axis=1)
        table = jnp.where(lanes((1024, 256)) == wide, 1.0, 0.0).astype(BF16)
        t = dot(table, both_pulls)
        value = jnp.where(stay, t[:, :128] + t[:, 128:256], t[:, 256:384] + t[:, 384:])
        return barrel_16(value, (8 - amount) & 7)

    value = jnp.where(lane < 80, picked(2 * second, step), picked(1, side_step))
    back[...] = value.reshape(128, 8, 128)


def forces(returned, from_slot, az, spread_t, fracs, fx_out, fy_out, fz_out):
    t = exact_left(from_slot[...], returned[...].reshape(1024, 128))
    amount = (16 - az) & 15
    box = jnp.concatenate([barrel(t[:256], amount), barrel(t[256:], amount)], axis=1)
    corner = exact_right(box, spread_t[...])
    fx, fy, fz = fracs[0], fracs[1], fracs[2]
    along, across = [], []
    for d in range(4):
        here = corner[:, 128 * d : 128 * (d + 1)]
        change = group_roll(here, 15) - here
        along.append(here + fz * change)
        across.append(change)
    force_x = (1.0 - fy) * (along[2] - along[0]) + fy * (along[3] - along[1])
    force_y = (1.0 - fx) * (along[1] - along[0]) + fx * (along[3] - along[2])
    force_z = (1.0 - fx) * ((1.0 - fy) * across[0] + fy * across[1]) + fx * (
        (1.0 - fy) * across[2] + fy * across[3]
    )
    piece = lanes((16, 128)) // 32
    for force, out in ((force_x, fx_out), (force_y, fy_out), (force_z, fz_out)):
        for q in range(4):
            group = [force[16 * (4 * q + k) : 16 * (4 * q + k) + 16] for k in range(4)]
            for v in range(4):
                value = roll(group[0], -32 * v, 1)
                for k in range(1, 4):
                    value = jnp.where(piece == k, roll(group[k], 32 * (k - v), 1), value)
                out[q, pl.ds(v, 16, stride=4), :] = value


def divergence(fx, fy, fz, x_low, x_high, y_low, y_high, out, tz):
    def wide(ref):
        return jnp.concatenate([ref[q] for q in range(4)], axis=1)

    def four(value):
        return jnp.concatenate([value] * 4, axis=1)

    def edge(ref, i):
        return jnp.concatenate([ref[q, i : i + 1, :] for q in range(4)], axis=1)

    f = wide(fx)
    lane = lanes((64, 512))
    before = jnp.where(lane < 16, four(roll(x_low[...], 16, 1)), roll(f, 16, 1))
    after = jnp.where(lane >= 496, four(roll(x_high[...], 112, 1)), roll(f, -16, 1))
    total = after - before
    g = wide(fy)
    line = lanes((64, 512), 0)
    before = jnp.where(line == 0, edge(y_low, 7), roll(g, 1, 0))
    after = jnp.where(line == 63, edge(y_high, 0), roll(g, -1, 0))
    total = total + (after - before)
    h = wide(fz)
    z = lane % 16
    after = jnp.where(z == 15, roll(h, 15, 1), roll(h, -1, 1))
    before = jnp.where(z == 0, roll(h, -15, 1), roll(h, 1, 1))
    total = (total + (after - before)) * (0.5 * SECOND_ORDER)
    total = jnp.concatenate([total, jnp.zeros_like(total)], axis=0)
    for q in range(4):
        tz[pl.ds(128 * q, 128), :] = jnp.transpose(total[:, 128 * q : 128 * (q + 1)])
    for z in range(NZ):
        value = tz[pl.ds(z, 32, stride=16), :]
        out[z] = jnp.where(
            lanes((16, 128)) < 64, value[0:16], roll(value[16:32], 64, 1)
        )


def weights(kept, pulled, out, wzz, wxz, wyz):
    for z in range(NZ):
        g = pulled[z]
        wzz[z] = g * kept[2, z]
        wxz[z] = g * kept[4, z]
        wyz[z] = g * kept[5, z]
    for z in range(NZ):
        a, b = (z + 1) % 16, (z + 15) % 16
        g = pulled[z]
        wx, wy, wxy = g * kept[0, z], g * kept[1, z], g * kept[3, z]
        dx = 0.25 * (wxz[a] - wxz[b])
        dy = 0.25 * ((wyz[a] - wyz[b]) + (up(wxy, 0) - down(wxy, 0)))
        along_x = up(wx + dx, 0) + down(wx - dx, 0)
        along_y = up(wy + dy, 1) + down(wy - dy, 1)
        along_z = wzz[a] + wzz[b]
        out[z] = pack(along_x + along_y + along_z - 2.0 * (wx + wy + wzz[z]))


def finish(pulled_modes, last_modes, sums, tzh, tzl, gradient):
    slot = lanes((32, 128)) // 16
    for m in range(16):
        sums[m, 0:32, :] = pulled_modes[m, 0:32, :] * (1.0 / SECOND_ORDER) + last_modes[m, 0:32, :]
    quarters = []
    for q in range(4):
        parts = []
        for p in range(2):
            value = None
            for k in range(8):
                piece = roll(sums[8 * p + k, 0:32, :], 16 * (k - q), 1)
                value = piece if value is None else jnp.where(slot == k, piece, value)
            parts.append(value)
        quarters.append(jnp.concatenate(parts, axis=1))
    t = right_product(jnp.concatenate(quarters, axis=0), tzh[...], tzl[...])
    for q in range(4):
        gradient[:, pl.ds(256 * q, 256)] = t[32 * q : 32 * q + 32]


def columns(rows):
    stack = jnp.concatenate([r.astype(F32) for r in rows] + [jnp.zeros((124, 256), F32)], axis=0)
    turned = jnp.concatenate([jnp.transpose(stack[:, :128]), jnp.transpose(stack[:, 128:])], axis=0)
    return [turned[:, i : i + 1].astype(jnp.int32) for i in range(len(rows))]


N_TABLES = 14


def whole_kernel(nbar, bias, delta, owner, anchor_x, anchor_y, anchor_z, *refs):
    counts_far, tables = refs[0], refs[1 : 1 + N_TABLES]
    gradient, density = refs[1 + N_TABLES : 3 + N_TABLES]
    rest = list(refs[3 + N_TABLES :])

    def take(n):
        taken, rest[:] = rest[:n], rest[n:]
        return taken

    held, (counts,) = take(N_TABLES), take(1)
    buffers = [take(8) for _ in range(4)]
    first, second, pulled, total, wzz, wxz, wyz, kept = take(8)
    src, factor, fracs, tz, tt = take(5)
    payload, arrived, back, returned, dens, pulls, weighted = take(7)
    to_slot, from_slot = take(2)
    fx, fy, fz, x_low, x_high, y_low, y_high = take(7)
    table_sem, *exchange_sems, own, hand_sem, edge_sem = rest
    row, col = lax.axis_index("row"), lax.axis_index("col")
    me = row * NCOL + col
    pending = []

    def semaphores(i):
        return [s.at[i] for s in exchange_sems] + [own.at[i]]

    barrier = pltpu.get_barrier_semaphore()

    @pl.loop(1, 128)
    def _(k):
        peer = lax.rem(me + k, 128)
        pl.semaphore_signal(
            barrier,
            inc=1,
            device_id={"row": peer // NCOL, "col": lax.rem(peer, NCOL)},
            device_id_type=MESH,
        )

    loads = [
        pltpu.make_async_copy(t, h, table_sem.at[i])
        for i, (t, h) in enumerate(zip((*tables, counts_far), (*held, counts)))
    ]
    for load in loads:
        load.start()
    tzh, tzl, *main, spread, spread_t, bzh, bzl = held
    loads[0].wait()
    loads[1].wait()
    delta_modes(delta, tzh, tzl, buffers[0][0])
    pl.semaphore_wait(barrier, 127)

    owner_row = owner[...]
    owner_col, ax, ay, az = columns((owner_row, anchor_x[...], anchor_y[...], anchor_z[...]))

    def get_ready():
        factor[...] = modes_factor(row, col)
        for load in loads[2:]:
            load.wait()

    place = (row, col)
    fill = (
        get_ready,
        lambda: weigh_counts(bias, counts, weighted),
        lambda: place_tables(*slots(owner_row, owner_col), to_slot, from_slot),
        None,
    )
    solve(place, buffers[0], semaphores(0), main, factor, first, pending, fill)
    source(first, src)
    to_modes(src, buffers[1][0])
    fill = (
        lambda: keep_curvatures(first, kept, range(8)),
        None,
        None,
        lambda: keep_curvatures(first, kept, range(8, 16)),
    )
    solve(place, buffers[1], semaphores(1), main, factor, second, pending, fill)
    paint(first, second, to_slot, ax, ay, az, spread, payload, total, fracs, tz, tt)
    pending.append(handover(row, col, payload, arrived, hand_sem.at[0], hand_sem.at[1], hand_sem.at[2]))
    own_cells(nbar, bias, arrived, weighted, density, back, dens, pulls)
    pending.append(handover(row, col, back, returned, hand_sem.at[3], hand_sem.at[4], hand_sem.at[5]))
    forces(returned, from_slot, az, spread_t, fracs, fx, fy, fz)
    neighbours(row, col, fx, fy, x_low, x_high, y_low, y_high, edge_sem, pending)
    divergence(fx, fy, fz, x_low, x_high, y_low, y_high, src, tz)
    to_modes(src, buffers[2][0])
    solve(place, buffers[2], semaphores(2), main, factor, pulled, pending)
    weights(kept, pulled, src, wzz, wxz, wyz)
    to_modes(src, buffers[3][0])
    solve(place, buffers[3], semaphores(3), main, factor, None, pending)
    finish(buffers[2][7], buffers[3][7], total, bzh, bzl, gradient)
    for copy in pending:
        copy.wait_send()


def delta_table():
    t = np.zeros((16, 16, 16, 16))
    for y in range(16):
        t[y, :, :, y] = ZB.T
    return t.reshape(256, 256)


def spread_tables():
    spread = make_spread()
    return [spread.astype(jnp.bfloat16), spread.T.copy().astype(jnp.bfloat16)]


TABLES = [
    *two_terms(delta_table()),
    *make_tables(),
    *spread_tables(),
    *two_terms(delta_table().T.copy()),
]


def on_device(delta, counts, nbar, bias, owner, anchor_x, anchor_y, anchor_z):
    tables = [jnp.asarray(t) for t in TABLES]
    flat = [a.reshape(1, 256) for a in (owner, anchor_x, anchor_y, anchor_z)]
    field = pltpu.VMEM((NZ, XH, 128), F32)
    hand = pltpu.VMEM((128, 8, 128), F32)
    scratch = [pltpu.VMEM(t.shape, BF16) for t in tables] + [pltpu.VMEM(counts.shape, jnp.int32)]
    for _ in range(4):
        for s in ((NROW, 16, 128), (NCOL, 32, 128), (NCOL, 64, 128), (NROW, XH, 128)):
            scratch += [pltpu.VMEM(s, F32), pltpu.VMEM(s, F32)]
    scratch += [field] * 7 + [pltpu.VMEM((6, NZ, XH, 128), F32)]
    scratch += [pltpu.VMEM((NZ, 16, 128), F32), pltpu.VMEM((64, GRID), F32)]
    scratch += [pltpu.VMEM((3, 256, 128), F32), pltpu.VMEM((512, 128), F32)]
    scratch += [pltpu.VMEM((4, 64, 128), F32)]
    scratch += [hand] * 4 + [pltpu.VMEM((256, 128), F32)] * 3
    scratch += [pltpu.VMEM((1024, 512), BF16), pltpu.VMEM((512, 1024), BF16)]
    scratch += [pltpu.VMEM((4, 64, 128), F32)] * 3
    scratch += [pltpu.VMEM((64, 128), F32)] * 2 + [pltpu.VMEM((4, 8, 128), F32)] * 2
    scratch += [pltpu.SemaphoreType.DMA((len(tables) + 1,))]
    for n in (NROW, NCOL, NCOL, NROW):
        scratch += [pltpu.SemaphoreType.DMA((4, n)), pltpu.SemaphoreType.DMA((4, n))]
    scratch += [
        pltpu.SemaphoreType.DMA((4, 4)),
        pltpu.SemaphoreType.DMA((6,)),
        pltpu.SemaphoreType.DMA((2, 4)),
    ]
    smem = pl.BlockSpec(memory_space=pltpu.SMEM)
    return pl.pallas_call(
        whole_kernel,
        out_shape=[
            jax.ShapeDtypeStruct((CX, CY * NZ), F32),
            jax.ShapeDtypeStruct((CX, CY * NZ), F32),
        ],
        in_specs=[smem] * 2 + [VM] * 5 + [ANY] * (1 + len(tables)),
        out_specs=[VM, VM],
        scratch_shapes=scratch,
        compiler_params=pltpu.CompilerParams(
            collective_id=0, has_side_effects=True, vmem_limit_bytes=60 << 20
        ),
        name="whole",
    )(nbar, bias, delta, *flat, counts, *tables)


def solution(mesh):
    return jax.shard_map(
        on_device,
        mesh=mesh,
        in_specs=(
            P("row", "col"),
            P(None, "row", "col"),
            P(),
            P(),
            P(("row", "col"), None),
            P(("row", "col")),
            P(("row", "col")),
            P(("row", "col")),
        ),
        out_specs=(P("row", "col"), P("row", "col")),
        check_vma=False,
    )
```

```python
import functools
import math

import jax
import jax.numpy as jnp
import numpy as np
from jax import lax
from jax.experimental import pallas as pl
from jax.experimental.pallas import tpu as pltpu
from jax.sharding import PartitionSpec as P

GRID, NZ = 512, 16
NROW, NCOL = 16, 8
CX, CY = 32, 64
NBIN = 8
XH = 40
SECOND_ORDER = 3.0 / 7.0
F32, BF16 = jnp.float32, jnp.bfloat16
MESH = pl.DeviceIdType.MESH


def real_basis(n):
    k = np.arange(n)
    rows = []
    for m in range(n):
        if m == 0:
            rows.append(np.full(n, 1.0 / math.sqrt(n)))
        elif m < n // 2:
            rows.append(math.sqrt(2.0 / n) * np.cos(2 * np.pi * (m * k % n) / n))
        elif m == n // 2:
            rows.append((1.0 - 2.0 * (k % 2)) / math.sqrt(n))
        else:
            rows.append(math.sqrt(2.0 / n) * np.sin(2 * np.pi * ((m - n // 2) * k % n) / n))
    return np.stack(rows)


def two_terms(table):
    table = table.astype(np.float32)
    high = table.astype(jnp.bfloat16)
    low = (table - high.astype(np.float32)).astype(jnp.bfloat16)
    return high, low


def make_tables():
    basis = real_basis(GRID)
    r, i = np.divmod(np.arange(256), 16)
    first, second = 32 * r + i, 32 * r + 16 + i
    c, k = np.divmod(np.arange(256), 32)
    low, high = 64 * c + k, 64 * c + 32 + k
    fx = np.stack(
        [
            basis[low][:, first],
            basis[high][:, second],
            basis[high][:, first],
            basis[low][:, second],
        ]
    )
    fx = fx.reshape(4, 4, 64, 256).transpose(1, 0, 2, 3).reshape(1024, 256)
    fy = basis.T
    gy = np.zeros((GRID, NCOL, 128))
    for c in range(NCOL):
        for y in range(-2, CY + 2):
            gy[:, c, y % 128] = basis[:, (CY * c + y) % GRID]
    gx = np.zeros((NROW, XH, GRID))
    for r in range(NROW):
        for x in range(-2, CX + 2):
            gx[r, x % XH] = basis[:, (CX * r + x) % GRID]
    tables = []
    for t in (fx, fy, gy.reshape(GRID, NCOL * 128), gx.reshape(NROW * XH, GRID)):
        tables.extend(two_terms(t))
    return tables


ZB = real_basis(NZ)


def box_lane(a, b, z):
    if a == 0:
        return b * 16 + z
    if a == 2:
        return 128 + b * 16 + z
    return 80 + b * 16 + z if b < 3 else 208 + (b - 3) * 16 + z


def make_spread():
    e = np.zeros((4, 128, 256), np.float32)
    for dx in range(2):
        for dy in range(2):
            for v in range(4):
                for u in range(2):
                    for z in range(16):
                        e[dx * 2 + dy, 32 * v + 16 * u + z, box_lane(u + dx, v + dy, z)] = 1.0
    return e.reshape(512, 256)


def dot(a, b):
    return lax.dot_general(a, b, (((1,), (0,)), ((), ())), preferred_element_type=F32)


def split(x):
    high = x.astype(BF16)
    return high, (x - high.astype(F32)).astype(BF16)


def split_3(x):
    high = x.astype(BF16)
    rest = x - high.astype(F32)
    middle = rest.astype(BF16)
    return high, middle, (rest - middle.astype(F32)).astype(BF16)


def left_product(high, low, pair, last):
    n = last.shape[1]
    t = dot(high, pair)
    u = dot(low, pair)
    return t[:, :n] + ((t[:, n:] + u[:, :n]) + (u[:, n:] + dot(high, last)))


def left_terms(b):
    b0, b1, b2 = split_3(b)
    return jnp.concatenate([b0, b1], axis=1), b2


def right_product(a, high, low):
    m = a.shape[0]
    a0, a1, a2 = split_3(a)
    pair = jnp.concatenate([a0, a1], axis=0)
    t = dot(jnp.concatenate([pair, a2], axis=0), high)
    s = dot(pair, low)
    return t[:m] + ((t[m : 2 * m] + s[:m]) + (s[m:] + t[2 * m :]))


def exact_left(zero_one, b):
    n = b.shape[1]
    t = dot(zero_one, jnp.concatenate(split(b), axis=1))
    return t[:, :n] + t[:, n:]


def exact_right(a, zero_one):
    m = a.shape[0]
    t = dot(jnp.concatenate(split(a), axis=0), zero_one)
    return t[:m] + t[m:]


def lanes(shape, axis=1):
    return lax.broadcasted_iota(jnp.int32, shape, axis)


def roll(x, shift, axis):
    shift = shift % x.shape[axis]
    return x if shift == 0 else pltpu.roll(x, shift, axis)


def up(x, axis):
    return roll(x, -1, axis)


def down(x, axis):
    return roll(x, 1, axis)


def forward_z(v):
    even = [v[0]] + [v[z] + v[16 - z] for z in range(1, 8)] + [v[8]]
    odd = [None] + [v[z] - v[16 - z] for z in range(1, 8)]
    out = []
    for m in range(9):
        s = even[0] * float(ZB[m, 0])
        for z in range(1, 9):
            s = s + even[z] * float(ZB[m, z])
        out.append(s)
    for m in range(9, 16):
        s = odd[1] * float(ZB[m, 1])
        for z in range(2, 8):
            s = s + odd[z] * float(ZB[m, z])
        out.append(s)
    return out


def inverse_z(v):
    out = [None] * 16
    for z in range(9):
        even = v[0] * float(ZB[0, z])
        for m in range(1, 9):
            even = even + v[m] * float(ZB[m, z])
        if z in (0, 8):
            out[z] = even
            continue
        odd = v[9] * float(ZB[9, z])
        for m in range(10, 16):
            odd = odd + v[m] * float(ZB[m, z])
        out[z] = even + odd
        out[16 - z] = even - odd
    return out


class Exchange:
    def __init__(self, n, me, axis, src, dst, send, recv, own, pending):
        self.n, self.me, self.axis = n, me, axis
        self.src, self.dst, self.send, self.recv, self.own = src, dst, send, recv, own
        self.pending = pending

    def copy(self, peer, slot):
        return pltpu.make_async_remote_copy(
            src_ref=self.src.at[peer],
            dst_ref=self.dst.at[slot],
            send_sem=self.send.at[peer],
            recv_sem=self.recv.at[slot],
            device_id={self.axis: peer},
            device_id_type=MESH,
        )

    def start(self, peer):
        copy = self.copy(peer, self.me)
        copy.start()
        self.pending.append(copy)

    def group(self, g, j, size):
        if j:
            for e in range(size):
                self.start(g * size + e)
            return
        for e in range(1, size):
            self.start(g * size + lax.rem(lax.rem(self.me, size) + e, size))
        self.local = pltpu.make_async_copy(
            self.src.at[self.me], self.dst.at[self.me], self.own
        )
        self.local.start()

    def arrive(self):
        self.local.wait()
        for k in range(1, self.n):
            origin = lax.rem(self.me + k, self.n)
            self.copy(origin, origin).wait_recv()


ORDER = (2, 1, 3, 0)


def modes_factor(row, col):
    kx = lanes((64, GRID), 0) + col * 64
    ky = lanes((64, GRID), 1)
    kx = jnp.where(kx <= GRID // 2, kx, kx - GRID // 2).astype(F32) * (2.0 * math.pi / GRID)
    ky = jnp.where(ky <= GRID // 2, ky, ky - GRID // 2).astype(F32) * (2.0 * math.pi / GRID)
    kz = jnp.where(row <= NZ // 2, row, row - NZ // 2)
    kz = jnp.full((64, GRID), kz, jnp.int32).astype(F32) * (2.0 * math.pi / NZ)
    square = kx * kx + ky * ky + kz * kz
    return jnp.where(square > 0, -1.0 / jnp.where(square > 0, square, 1.0), 0.0)


def solve(place, buffers, semaphores, held, factor, out, pending, fill=(None,) * 4):
    row, col = place
    mo, r1, pk, r2, zb, r3, xb, r4 = buffers
    s1, q1, s2, q2, s3, q3, s4, q4, own = semaphores
    fxh, fxl, fyh, fyl, gyh, gyl, gxh, gxl = held
    def groups(me, size):
        return [(lax.rem(lax.div(me, size) + j, 4), j) for j in ORDER]

    swap = Exchange(NROW, row, "row", mo, r1, s1, q1, own.at[0], pending)
    for g, j in groups(row, 4):
        swap.group(g, j, 4)
    if fill[0]:
        fill[0]()
    swap.arrive()

    swap = Exchange(NCOL, col, "col", pk, r2, s2, q2, own.at[1], pending)
    pair, last = left_terms(r1[...].reshape(256, 128))
    low_half = lanes((64, 128)) < 64
    for g, j in groups(col, 2):
        rows = pl.ds(pl.multiple_of(256 * g, 256), 256)
        t = left_product(fxh[rows, :], fxl[rows, :], pair, last)
        packed = jnp.where(low_half, t[:64], t[64:128]) + roll(
            jnp.where(low_half, t[128:192], t[192:]), 64, 1
        )
        pk[pl.ds(2 * g, 2)] = packed.reshape(2, 32, 128)
        swap.group(g, j, 2)
    if fill[1]:
        fill[1]()
    swap.arrive()

    half = lanes((32, 128)) < 64
    top, bottom = [], []
    for p in range(4):
        a, b = r2[2 * p], r2[2 * p + 1]
        top.append(jnp.where(half, a, roll(b, 64, 1)))
        bottom.append(jnp.where(half, roll(a, 64, 1), b))
    full = jnp.concatenate(
        [jnp.concatenate(top, axis=1), jnp.concatenate(bottom, axis=1)], axis=0
    )
    modes = right_product(full, fyh[...], fyl[...]) * factor[...]
    swap = Exchange(NCOL, col, "col", zb, r3, s3, q3, own.at[2], pending)
    pair = jnp.concatenate(split_3(modes), axis=0)
    for g, j in groups(col, 2):
        lane = pl.ds(pl.multiple_of(256 * g, 256), 256)
        t = dot(pair, gyh[:, lane])
        u = dot(pair[:128], gyl[:, lane])
        back = t[:64] + ((t[64:128] + u[:64]) + (u[64:] + t[128:]))
        zb[2 * g] = back[:, :128]
        zb[2 * g + 1] = back[:, 128:]
        swap.group(g, j, 2)
    if fill[2]:
        fill[2]()
    swap.arrive()

    swap = Exchange(NROW, row, "row", xb, r4, s4, q4, own.at[3], pending)
    pair, last = left_terms(r3[...].reshape(GRID, 128))
    for g, j in groups(row, 4):
        rows = pl.ds(pl.multiple_of(4 * XH * g, 4 * XH), 4 * XH)
        t = left_product(gxh[rows, :], gxl[rows, :], pair, last)
        xb[pl.ds(4 * g, 4)] = t.reshape(4, XH, 128)
        swap.group(g, j, 4)
    if fill[3]:
        fill[3]()
    swap.arrive()
    for s in range(5 if out is not None else 0):
        rows = pl.ds(8 * s, 8)
        for z, value in enumerate(inverse_z([r4[m, rows, :] for m in range(16)])):
            out[z, rows, :] = value


def to_modes(src, mo):
    for s in range(2):
        rows = pl.ds(8 * s, 8)
        for m, value in enumerate(forward_z([src[z, rows, :] for z in range(16)])):
            mo[m, rows, :] = value


def delta_modes(delta, tzh, tzl, mo):
    d = delta[...]
    t = right_product(
        jnp.concatenate([d[:, 256 * q : 256 * (q + 1)] for q in range(4)], axis=0),
        tzh[...],
        tzl[...],
    )
    slot = lanes((16, 128)) // 16
    for m in range(16):
        part = 128 * (m // 8)
        value = None
        for h in range(2):
            for q in range(4):
                piece = t[32 * q + 16 * h : 32 * q + 16 * h + 16, part : part + 128]
                piece = roll(piece, 16 * (4 * h + q - m % 8), 1)
                value = piece if value is None else jnp.where(slot == 4 * h + q, piece, value)
        mo[m] = value


class Handover:
    def __init__(self, row, col, src, dst, sems):
        self.me, self.col = row * NCOL + col, col
        self.src, self.dst = src, dst
        self.send, self.recv, self.own = sems

    def groups(self):
        return [(lax.rem(lax.div(self.me, 32) + j, 4), j) for j in ORDER]

    def group(self, g, j):
        @pl.loop(0 if j else 1, 32)
        def _(k):
            peer = 32 * g + lax.rem(lax.rem(self.me, 32) + k, 32)
            pltpu.make_async_remote_copy(
                src_ref=self.src.at[peer],
                dst_ref=self.dst.at[self.me],
                send_sem=self.send,
                recv_sem=self.recv,
                device_id={"row": lax.div(peer, NCOL), "col": lax.rem(peer, NCOL)},
                device_id_type=MESH,
            ).start()

        if j == 0:
            self.local = pltpu.make_async_copy(
                self.src.at[self.me], self.dst.at[self.me], self.own
            )
            self.local.start()

    def arrive(self, pending):
        self.local.wait()
        all_of_them = pltpu.make_async_remote_copy(
            src_ref=self.src.at[pl.ds(0, 127)],
            dst_ref=self.dst.at[pl.ds(0, 127)],
            send_sem=self.send,
            recv_sem=self.recv,
            device_id={"col": lax.rem(self.col + 1, NCOL)},
            device_id_type=MESH,
        )
        all_of_them.wait_recv()
        pending.append(all_of_them)


def neighbours(row, col, fx, fy, x_low, x_high, y_low, y_high, sems, pending):
    copies = []
    for i, (axis, peer, src, dst) in enumerate(
        (
            ("row", lax.rem(row + 1, NROW), fx.at[3], x_low),
            ("row", lax.rem(row + NROW - 1, NROW), fx.at[0], x_high),
            ("col", lax.rem(col + 1, NCOL), fy.at[:, pl.ds(56, 8)], y_low),
            ("col", lax.rem(col + NCOL - 1, NCOL), fy.at[:, pl.ds(0, 8)], y_high),
        )
    ):
        copies.append(
            pltpu.make_async_remote_copy(
                src_ref=src,
                dst_ref=dst,
                send_sem=sems.at[0, i],
                recv_sem=sems.at[1, i],
                device_id={axis: peer},
                device_id_type=MESH,
            )
        )
        copies[-1].start()
    for copy in copies:
        copy.wait_recv()
    pending.extend(copies)


VM = pl.BlockSpec(memory_space=pltpu.VMEM)
ANY = pl.BlockSpec(memory_space=pl.ANY)


def pack(f):
    return jnp.where(lanes((16, 128)) < 64, f[0:16], roll(f[16:32], 64, 1))


def curvatures(below, here, above):
    xx = up(here, 0) - 2.0 * here + down(here, 0)
    yy = up(here, 1) - 2.0 * here + down(here, 1)
    zz = above - 2.0 * here + below
    dx = up(here, 0) - down(here, 0)
    dz = above - below
    xy = (up(dx, 1) - down(dx, 1)) * 0.25
    xz = (up(dz, 0) - down(dz, 0)) * 0.25
    yz = (up(dz, 1) - down(dz, 1)) * 0.25
    return xx, yy, zz, xy, xz, yz


def source(first, out):
    for z in range(NZ):
        xx, yy, zz, xy, xz, yz = curvatures(
            first[(z + 15) % 16], first[z], first[(z + 1) % 16]
        )
        out[z] = pack(xx * (yy + zz) + yy * zz - (xy * xy + xz * xz + yz * yz))


def keep_curvatures(first, kept, zs):
    for z in zs:
        xx, yy, zz, xy, xz, yz = curvatures(
            first[(z + 15) % 16], first[z], first[(z + 1) % 16]
        )
        for i, value in enumerate((yy + zz, xx + zz, xx + yy, -2.0 * xy, -2.0 * xz, -2.0 * yz)):
            kept[i, z] = value


def group_roll(x, s):
    z = lanes(x.shape) % 16
    return jnp.where(z >= s, roll(x, s, 1), roll(x, s - 16, 1))


def barrel(x, amount):
    for bit in (1, 2, 4, 8):
        x = jnp.where((amount & bit) > 0, group_roll(x, bit), x)
    return x


def barrel_16(x, amount):
    for bit in (1, 2, 4):
        x = jnp.where((amount & bit) > 0, roll(x, 16 * bit, 1), x)
    return x


def slots(owner_row, owner_col):
    device = lanes((128, 256), 0)
    chosen_t = jnp.where(device == owner_row, 1.0, 0.0)
    order = jnp.where(lanes((256, 256), 0) < lanes((256, 256), 1), 1.0, 0.0)
    earlier_t = dot(chosen_t.astype(BF16), order.astype(BF16))
    along = jnp.sum(earlier_t * chosen_t, axis=0, keepdims=True)
    along = owner_row * 8 + along.astype(jnp.int32)
    chosen = jnp.where(lanes((256, 128)) == owner_col, 1.0, 0.0)
    order = jnp.where(lanes((256, 256), 0) > lanes((256, 256), 1), 1.0, 0.0)
    earlier = dot(order.astype(BF16), chosen.astype(BF16))
    down_ = jnp.sum(earlier * chosen, axis=1, keepdims=True)
    down_ = owner_col * 8 + down_.astype(jnp.int32)
    return along, down_


def place_tables(along, down_rows, to_slot, from_slot):
    target = jnp.concatenate([along, along + 4], axis=1)
    for i in range(4):
        rows = lanes((256, 512), 0) + 256 * i
        to_slot[pl.ds(256 * i, 256), :] = jnp.where(rows == target, 1.0, 0.0).astype(BF16)
    for i in range(2):
        table = jnp.where(lanes((256, 1024)) == down_rows + 4 * i, 1.0, 0.0)
        from_slot[pl.ds(256 * i, 256), :] = table.astype(BF16)


def paint(first, second, to_slot, ax, ay, az, spread, out, total, fracs, tz, tt, hand):
    piece = lanes((16, 128)) // 32
    for z in range(NZ):
        total[z] = first[z] + SECOND_ORDER * second[z]
    for axis in range(3):
        for z in range(NZ):
            if axis == 2:
                slope = total[(z + 1) % 16, 0:32, :] - total[(z + 15) % 16, 0:32, :]
            elif axis == 1:
                here = total[z, 0:32, :]
                slope = up(here, 1) - down(here, 1)
            else:
                here = total[z]
                slope = (up(here, 0) - down(here, 0))[0:32]
            tz[pl.ds(z, 32, stride=16), :] = 0.5 - 0.5 * slope
        for q in range(4):
            tt[q] = jnp.transpose(tz[pl.ds(128 * q, 128), :])[0:64]
        for q in range(4):
            quarter = [tt[q, pl.ds(v, 16, stride=4), :] for v in range(4)]
            for k in range(4):
                block = roll(quarter[0], -32 * k, 1)
                for v in range(1, 4):
                    block = jnp.where(piece == v, roll(quarter[v], 32 * (v - k), 1), block)
                fracs[axis, pl.ds(16 * (4 * q + k), 16), :] = block
    fx, fy, fz = fracs[0], fracs[1], fracs[2]
    fields = []
    for wx in (1.0 - fx, fx):
        for wy in (1.0 - fy, fy):
            q = wx * wy
            upper = q * fz
            fields.append(q - upper + group_roll(upper, 1))
    box = exact_right(jnp.concatenate(fields, axis=1), spread[...])
    box_0, box_1 = barrel(box[:, :128], az), barrel(box[:, 128:], az)
    lane = lanes((256, 128))
    box_1 = jnp.where(lane == 112, ax.astype(F32), box_1)
    box_1 = jnp.where(lane == 113, ay.astype(F32), box_1)
    stacked = jnp.concatenate([box_0, box_1], axis=0)
    pair = jnp.concatenate(split(stacked), axis=1)
    for g, j in hand.groups():
        t = dot(to_slot[pl.ds(pl.multiple_of(256 * g, 256), 256), :], pair)
        out[pl.ds(32 * g, 32)] = (t[:, :128] + t[:, 128:]).reshape(32, 8, 128)
        hand.group(g, j)


def weigh_counts(bias, counts, weighted):
    for j in range(8):
        value = None
        for b in range(NBIN):
            term = bias[b] * counts[b, :, pl.ds(128 * j, 128)].astype(F32)
            value = term if value is None else value + term
        weighted[pl.ds(32 * j, 32), :] = value


def geometry(data):
    n = data.shape[0]
    second = lanes((n, 128), 0) // 4 % 2

    def both(lane):
        column = jnp.broadcast_to(data[:, lane : lane + 1], (n, 128))
        return jnp.where(second == 1, column, roll(column, -4, 0)).astype(jnp.int32)

    ax, ay = both(112), both(113)
    step = ay & 7
    return (
        second,
        (ay >> 3) * 32 + ax,
        step,
        (3 * second + 3 + ay) & 7,
        lanes((n, 128)) >= step * 16,
    )


def own_cells(nbar, bias, arrived, weighted, density, back, dens, pulls, hand):
    data = arrived[...].reshape(1024, 128)
    second, base, step, side_step, stay = geometry(data)
    flipped = jnp.concatenate(
        [jnp.transpose(data[128 * i : 128 * (i + 1)]) for i in range(8)], axis=1
    )
    second_row = lanes((1, 1024)) // 4 % 2

    def both_row(lane):
        line = flipped[lane : lane + 1]
        line = jnp.where(second_row == 1, line, roll(line, -4, 1))
        return line.astype(jnp.int32)

    ax_row, ay_row = both_row(112), both_row(113)
    base_row = (ay_row >> 3) * 32 + ax_row
    lane = lanes((1024, 128))
    main = barrel_16(jnp.where(lane < 80, data, 0.0), step)
    side_mask = (lane >= 80) & (lane < 112 + 16 * (1 - second))
    side = barrel_16(jnp.where(side_mask, data, 0.0), side_step)
    total = None
    for part, offset in ((main, 2 * second_row), (side, 1)):
        table = jnp.where(lanes((256, 1024), 0) == base_row + offset, 1.0, 0.0).astype(BF16)
        near = split(jnp.where(stay, part, 0.0))
        far = split(jnp.where(stay, 0.0, part))
        t = dot(table, jnp.concatenate([*near, *far], axis=1))
        total = t if total is None else total + t
    near = total[:, :128] + total[:, 128:256]
    far = total[:, 256:384] + total[:, 384:]
    dens[...] = near + jnp.where(lanes((256, 128), 0) >= 32, roll(far, 32, 0), 0.0)
    for j in range(8):
        here = dens[pl.ds(32 * j, 32), :]
        density[:, pl.ds(128 * j, 128)] = here
        contrast = here - 1.0
        pull = weighted[pl.ds(32 * j, 32), :]
        for b in range(NBIN):
            pull = pull - (bias[b] * nbar[b]) * jnp.exp(bias[b] * contrast)
        pulls[pl.ds(32 * j, 32), :] = pull
    pull = pulls[...]
    ahead = jnp.where(lanes((256, 128), 0) < 224, roll(pull, -32, 0), 0.0)
    both_pulls = jnp.concatenate([*split(pull), *split(ahead)], axis=1)

    lane = lanes((256, 128))
    row_of = lanes((256, 256))
    for g, j in hand.groups():
        data = arrived[pl.ds(32 * g, 32)].reshape(256, 128)
        second, base, step, side_step, stay = geometry(data)
        parts = []
        for offset, amount in ((2 * second, step), (1, side_step)):
            wide = base + offset
            table = jnp.where(row_of == jnp.concatenate([wide, wide], axis=1), 1.0, 0.0)
            t = dot(table.astype(BF16), both_pulls)
            value = jnp.where(stay, t[:, :128] + t[:, 128:256], t[:, 256:384] + t[:, 384:])
            parts.append(barrel_16(value, (8 - amount) & 7))
        back[pl.ds(32 * g, 32)] = jnp.where(lane < 80, *parts).reshape(32, 8, 128)
        hand.group(g, j)


def forces(returned, from_slot, az, spread_t, fracs, fx_out, fy_out, fz_out):
    t = exact_left(from_slot[...], returned[...].reshape(1024, 128))
    amount = (16 - az) & 15
    box = jnp.concatenate([barrel(t[:256], amount), barrel(t[256:], amount)], axis=1)
    corner = exact_right(box, spread_t[...])
    fx, fy, fz = fracs[0], fracs[1], fracs[2]
    along, across = [], []
    for d in range(4):
        here = corner[:, 128 * d : 128 * (d + 1)]
        change = group_roll(here, 15) - here
        along.append(here + fz * change)
        across.append(change)
    force_x = (1.0 - fy) * (along[2] - along[0]) + fy * (along[3] - along[1])
    force_y = (1.0 - fx) * (along[1] - along[0]) + fx * (along[3] - along[2])
    force_z = (1.0 - fx) * ((1.0 - fy) * across[0] + fy * across[1]) + fx * (
        (1.0 - fy) * across[2] + fy * across[3]
    )
    piece = lanes((16, 128)) // 32
    for force, out in ((force_x, fx_out), (force_y, fy_out), (force_z, fz_out)):
        for q in range(4):
            group = [force[16 * (4 * q + k) : 16 * (4 * q + k) + 16] for k in range(4)]
            for v in range(4):
                value = roll(group[0], -32 * v, 1)
                for k in range(1, 4):
                    value = jnp.where(piece == k, roll(group[k], 32 * (k - v), 1), value)
                out[q, pl.ds(v, 16, stride=4), :] = value


def divergence(fx, fy, fz, x_low, x_high, y_low, y_high, out, tz):
    def wide(ref):
        return jnp.concatenate([ref[q] for q in range(4)], axis=1)

    def four(value):
        return jnp.concatenate([value] * 4, axis=1)

    def edge(ref, i):
        return jnp.concatenate([ref[q, i : i + 1, :] for q in range(4)], axis=1)

    f = wide(fx)
    lane = lanes((64, 512))
    before = jnp.where(lane < 16, four(roll(x_low[...], 16, 1)), roll(f, 16, 1))
    after = jnp.where(lane >= 496, four(roll(x_high[...], 112, 1)), roll(f, -16, 1))
    total = after - before
    g = wide(fy)
    line = lanes((64, 512), 0)
    before = jnp.where(line == 0, edge(y_low, 7), roll(g, 1, 0))
    after = jnp.where(line == 63, edge(y_high, 0), roll(g, -1, 0))
    total = total + (after - before)
    h = wide(fz)
    z = lane % 16
    after = jnp.where(z == 15, roll(h, 15, 1), roll(h, -1, 1))
    before = jnp.where(z == 0, roll(h, -15, 1), roll(h, 1, 1))
    total = (total + (after - before)) * (0.5 * SECOND_ORDER)
    total = jnp.concatenate([total, jnp.zeros_like(total)], axis=0)
    for q in range(4):
        tz[pl.ds(128 * q, 128), :] = jnp.transpose(total[:, 128 * q : 128 * (q + 1)])
    for z in range(NZ):
        value = tz[pl.ds(z, 32, stride=16), :]
        out[z] = jnp.where(
            lanes((16, 128)) < 64, value[0:16], roll(value[16:32], 64, 1)
        )


def weights(kept, pulled, out, wzz, wxz, wyz):
    for z in range(NZ):
        g = pulled[z]
        wzz[z] = g * kept[2, z]
        wxz[z] = g * kept[4, z]
        wyz[z] = g * kept[5, z]
    for z in range(NZ):
        a, b = (z + 1) % 16, (z + 15) % 16
        g = pulled[z]
        wx, wy, wxy = g * kept[0, z], g * kept[1, z], g * kept[3, z]
        dx = 0.25 * (wxz[a] - wxz[b])
        dy = 0.25 * ((wyz[a] - wyz[b]) + (up(wxy, 0) - down(wxy, 0)))
        along_x = up(wx + dx, 0) + down(wx - dx, 0)
        along_y = up(wy + dy, 1) + down(wy - dy, 1)
        along_z = wzz[a] + wzz[b]
        out[z] = pack(along_x + along_y + along_z - 2.0 * (wx + wy + wzz[z]))


def finish(pulled_modes, last_modes, sums, tzh, tzl, gradient):
    slot = lanes((32, 128)) // 16
    for m in range(16):
        sums[m, 0:32, :] = pulled_modes[m, 0:32, :] * (1.0 / SECOND_ORDER) + last_modes[m, 0:32, :]
    quarters = []
    for q in range(4):
        parts = []
        for p in range(2):
            value = None
            for k in range(8):
                piece = roll(sums[8 * p + k, 0:32, :], 16 * (k - q), 1)
                value = piece if value is None else jnp.where(slot == k, piece, value)
            parts.append(value)
        quarters.append(jnp.concatenate(parts, axis=1))
    t = right_product(jnp.concatenate(quarters, axis=0), tzh[...], tzl[...])
    for q in range(4):
        gradient[:, pl.ds(256 * q, 256)] = t[32 * q : 32 * q + 32]


def columns(rows):
    stack = jnp.concatenate([r.astype(F32) for r in rows] + [jnp.zeros((124, 256), F32)], axis=0)
    turned = jnp.concatenate([jnp.transpose(stack[:, :128]), jnp.transpose(stack[:, 128:])], axis=0)
    return [turned[:, i : i + 1].astype(jnp.int32) for i in range(len(rows))]


N_TABLES = 14


def whole_kernel(nbar, bias, delta, owner, anchor_x, anchor_y, anchor_z, *refs):
    counts_far, tables = refs[0], refs[1 : 1 + N_TABLES]
    gradient, density = refs[1 + N_TABLES : 3 + N_TABLES]
    rest = list(refs[3 + N_TABLES :])

    def take(n):
        taken, rest[:] = rest[:n], rest[n:]
        return taken

    held, (counts,) = take(N_TABLES), take(1)
    buffers = [take(8) for _ in range(4)]
    first, second, pulled, total, wzz, wxz, wyz, kept = take(8)
    src, factor, fracs, tz, tt = take(5)
    payload, arrived, back, returned, dens, pulls, weighted = take(7)
    to_slot, from_slot = take(2)
    fx, fy, fz, x_low, x_high, y_low, y_high = take(7)
    table_sem, *exchange_sems, own, hand_sem, edge_sem = rest
    row, col = lax.axis_index("row"), lax.axis_index("col")
    me = row * NCOL + col
    pending = []

    def semaphores(i):
        return [s.at[i] for s in exchange_sems] + [own.at[i]]

    barrier = pltpu.get_barrier_semaphore()

    @pl.loop(1, 128)
    def _(k):
        peer = lax.rem(me + k, 128)
        pl.semaphore_signal(
            barrier,
            inc=1,
            device_id={"row": peer // NCOL, "col": lax.rem(peer, NCOL)},
            device_id_type=MESH,
        )

    loads = [
        pltpu.make_async_copy(t, h, table_sem.at[i])
        for i, (t, h) in enumerate(zip((*tables, counts_far), (*held, counts)))
    ]
    for load in loads:
        load.start()
    tzh, tzl, *main, spread, spread_t, bzh, bzl = held
    loads[0].wait()
    loads[1].wait()
    delta_modes(delta, tzh, tzl, buffers[0][0])
    pl.semaphore_wait(barrier, 127)

    owner_row = owner[...]
    owner_col, ax, ay, az = columns((owner_row, anchor_x[...], anchor_y[...], anchor_z[...]))

    def get_ready():
        factor[...] = modes_factor(row, col)
        for load in loads[2:]:
            load.wait()

    place = (row, col)
    fill = (
        get_ready,
        lambda: weigh_counts(bias, counts, weighted),
        lambda: place_tables(*slots(owner_row, owner_col), to_slot, from_slot),
        None,
    )
    solve(place, buffers[0], semaphores(0), main, factor, first, pending, fill)
    source(first, src)
    to_modes(src, buffers[1][0])
    fill = (
        lambda: keep_curvatures(first, kept, range(8)),
        None,
        None,
        lambda: keep_curvatures(first, kept, range(8, 16)),
    )
    solve(place, buffers[1], semaphores(1), main, factor, second, pending, fill)
    hand = Handover(row, col, payload, arrived, [hand_sem.at[i] for i in range(3)])
    paint(first, second, to_slot, ax, ay, az, spread, payload, total, fracs, tz, tt, hand)
    hand.arrive(pending)
    hand = Handover(row, col, back, returned, [hand_sem.at[i] for i in range(3, 6)])
    own_cells(nbar, bias, arrived, weighted, density, back, dens, pulls, hand)
    hand.arrive(pending)
    forces(returned, from_slot, az, spread_t, fracs, fx, fy, fz)
    neighbours(row, col, fx, fy, x_low, x_high, y_low, y_high, edge_sem, pending)
    divergence(fx, fy, fz, x_low, x_high, y_low, y_high, src, tz)
    to_modes(src, buffers[2][0])
    solve(place, buffers[2], semaphores(2), main, factor, pulled, pending)
    weights(kept, pulled, src, wzz, wxz, wyz)
    to_modes(src, buffers[3][0])
    solve(place, buffers[3], semaphores(3), main, factor, None, pending)
    finish(buffers[2][7], buffers[3][7], total, bzh, bzl, gradient)
    for copy in pending:
        copy.wait_send()


def delta_table():
    t = np.zeros((16, 16, 16, 16))
    for y in range(16):
        t[y, :, :, y] = ZB.T
    return t.reshape(256, 256)


def spread_tables():
    spread = make_spread()
    return [spread.astype(jnp.bfloat16), spread.T.copy().astype(jnp.bfloat16)]


TABLES = [
    *two_terms(delta_table()),
    *make_tables(),
    *spread_tables(),
    *two_terms(delta_table().T.copy()),
]


def on_device(delta, counts, nbar, bias, owner, anchor_x, anchor_y, anchor_z):
    tables = [jnp.asarray(t) for t in TABLES]
    flat = [a.reshape(1, 256) for a in (owner, anchor_x, anchor_y, anchor_z)]
    field = pltpu.VMEM((NZ, XH, 128), F32)
    hand = pltpu.VMEM((128, 8, 128), F32)
    scratch = [pltpu.VMEM(t.shape, BF16) for t in tables] + [pltpu.VMEM(counts.shape, jnp.int32)]
    for _ in range(4):
        for s in ((NROW, 16, 128), (NCOL, 32, 128), (NCOL, 64, 128), (NROW, XH, 128)):
            scratch += [pltpu.VMEM(s, F32), pltpu.VMEM(s, F32)]
    scratch += [field] * 7 + [pltpu.VMEM((6, NZ, XH, 128), F32)]
    scratch += [pltpu.VMEM((NZ, 16, 128), F32), pltpu.VMEM((64, GRID), F32)]
    scratch += [pltpu.VMEM((3, 256, 128), F32), pltpu.VMEM((512, 128), F32)]
    scratch += [pltpu.VMEM((4, 64, 128), F32)]
    scratch += [hand] * 4 + [pltpu.VMEM((256, 128), F32)] * 3
    scratch += [pltpu.VMEM((1024, 512), BF16), pltpu.VMEM((512, 1024), BF16)]
    scratch += [pltpu.VMEM((4, 64, 128), F32)] * 3
    scratch += [pltpu.VMEM((64, 128), F32)] * 2 + [pltpu.VMEM((4, 8, 128), F32)] * 2
    scratch += [pltpu.SemaphoreType.DMA((len(tables) + 1,))]
    for n in (NROW, NCOL, NCOL, NROW):
        scratch += [pltpu.SemaphoreType.DMA((4, n)), pltpu.SemaphoreType.DMA((4, n))]
    scratch += [
        pltpu.SemaphoreType.DMA((4, 4)),
        pltpu.SemaphoreType.DMA((6,)),
        pltpu.SemaphoreType.DMA((2, 4)),
    ]
    smem = pl.BlockSpec(memory_space=pltpu.SMEM)
    return pl.pallas_call(
        whole_kernel,
        out_shape=[
            jax.ShapeDtypeStruct((CX, CY * NZ), F32),
            jax.ShapeDtypeStruct((CX, CY * NZ), F32),
        ],
        in_specs=[smem] * 2 + [VM] * 5 + [ANY] * (1 + len(tables)),
        out_specs=[VM, VM],
        scratch_shapes=scratch,
        compiler_params=pltpu.CompilerParams(
            collective_id=0, has_side_effects=True, vmem_limit_bytes=60 << 20
        ),
        name="whole",
    )(nbar, bias, delta, *flat, counts, *tables)


def solution(mesh):
    return jax.shard_map(
        on_device,
        mesh=mesh,
        in_specs=(
            P("row", "col"),
            P(None, "row", "col"),
            P(),
            P(),
            P(("row", "col"), None),
            P(("row", "col")),
            P(("row", "col")),
            P(("row", "col")),
        ),
        out_specs=(P("row", "col"), P("row", "col")),
        check_vma=False,
    )
```

```python
import functools
import math

import jax
import jax.numpy as jnp
import numpy as np
from jax import lax
from jax.experimental import pallas as pl
from jax.experimental.pallas import tpu as pltpu
from jax.sharding import PartitionSpec as P

GRID, NZ = 512, 16
NROW, NCOL = 16, 8
CX, CY = 32, 64
NBIN = 8
XH = 40
SECOND_ORDER = 3.0 / 7.0
F32, BF16 = jnp.float32, jnp.bfloat16
MESH = pl.DeviceIdType.MESH


def real_basis(n):
    k = np.arange(n)
    rows = []
    for m in range(n):
        if m == 0:
            rows.append(np.full(n, 1.0 / math.sqrt(n)))
        elif m < n // 2:
            rows.append(math.sqrt(2.0 / n) * np.cos(2 * np.pi * (m * k % n) / n))
        elif m == n // 2:
            rows.append((1.0 - 2.0 * (k % 2)) / math.sqrt(n))
        else:
            rows.append(math.sqrt(2.0 / n) * np.sin(2 * np.pi * ((m - n // 2) * k % n) / n))
    return np.stack(rows)


def two_terms(table):
    table = table.astype(np.float32)
    high = table.astype(jnp.bfloat16)
    low = (table - high.astype(np.float32)).astype(jnp.bfloat16)
    return high, low


def make_tables():
    basis = real_basis(GRID)
    r, i = np.divmod(np.arange(256), 16)
    first, second = 32 * r + i, 32 * r + 16 + i
    c, k = np.divmod(np.arange(256), 32)
    low, high = 64 * c + k, 64 * c + 32 + k
    fx = np.stack(
        [
            basis[low][:, first],
            basis[high][:, second],
            basis[high][:, first],
            basis[low][:, second],
        ]
    )
    fx = fx.reshape(4, 4, 64, 256).transpose(1, 0, 2, 3).reshape(1024, 256)
    hx = np.stack(
        [
            basis[low][:, first].T,
            basis[high][:, second].T,
            basis[low][:, second].T,
            basis[high][:, first].T,
        ]
    )
    hx = hx.reshape(4, 4, 64, 256).transpose(1, 0, 2, 3).reshape(1024, 256)
    fy = basis.T
    gy = np.zeros((GRID, NCOL, 128))
    for c in range(NCOL):
        for y in range(-2, CY + 2):
            gy[:, c, y % 128] = basis[:, (CY * c + y) % GRID]
    gx = np.zeros((NROW, XH, GRID))
    for r in range(NROW):
        for x in range(-2, CX + 2):
            gx[r, x % XH] = basis[:, (CX * r + x) % GRID]
    tables = []
    for t in (fx, fy, gy.reshape(GRID, NCOL * 128), gx.reshape(NROW * XH, GRID), hx):
        tables.extend(two_terms(t))
    return tables


ZB = real_basis(NZ)


def box_lane(a, b, z):
    if a == 0:
        return b * 16 + z
    if a == 2:
        return 128 + b * 16 + z
    return 80 + b * 16 + z if b < 3 else 208 + (b - 3) * 16 + z


def make_spread():
    e = np.zeros((4, 128, 256), np.float32)
    for dx in range(2):
        for dy in range(2):
            for v in range(4):
                for u in range(2):
                    for z in range(16):
                        e[dx * 2 + dy, 32 * v + 16 * u + z, box_lane(u + dx, v + dy, z)] = 1.0
    return e.reshape(512, 256)


def dot(a, b):
    return lax.dot_general(a, b, (((1,), (0,)), ((), ())), preferred_element_type=F32)


def dot_turned(a, b):
    return lax.dot_general(a, b, (((1,), (1,)), ((), ())), preferred_element_type=F32)


def split(x):
    high = x.astype(BF16)
    return high, (x - high.astype(F32)).astype(BF16)


def split_3(x):
    high = x.astype(BF16)
    rest = x - high.astype(F32)
    middle = rest.astype(BF16)
    return high, middle, (rest - middle.astype(F32)).astype(BF16)


def left_product(high, low, pair, last):
    n = last.shape[1]
    t = dot(high, pair)
    u = dot(low, pair)
    return t[:, :n] + ((t[:, n:] + u[:, :n]) + (u[:, n:] + dot(high, last)))


def left_terms(b):
    b0, b1, b2 = split_3(b)
    return jnp.concatenate([b0, b1], axis=1), b2


def right_product(a, high, low):
    m = a.shape[0]
    a0, a1, a2 = split_3(a)
    pair = jnp.concatenate([a0, a1], axis=0)
    t = dot(jnp.concatenate([pair, a2], axis=0), high)
    s = dot(pair, low)
    return t[:m] + ((t[m : 2 * m] + s[:m]) + (s[m:] + t[2 * m :]))


def exact_left(zero_one, b):
    n = b.shape[1]
    t = dot(zero_one, jnp.concatenate(split(b), axis=1))
    return t[:, :n] + t[:, n:]


def exact_right(a, zero_one):
    m = a.shape[0]
    t = dot(jnp.concatenate(split(a), axis=0), zero_one)
    return t[:m] + t[m:]


def lanes(shape, axis=1):
    return lax.broadcasted_iota(jnp.int32, shape, axis)


def roll(x, shift, axis):
    shift = shift % x.shape[axis]
    return x if shift == 0 else pltpu.roll(x, shift, axis)


def up(x, axis):
    return roll(x, -1, axis)


def down(x, axis):
    return roll(x, 1, axis)


def forward_z(v):
    even = [v[0]] + [v[z] + v[16 - z] for z in range(1, 8)] + [v[8]]
    odd = [None] + [v[z] - v[16 - z] for z in range(1, 8)]
    out = []
    for m in range(9):
        s = even[0] * float(ZB[m, 0])
        for z in range(1, 9):
            s = s + even[z] * float(ZB[m, z])
        out.append(s)
    for m in range(9, 16):
        s = odd[1] * float(ZB[m, 1])
        for z in range(2, 8):
            s = s + odd[z] * float(ZB[m, z])
        out.append(s)
    return out


def inverse_z(v):
    out = [None] * 16
    for z in range(9):
        even = v[0] * float(ZB[0, z])
        for m in range(1, 9):
            even = even + v[m] * float(ZB[m, z])
        if z in (0, 8):
            out[z] = even
            continue
        odd = v[9] * float(ZB[9, z])
        for m in range(10, 16):
            odd = odd + v[m] * float(ZB[m, z])
        out[z] = even + odd
        out[16 - z] = even - odd
    return out


class Exchange:
    def __init__(self, n, me, axis, src, dst, send, recv, own, pending):
        self.n, self.me, self.axis = n, me, axis
        self.src, self.dst, self.send, self.recv, self.own = src, dst, send, recv, own
        self.pending = pending

    def copy(self, peer, slot):
        return pltpu.make_async_remote_copy(
            src_ref=self.src.at[peer],
            dst_ref=self.dst.at[slot],
            send_sem=self.send.at[peer],
            recv_sem=self.recv.at[slot],
            device_id={self.axis: peer},
            device_id_type=MESH,
        )

    def start(self, peer):
        copy = self.copy(peer, self.me)
        copy.start()
        self.pending.append(copy)

    def group(self, g, j, size):
        if j:
            for e in range(size):
                self.start(g * size + e)
            return
        for e in range(1, size):
            self.start(g * size + lax.rem(lax.rem(self.me, size) + e, size))
        self.local = pltpu.make_async_copy(
            self.src.at[self.me], self.dst.at[self.me], self.own
        )
        self.local.start()

    def arrive(self):
        self.local.wait()
        for k in range(1, self.n):
            origin = lax.rem(self.me + k, self.n)
            self.copy(origin, origin).wait_recv()


ORDER = (2, 1, 3, 0)


def modes_factor(row, col):
    kx = lanes((64, GRID), 0) + col * 64
    ky = lanes((64, GRID), 1)
    kx = jnp.where(kx <= GRID // 2, kx, kx - GRID // 2).astype(F32) * (2.0 * math.pi / GRID)
    ky = jnp.where(ky <= GRID // 2, ky, ky - GRID // 2).astype(F32) * (2.0 * math.pi / GRID)
    kz = jnp.where(row <= NZ // 2, row, row - NZ // 2)
    kz = jnp.full((64, GRID), kz, jnp.int32).astype(F32) * (2.0 * math.pi / NZ)
    square = kx * kx + ky * ky + kz * kz
    return jnp.where(square > 0, -1.0 / jnp.where(square > 0, square, 1.0), 0.0)


def solve(place, buffers, semaphores, held, factor, out, pending, fill=(None,) * 4):
    row, col = place
    mo, r1, pk, r2, zb, r3, xb, r4 = buffers
    s1, q1, s2, q2, s3, q3, s4, q4, own = semaphores
    fxh, fxl, fyh, fyl, gyh, gyl, gxh, gxl, hxh, hxl = held
    def groups(me, size):
        return [(lax.rem(lax.div(me, size) + j, 4), j) for j in ORDER]

    swap = Exchange(NROW, row, "row", mo, r1, s1, q1, own.at[0], pending)
    for g, j in groups(row, 4):
        swap.group(g, j, 4)
    if fill[0]:
        fill[0]()
    swap.arrive()

    swap = Exchange(NCOL, col, "col", pk, r2, s2, q2, own.at[1], pending)
    pair, last = left_terms(r1[...].reshape(256, 128))
    low_half = lanes((64, 128)) < 64
    for g, j in groups(col, 2):
        rows = pl.ds(pl.multiple_of(256 * g, 256), 256)
        t = left_product(fxh[rows, :], fxl[rows, :], pair, last)
        packed = jnp.where(low_half, t[:64], t[64:128]) + roll(
            jnp.where(low_half, t[128:192], t[192:]), 64, 1
        )
        pk[pl.ds(2 * g, 2)] = packed.reshape(2, 32, 128)
        swap.group(g, j, 2)
    if fill[1]:
        fill[1]()
    swap.arrive()

    half = lanes((32, 128)) < 64
    top, bottom = [], []
    for p in range(4):
        a, b = r2[2 * p], r2[2 * p + 1]
        top.append(jnp.where(half, a, roll(b, 64, 1)))
        bottom.append(jnp.where(half, roll(a, 64, 1), b))
    full = jnp.concatenate(
        [jnp.concatenate(top, axis=1), jnp.concatenate(bottom, axis=1)], axis=0
    )
    modes = right_product(full, fyh[...], fyl[...]) * factor[...]
    swap = Exchange(NCOL, col, "col", zb, r3, s3, q3, own.at[2], pending)
    pair = jnp.concatenate(split_3(modes), axis=0)
    for g, j in groups(col, 2) if out is None else ():
        rows = pl.ds(pl.multiple_of(128 * g, 128), 128)
        t = dot_turned(pair, fyh[rows, :])
        u = dot_turned(pair[:128], fyl[rows, :])
        back = t[:64] + ((t[64:128] + u[:64]) + (u[64:] + t[128:]))
        a, b = back[:32], back[32:]
        zb[2 * g] = jnp.where(half, a, roll(b, 64, 1))
        zb[2 * g + 1] = jnp.where(half, roll(a, 64, 1), b)
        swap.group(g, j, 2)
    for g, j in groups(col, 2) if out is not None else ():
        lane = pl.ds(pl.multiple_of(256 * g, 256), 256)
        t = dot(pair, gyh[:, lane])
        u = dot(pair[:128], gyl[:, lane])
        back = t[:64] + ((t[64:128] + u[:64]) + (u[64:] + t[128:]))
        zb[2 * g] = back[:, :128]
        zb[2 * g + 1] = back[:, 128:]
        swap.group(g, j, 2)
    if fill[2]:
        fill[2]()
    swap.arrive()

    swap = Exchange(NROW, row, "row", xb, r4, s4, q4, own.at[3], pending)
    pair, last = left_terms(r3[...].reshape(-1, 128))
    for g, j in groups(row, 4) if out is None else ():
        rows = pl.ds(pl.multiple_of(256 * g, 256), 256)
        t = left_product(hxh[rows, :], hxl[rows, :], pair, last)
        packed = jnp.where(low_half, t[:64], t[64:128]) + roll(
            jnp.where(low_half, t[128:192], t[192:]), 64, 1
        )
        xb[pl.ds(4 * g, 4)] = packed.reshape(4, 16, 128)
        swap.group(g, j, 4)
    for g, j in groups(row, 4) if out is not None else ():
        rows = pl.ds(pl.multiple_of(4 * XH * g, 4 * XH), 4 * XH)
        t = left_product(gxh[rows, :], gxl[rows, :], pair, last)
        xb[pl.ds(4 * g, 4)] = t.reshape(4, XH, 128)
        swap.group(g, j, 4)
    if fill[3]:
        fill[3]()
    swap.arrive()
    for s in range(5 if out is not None else 0):
        rows = pl.ds(8 * s, 8)
        for z, value in enumerate(inverse_z([r4[m, rows, :] for m in range(16)])):
            out[z, rows, :] = value


def to_modes(src, mo):
    for s in range(2):
        rows = pl.ds(8 * s, 8)
        for m, value in enumerate(forward_z([src[z, rows, :] for z in range(16)])):
            mo[m, rows, :] = value


def delta_modes(delta, tzh, tzl, mo):
    d = delta[...]
    t = right_product(
        jnp.concatenate([d[:, 256 * q : 256 * (q + 1)] for q in range(4)], axis=0),
        tzh[...],
        tzl[...],
    )
    slot = lanes((16, 128)) // 16
    for m in range(16):
        part = 128 * (m // 8)
        value = None
        for h in range(2):
            for q in range(4):
                piece = t[32 * q + 16 * h : 32 * q + 16 * h + 16, part : part + 128]
                piece = roll(piece, 16 * (4 * h + q - m % 8), 1)
                value = piece if value is None else jnp.where(slot == 4 * h + q, piece, value)
        mo[m] = value


class Handover:
    def __init__(self, row, col, src, dst, sems):
        self.me, self.col = row * NCOL + col, col
        self.src, self.dst = src, dst
        self.send, self.recv, self.own = sems

    def groups(self):
        return [(lax.rem(lax.div(self.me, 32) + j, 4), j) for j in ORDER]

    def group(self, g, j):
        @pl.loop(0 if j else 1, 32)
        def _(k):
            peer = 32 * g + lax.rem(lax.rem(self.me, 32) + k, 32)
            pltpu.make_async_remote_copy(
                src_ref=self.src.at[peer],
                dst_ref=self.dst.at[self.me],
                send_sem=self.send,
                recv_sem=self.recv,
                device_id={"row": lax.div(peer, NCOL), "col": lax.rem(peer, NCOL)},
                device_id_type=MESH,
            ).start()

        if j == 0:
            self.local = pltpu.make_async_copy(
                self.src.at[self.me], self.dst.at[self.me], self.own
            )
            self.local.start()

    def arrive(self, pending):
        self.local.wait()
        all_of_them = pltpu.make_async_remote_copy(
            src_ref=self.src.at[pl.ds(0, 127)],
            dst_ref=self.dst.at[pl.ds(0, 127)],
            send_sem=self.send,
            recv_sem=self.recv,
            device_id={"col": lax.rem(self.col + 1, NCOL)},
            device_id_type=MESH,
        )
        all_of_them.wait_recv()
        pending.append(all_of_them)


def start_edges(row, col, axis, field, low, high, sems):
    if axis == 0:
        n, me, name, last, first = NROW, row, "row", field.at[3], field.at[0]
    else:
        n, me, name = NCOL, col, "col"
        last, first = field.at[:, pl.ds(56, 8)], field.at[:, pl.ds(0, 8)]
    copies = []
    for i, (step, src, dst) in enumerate(((1, last, low), (n - 1, first, high))):
        copy = pltpu.make_async_remote_copy(
            src_ref=src,
            dst_ref=dst,
            send_sem=sems.at[0, 2 * axis + i],
            recv_sem=sems.at[1, 2 * axis + i],
            device_id={name: lax.rem(me + step, n)},
            device_id_type=MESH,
        )
        copy.start()
        copies.append(copy)
    return copies


VM = pl.BlockSpec(memory_space=pltpu.VMEM)
ANY = pl.BlockSpec(memory_space=pl.ANY)


def pack(f):
    return jnp.where(lanes((16, 128)) < 64, f[0:16], roll(f[16:32], 64, 1))


def curvatures(below, here, above):
    xx = up(here, 0) - 2.0 * here + down(here, 0)
    yy = up(here, 1) - 2.0 * here + down(here, 1)
    zz = above - 2.0 * here + below
    dx = up(here, 0) - down(here, 0)
    dz = above - below
    xy = (up(dx, 1) - down(dx, 1)) * 0.25
    xz = (up(dz, 0) - down(dz, 0)) * 0.25
    yz = (up(dz, 1) - down(dz, 1)) * 0.25
    return xx, yy, zz, xy, xz, yz


def source(first, out):
    for z in range(NZ):
        xx, yy, zz, xy, xz, yz = curvatures(
            first[(z + 15) % 16], first[z], first[(z + 1) % 16]
        )
        out[z] = pack(xx * (yy + zz) + yy * zz - (xy * xy + xz * xz + yz * yz))


def keep_curvatures(first, kept, zs):
    for z in zs:
        xx, yy, zz, xy, xz, yz = curvatures(
            first[(z + 15) % 16], first[z], first[(z + 1) % 16]
        )
        for i, value in enumerate((yy + zz, xx + zz, xx + yy, -2.0 * xy, -2.0 * xz, -2.0 * yz)):
            kept[i, z] = value


def group_roll(x, s):
    z = lanes(x.shape) % 16
    return jnp.where(z >= s, roll(x, s, 1), roll(x, s - 16, 1))


def barrel(x, amount):
    for bit in (1, 2, 4, 8):
        x = jnp.where((amount & bit) > 0, group_roll(x, bit), x)
    return x


def barrel_16(x, amount):
    for bit in (1, 2, 4):
        x = jnp.where((amount & bit) > 0, roll(x, 16 * bit, 1), x)
    return x


def slots(owner_row, owner_col):
    device = lanes((128, 256), 0)
    chosen_t = jnp.where(device == owner_row, 1.0, 0.0)
    order = jnp.where(lanes((256, 256), 0) < lanes((256, 256), 1), 1.0, 0.0)
    earlier_t = dot(chosen_t.astype(BF16), order.astype(BF16))
    along = jnp.sum(earlier_t * chosen_t, axis=0, keepdims=True)
    along = owner_row * 8 + along.astype(jnp.int32)
    chosen = jnp.where(lanes((256, 128)) == owner_col, 1.0, 0.0)
    order = jnp.where(lanes((256, 256), 0) > lanes((256, 256), 1), 1.0, 0.0)
    earlier = dot(order.astype(BF16), chosen.astype(BF16))
    down_ = jnp.sum(earlier * chosen, axis=1, keepdims=True)
    down_ = owner_col * 8 + down_.astype(jnp.int32)
    return along, down_


def place_tables(along, down_rows, to_slot, from_slot):
    target = jnp.concatenate([along, along + 4], axis=1)
    for i in range(4):
        rows = lanes((256, 512), 0) + 256 * i
        to_slot[pl.ds(256 * i, 256), :] = jnp.where(rows == target, 1.0, 0.0).astype(BF16)
    for i in range(2):
        table = jnp.where(lanes((256, 1024)) == down_rows + 4 * i, 1.0, 0.0)
        from_slot[pl.ds(256 * i, 256), :] = table.astype(BF16)


def paint(first, second, to_slot, ax, ay, az, spread, out, total, fracs, tz, tt, hand):
    piece = lanes((16, 128)) // 32
    for z in range(NZ):
        total[z] = first[z] + SECOND_ORDER * second[z]
    for axis in range(3):
        for z in range(NZ):
            if axis == 2:
                slope = total[(z + 1) % 16, 0:32, :] - total[(z + 15) % 16, 0:32, :]
            elif axis == 1:
                here = total[z, 0:32, :]
                slope = up(here, 1) - down(here, 1)
            else:
                here = total[z]
                slope = (up(here, 0) - down(here, 0))[0:32]
            tz[pl.ds(z, 32, stride=16), :] = 0.5 - 0.5 * slope
        for q in range(4):
            tt[q] = jnp.transpose(tz[pl.ds(128 * q, 128), :])[0:64]
        for q in range(4):
            quarter = [tt[q, pl.ds(v, 16, stride=4), :] for v in range(4)]
            for k in range(4):
                block = roll(quarter[0], -32 * k, 1)
                for v in range(1, 4):
                    block = jnp.where(piece == v, roll(quarter[v], 32 * (v - k), 1), block)
                fracs[axis, pl.ds(16 * (4 * q + k), 16), :] = block
    fx, fy, fz = fracs[0], fracs[1], fracs[2]
    fields = []
    for wx in (1.0 - fx, fx):
        for wy in (1.0 - fy, fy):
            q = wx * wy
            upper = q * fz
            fields.append(q - upper + group_roll(upper, 1))
    box = exact_right(jnp.concatenate(fields, axis=1), spread[...])
    box_0, box_1 = barrel(box[:, :128], az), barrel(box[:, 128:], az)
    lane = lanes((256, 128))
    box_1 = jnp.where(lane == 112, ax.astype(F32), box_1)
    box_1 = jnp.where(lane == 113, ay.astype(F32), box_1)
    stacked = jnp.concatenate([box_0, box_1], axis=0)
    pair = jnp.concatenate(split(stacked), axis=1)
    for g, j in hand.groups():
        t = dot(to_slot[pl.ds(pl.multiple_of(256 * g, 256), 256), :], pair)
        out[pl.ds(32 * g, 32)] = (t[:, :128] + t[:, 128:]).reshape(32, 8, 128)
        hand.group(g, j)


def weigh_counts(bias, counts, weighted):
    for j in range(8):
        value = None
        for b in range(NBIN):
            term = bias[b] * counts[b, :, pl.ds(128 * j, 128)].astype(F32)
            value = term if value is None else value + term
        weighted[pl.ds(32 * j, 32), :] = value


def geometry(data):
    n = data.shape[0]
    second = lanes((n, 128), 0) // 4 % 2

    def both(lane):
        column = jnp.broadcast_to(data[:, lane : lane + 1], (n, 128))
        return jnp.where(second == 1, column, roll(column, -4, 0)).astype(jnp.int32)

    ax, ay = both(112), both(113)
    step = ay & 7
    return (
        second,
        (ay >> 3) * 32 + ax,
        step,
        (3 * second + 3 + ay) & 7,
        lanes((n, 128)) >= step * 16,
    )


def own_cells(nbar, bias, arrived, weighted, density, back, dens, pulls, hand):
    data = arrived[...].reshape(1024, 128)
    second, base, step, side_step, stay = geometry(data)
    flipped = jnp.concatenate(
        [jnp.transpose(data[128 * i : 128 * (i + 1)]) for i in range(8)], axis=1
    )
    second_row = lanes((1, 1024)) // 4 % 2

    def both_row(lane):
        line = flipped[lane : lane + 1]
        line = jnp.where(second_row == 1, line, roll(line, -4, 1))
        return line.astype(jnp.int32)

    ax_row, ay_row = both_row(112), both_row(113)
    base_row = (ay_row >> 3) * 32 + ax_row
    lane = lanes((1024, 128))
    main = barrel_16(jnp.where(lane < 80, data, 0.0), step)
    side_mask = (lane >= 80) & (lane < 112 + 16 * (1 - second))
    side = barrel_16(jnp.where(side_mask, data, 0.0), side_step)
    total = None
    for part, offset in ((main, 2 * second_row), (side, 1)):
        table = jnp.where(lanes((256, 1024), 0) == base_row + offset, 1.0, 0.0).astype(BF16)
        near = split(jnp.where(stay, part, 0.0))
        far = split(jnp.where(stay, 0.0, part))
        t = dot(table, jnp.concatenate([*near, *far], axis=1))
        total = t if total is None else total + t
    near = total[:, :128] + total[:, 128:256]
    far = total[:, 256:384] + total[:, 384:]
    dens[...] = near + jnp.where(lanes((256, 128), 0) >= 32, roll(far, 32, 0), 0.0)
    for j in range(8):
        here = dens[pl.ds(32 * j, 32), :]
        density[:, pl.ds(128 * j, 128)] = here
        contrast = here - 1.0
        pull = weighted[pl.ds(32 * j, 32), :]
        for b in range(NBIN):
            pull = pull - (bias[b] * nbar[b]) * jnp.exp(bias[b] * contrast)
        pulls[pl.ds(32 * j, 32), :] = pull
    pull = pulls[...]
    ahead = jnp.where(lanes((256, 128), 0) < 224, roll(pull, -32, 0), 0.0)
    both_pulls = jnp.concatenate([*split(pull), *split(ahead)], axis=1)

    lane = lanes((256, 128))
    row_of = lanes((256, 256))
    for g, j in hand.groups():
        data = arrived[pl.ds(32 * g, 32)].reshape(256, 128)
        second, base, step, side_step, stay = geometry(data)
        parts = []
        for offset, amount in ((2 * second, step), (1, side_step)):
            wide = base + offset
            table = jnp.where(row_of == jnp.concatenate([wide, wide], axis=1), 1.0, 0.0)
            t = dot(table.astype(BF16), both_pulls)
            value = jnp.where(stay, t[:, :128] + t[:, 128:256], t[:, 256:384] + t[:, 384:])
            parts.append(barrel_16(value, (8 - amount) & 7))
        back[pl.ds(32 * g, 32)] = jnp.where(lane < 80, *parts).reshape(32, 8, 128)
        hand.group(g, j)


def forces(returned, from_slot, az, spread_t, fracs, outs, after):
    t = exact_left(from_slot[...], returned[...].reshape(1024, 128))
    amount = (16 - az) & 15
    box = jnp.concatenate([barrel(t[:256], amount), barrel(t[256:], amount)], axis=1)
    corner = exact_right(box, spread_t[...])
    fx, fy, fz = fracs[0], fracs[1], fracs[2]
    along, across = [], []
    for d in range(4):
        here = corner[:, 128 * d : 128 * (d + 1)]
        change = group_roll(here, 15) - here
        along.append(here + fz * change)
        across.append(change)
    force_x = (1.0 - fy) * (along[2] - along[0]) + fy * (along[3] - along[1])
    force_y = (1.0 - fx) * (along[1] - along[0]) + fx * (along[3] - along[2])
    force_z = (1.0 - fx) * ((1.0 - fy) * across[0] + fy * across[1]) + fx * (
        (1.0 - fy) * across[2] + fy * across[3]
    )
    piece = lanes((16, 128)) // 32
    for axis, (force, out) in enumerate(zip((force_x, force_y, force_z), outs)):
        for q in range(4):
            group = [force[16 * (4 * q + k) : 16 * (4 * q + k) + 16] for k in range(4)]
            for v in range(4):
                value = roll(group[0], -32 * v, 1)
                for k in range(1, 4):
                    value = jnp.where(piece == k, roll(group[k], 32 * (k - v), 1), value)
                out[q, pl.ds(v, 16, stride=4), :] = value
        after[axis]()


def divergence(fx, fy, fz, x_low, x_high, y_low, y_high, out, tz):
    def wide(ref):
        return jnp.concatenate([ref[q] for q in range(4)], axis=1)

    def four(value):
        return jnp.concatenate([value] * 4, axis=1)

    def edge(ref, i):
        return jnp.concatenate([ref[q, i : i + 1, :] for q in range(4)], axis=1)

    f = wide(fx)
    lane = lanes((64, 512))
    before = jnp.where(lane < 16, four(roll(x_low[...], 16, 1)), roll(f, 16, 1))
    after = jnp.where(lane >= 496, four(roll(x_high[...], 112, 1)), roll(f, -16, 1))
    total = after - before
    g = wide(fy)
    line = lanes((64, 512), 0)
    before = jnp.where(line == 0, edge(y_low, 7), roll(g, 1, 0))
    after = jnp.where(line == 63, edge(y_high, 0), roll(g, -1, 0))
    total = total + (after - before)
    h = wide(fz)
    z = lane % 16
    after = jnp.where(z == 15, roll(h, 15, 1), roll(h, -1, 1))
    before = jnp.where(z == 0, roll(h, -15, 1), roll(h, 1, 1))
    total = (total + (after - before)) * (0.5 * SECOND_ORDER)
    total = jnp.concatenate([total, jnp.zeros_like(total)], axis=0)
    for q in range(4):
        tz[pl.ds(128 * q, 128), :] = jnp.transpose(total[:, 128 * q : 128 * (q + 1)])
    for z in range(NZ):
        value = tz[pl.ds(z, 32, stride=16), :]
        out[z] = jnp.where(
            lanes((16, 128)) < 64, value[0:16], roll(value[16:32], 64, 1)
        )


def weights(kept, pulled, out, wzz, wxz, wyz):
    for z in range(NZ):
        g = pulled[z]
        wzz[z] = g * kept[2, z]
        wxz[z] = g * kept[4, z]
        wyz[z] = g * kept[5, z]
    for z in range(NZ):
        a, b = (z + 1) % 16, (z + 15) % 16
        g = pulled[z]
        wx, wy, wxy = g * kept[0, z], g * kept[1, z], g * kept[3, z]
        dx = 0.25 * (wxz[a] - wxz[b])
        dy = 0.25 * ((wyz[a] - wyz[b]) + (up(wxy, 0) - down(wxy, 0)))
        along_x = up(wx + dx, 0) + down(wx - dx, 0)
        along_y = up(wy + dy, 1) + down(wy - dy, 1)
        along_z = wzz[a] + wzz[b]
        out[z] = pack(along_x + along_y + along_z - 2.0 * (wx + wy + wzz[z]))


def finish(pulled_modes, last_modes, sums, tzh, tzl, gradient):
    slot = lanes((32, 128)) // 16
    for m in range(16):
        here = last_modes[m]
        whole = jnp.concatenate([here, roll(here, 64, 1)], axis=0)
        sums[m, 0:32, :] = pulled_modes[m, 0:32, :] * (1.0 / SECOND_ORDER) + whole
    quarters = []
    for q in range(4):
        parts = []
        for p in range(2):
            value = None
            for k in range(8):
                piece = roll(sums[8 * p + k, 0:32, :], 16 * (k - q), 1)
                value = piece if value is None else jnp.where(slot == k, piece, value)
            parts.append(value)
        quarters.append(jnp.concatenate(parts, axis=1))
    t = right_product(jnp.concatenate(quarters, axis=0), tzh[...], tzl[...])
    for q in range(4):
        gradient[:, pl.ds(256 * q, 256)] = t[32 * q : 32 * q + 32]


def columns(rows):
    stack = jnp.concatenate([r.astype(F32) for r in rows] + [jnp.zeros((124, 256), F32)], axis=0)
    turned = jnp.concatenate([jnp.transpose(stack[:, :128]), jnp.transpose(stack[:, 128:])], axis=0)
    return [turned[:, i : i + 1].astype(jnp.int32) for i in range(len(rows))]


N_TABLES = 16


def whole_kernel(nbar, bias, delta, owner, anchor_x, anchor_y, anchor_z, *refs):
    counts_far, tables = refs[0], refs[1 : 1 + N_TABLES]
    gradient, density = refs[1 + N_TABLES : 3 + N_TABLES]
    rest = list(refs[3 + N_TABLES :])

    def take(n):
        taken, rest[:] = rest[:n], rest[n:]
        return taken

    held, (counts,) = take(N_TABLES), take(1)
    buffers = [take(8) for _ in range(4)]
    first, second, pulled, total, wzz, wxz, wyz, kept = take(8)
    src, factor, fracs, tz, tt = take(5)
    payload, arrived, back, returned, dens, pulls, weighted = take(7)
    to_slot, from_slot = take(2)
    fx, fy, fz, x_low, x_high, y_low, y_high = take(7)
    table_sem, *exchange_sems, own, hand_sem, edge_sem = rest
    row, col = lax.axis_index("row"), lax.axis_index("col")
    me = row * NCOL + col
    pending = []

    def semaphores(i):
        return [s.at[i] for s in exchange_sems] + [own.at[i]]

    barrier = pltpu.get_barrier_semaphore()

    @pl.loop(1, 128)
    def _(k):
        peer = lax.rem(me + k, 128)
        pl.semaphore_signal(
            barrier,
            inc=1,
            device_id={"row": peer // NCOL, "col": lax.rem(peer, NCOL)},
            device_id_type=MESH,
        )

    loads = [
        pltpu.make_async_copy(t, h, table_sem.at[i])
        for i, (t, h) in enumerate(zip((*tables, counts_far), (*held, counts)))
    ]
    for load in loads[:4]:
        load.start()
    tzh, tzl, *main, spread, spread_t, bzh, bzl = held
    loads[0].wait()
    loads[1].wait()
    delta_modes(delta, tzh, tzl, buffers[0][0])
    for load in loads[4:]:
        load.start()
    pl.semaphore_wait(barrier, 127)

    owner_row = owner[...]
    owner_col, ax, ay, az = columns((owner_row, anchor_x[...], anchor_y[...], anchor_z[...]))

    def loaded(first_load, end):
        for load in loads[first_load:end]:
            load.wait()

    def fill_0():
        factor[...] = modes_factor(row, col)
        loaded(2, 4)

    def fill_2():
        place_tables(*slots(owner_row, owner_col), to_slot, from_slot)
        loaded(8, 10)

    place = (row, col)
    fill = (fill_0, lambda: loaded(4, 8), fill_2, lambda: loaded(10, None))
    solve(place, buffers[0], semaphores(0), main, factor, first, pending, fill)
    source(first, src)
    to_modes(src, buffers[1][0])
    fill = (
        lambda: keep_curvatures(first, kept, range(8)),
        lambda: weigh_counts(bias, counts, weighted),
        None,
        lambda: keep_curvatures(first, kept, range(8, 16)),
    )
    solve(place, buffers[1], semaphores(1), main, factor, second, pending, fill)
    hand = Handover(row, col, payload, arrived, [hand_sem.at[i] for i in range(3)])
    paint(first, second, to_slot, ax, ay, az, spread, payload, total, fracs, tz, tt, hand)
    hand.arrive(pending)
    hand = Handover(row, col, back, returned, [hand_sem.at[i] for i in range(3, 6)])
    own_cells(nbar, bias, arrived, weighted, density, back, dens, pulls, hand)
    hand.arrive(pending)
    edges = []
    after = (
        lambda: edges.extend(start_edges(row, col, 0, fx, x_low, x_high, edge_sem)),
        lambda: edges.extend(start_edges(row, col, 1, fy, y_low, y_high, edge_sem)),
        lambda: None,
    )
    forces(returned, from_slot, az, spread_t, fracs, (fx, fy, fz), after)
    for copy in edges:
        copy.wait_recv()
    pending.extend(edges)
    divergence(fx, fy, fz, x_low, x_high, y_low, y_high, src, tz)
    to_modes(src, buffers[2][0])
    solve(place, buffers[2], semaphores(2), main, factor, pulled, pending)
    weights(kept, pulled, src, wzz, wxz, wyz)
    to_modes(src, buffers[3][0])
    solve(place, buffers[3], semaphores(3), main, factor, None, pending)
    finish(buffers[2][7], buffers[3][7], total, bzh, bzl, gradient)
    for copy in pending:
        copy.wait_send()


def delta_table():
    t = np.zeros((16, 16, 16, 16))
    for y in range(16):
        t[y, :, :, y] = ZB.T
    return t.reshape(256, 256)


def spread_tables():
    spread = make_spread()
    return [spread.astype(jnp.bfloat16), spread.T.copy().astype(jnp.bfloat16)]


TABLES = [
    *two_terms(delta_table()),
    *make_tables(),
    *spread_tables(),
    *two_terms(delta_table().T.copy()),
]


def on_device(delta, counts, nbar, bias, owner, anchor_x, anchor_y, anchor_z):
    tables = [jnp.asarray(t) for t in TABLES]
    flat = [a.reshape(1, 256) for a in (owner, anchor_x, anchor_y, anchor_z)]
    field = pltpu.VMEM((NZ, XH, 128), F32)
    hand = pltpu.VMEM((128, 8, 128), F32)
    scratch = [pltpu.VMEM(t.shape, BF16) for t in tables] + [pltpu.VMEM(counts.shape, jnp.int32)]
    for i in range(4):
        deep, tall = (64, XH) if i < 3 else (32, 16)
        for s in ((NROW, 16, 128), (NCOL, 32, 128), (NCOL, deep, 128), (NROW, tall, 128)):
            scratch += [pltpu.VMEM(s, F32), pltpu.VMEM(s, F32)]
    scratch += [field] * 7 + [pltpu.VMEM((6, NZ, XH, 128), F32)]
    scratch += [pltpu.VMEM((NZ, 16, 128), F32), pltpu.VMEM((64, GRID), F32)]
    scratch += [pltpu.VMEM((3, 256, 128), F32), pltpu.VMEM((512, 128), F32)]
    scratch += [pltpu.VMEM((4, 64, 128), F32)]
    scratch += [hand] * 4 + [pltpu.VMEM((256, 128), F32)] * 3
    scratch += [pltpu.VMEM((1024, 512), BF16), pltpu.VMEM((512, 1024), BF16)]
    scratch += [pltpu.VMEM((4, 64, 128), F32)] * 3
    scratch += [pltpu.VMEM((64, 128), F32)] * 2 + [pltpu.VMEM((4, 8, 128), F32)] * 2
    scratch += [pltpu.SemaphoreType.DMA((len(tables) + 1,))]
    for n in (NROW, NCOL, NCOL, NROW):
        scratch += [pltpu.SemaphoreType.DMA((4, n)), pltpu.SemaphoreType.DMA((4, n))]
    scratch += [
        pltpu.SemaphoreType.DMA((4, 4)),
        pltpu.SemaphoreType.DMA((6,)),
        pltpu.SemaphoreType.DMA((2, 4)),
    ]
    smem = pl.BlockSpec(memory_space=pltpu.SMEM)
    return pl.pallas_call(
        whole_kernel,
        out_shape=[
            jax.ShapeDtypeStruct((CX, CY * NZ), F32),
            jax.ShapeDtypeStruct((CX, CY * NZ), F32),
        ],
        in_specs=[smem] * 2 + [VM] * 5 + [ANY] * (1 + len(tables)),
        out_specs=[VM, VM],
        scratch_shapes=scratch,
        compiler_params=pltpu.CompilerParams(
            collective_id=0, has_side_effects=True, vmem_limit_bytes=60 << 20
        ),
        name="whole",
    )(nbar, bias, delta, *flat, counts, *tables)


def solution(mesh):
    return jax.shard_map(
        on_device,
        mesh=mesh,
        in_specs=(
            P("row", "col"),
            P(None, "row", "col"),
            P(),
            P(),
            P(("row", "col"), None),
            P(("row", "col")),
            P(("row", "col")),
            P(("row", "col")),
        ),
        out_specs=(P("row", "col"), P("row", "col")),
        check_vma=False,
    )
```

```python
import functools
import math

import jax
import jax.numpy as jnp
import numpy as np
from jax import lax
from jax.experimental import pallas as pl
from jax.experimental.pallas import tpu as pltpu
from jax.sharding import PartitionSpec as P

GRID, NZ = 512, 16
NROW, NCOL = 16, 8
CX, CY = 32, 64
NBIN = 8
XH = 40
SECOND_ORDER = 3.0 / 7.0
F32, BF16 = jnp.float32, jnp.bfloat16
MESH = pl.DeviceIdType.MESH


def real_basis(n):
    k = np.arange(n)
    rows = []
    for m in range(n):
        if m == 0:
            rows.append(np.full(n, 1.0 / math.sqrt(n)))
        elif m < n // 2:
            rows.append(math.sqrt(2.0 / n) * np.cos(2 * np.pi * (m * k % n) / n))
        elif m == n // 2:
            rows.append((1.0 - 2.0 * (k % 2)) / math.sqrt(n))
        else:
            rows.append(math.sqrt(2.0 / n) * np.sin(2 * np.pi * ((m - n // 2) * k % n) / n))
    return np.stack(rows)


def two_terms(table):
    table = table.astype(np.float32)
    high = table.astype(jnp.bfloat16)
    low = (table - high.astype(np.float32)).astype(jnp.bfloat16)
    return high, low


def make_tables():
    basis = real_basis(GRID)
    r, i = np.divmod(np.arange(256), 16)
    first, second = 32 * r + i, 32 * r + 16 + i
    c, k = np.divmod(np.arange(256), 32)
    low, high = 64 * c + k, 64 * c + 32 + k
    fx = np.stack(
        [
            basis[low][:, first],
            basis[high][:, second],
            basis[high][:, first],
            basis[low][:, second],
        ]
    )
    fx = fx.reshape(4, 4, 64, 256).transpose(1, 0, 2, 3).reshape(1024, 256)
    hx = np.stack(
        [
            basis[low][:, first].T,
            basis[high][:, second].T,
            basis[low][:, second].T,
            basis[high][:, first].T,
        ]
    )
    hx = hx.reshape(4, 4, 64, 256).transpose(1, 0, 2, 3).reshape(1024, 256)
    fy = basis.T
    gy = np.zeros((GRID, NCOL, 128))
    for c in range(NCOL):
        for y in range(-2, CY + 2):
            gy[:, c, y % 128] = basis[:, (CY * c + y) % GRID]
    gx = np.zeros((NROW, XH, GRID))
    for r in range(NROW):
        for x in range(-2, CX + 2):
            gx[r, x % XH] = basis[:, (CX * r + x) % GRID]
    tables = []
    for t in (fx, fy, gy.reshape(GRID, NCOL * 128), gx.reshape(NROW * XH, GRID), hx):
        tables.extend(two_terms(t))
    return tables


ZB = real_basis(NZ)


def box_lane(a, b, z):
    if a == 0:
        return b * 16 + z
    if a == 2:
        return 128 + b * 16 + z
    return 80 + b * 16 + z if b < 3 else 208 + (b - 3) * 16 + z


def make_spread():
    e = np.zeros((4, 128, 256), np.float32)
    for dx in range(2):
        for dy in range(2):
            for v in range(4):
                for u in range(2):
                    for z in range(16):
                        e[dx * 2 + dy, 32 * v + 16 * u + z, box_lane(u + dx, v + dy, z)] = 1.0
    return e.reshape(512, 256)


def dot(a, b):
    return lax.dot_general(a, b, (((1,), (0,)), ((), ())), preferred_element_type=F32)


def dot_turned(a, b):
    return lax.dot_general(a, b, (((1,), (1,)), ((), ())), preferred_element_type=F32)


def split(x):
    high = x.astype(BF16)
    return high, (x - high.astype(F32)).astype(BF16)


def split_3(x):
    high = x.astype(BF16)
    rest = x - high.astype(F32)
    middle = rest.astype(BF16)
    return high, middle, (rest - middle.astype(F32)).astype(BF16)


def left_product(high, low, pair, last):
    n = last.shape[1]
    t = dot(high, pair)
    u = dot(low, pair)
    return t[:, :n] + ((t[:, n:] + u[:, :n]) + (u[:, n:] + dot(high, last)))


def left_terms(b):
    b0, b1, b2 = split_3(b)
    return jnp.concatenate([b0, b1], axis=1), b2


def right_product(a, high, low):
    m = a.shape[0]
    a0, a1, a2 = split_3(a)
    pair = jnp.concatenate([a0, a1], axis=0)
    t = dot(jnp.concatenate([pair, a2], axis=0), high)
    s = dot(pair, low)
    return t[:m] + ((t[m : 2 * m] + s[:m]) + (s[m:] + t[2 * m :]))


def exact_left(zero_one, b):
    n = b.shape[1]
    t = dot(zero_one, jnp.concatenate(split(b), axis=1))
    return t[:, :n] + t[:, n:]


def exact_right(a, zero_one):
    m = a.shape[0]
    t = dot(jnp.concatenate(split(a), axis=0), zero_one)
    return t[:m] + t[m:]


def lanes(shape, axis=1):
    return lax.broadcasted_iota(jnp.int32, shape, axis)


def roll(x, shift, axis):
    shift = shift % x.shape[axis]
    return x if shift == 0 else pltpu.roll(x, shift, axis)


def up(x, axis):
    return roll(x, -1, axis)


def down(x, axis):
    return roll(x, 1, axis)


def forward_z(v):
    even = [v[0]] + [v[z] + v[16 - z] for z in range(1, 8)] + [v[8]]
    odd = [None] + [v[z] - v[16 - z] for z in range(1, 8)]
    out = []
    for m in range(9):
        s = even[0] * float(ZB[m, 0])
        for z in range(1, 9):
            s = s + even[z] * float(ZB[m, z])
        out.append(s)
    for m in range(9, 16):
        s = odd[1] * float(ZB[m, 1])
        for z in range(2, 8):
            s = s + odd[z] * float(ZB[m, z])
        out.append(s)
    return out


def inverse_z(v):
    out = [None] * 16
    for z in range(9):
        even = v[0] * float(ZB[0, z])
        for m in range(1, 9):
            even = even + v[m] * float(ZB[m, z])
        if z in (0, 8):
            out[z] = even
            continue
        odd = v[9] * float(ZB[9, z])
        for m in range(10, 16):
            odd = odd + v[m] * float(ZB[m, z])
        out[z] = even + odd
        out[16 - z] = even - odd
    return out


class Exchange:
    def __init__(self, n, me, axis, src, dst, send, recv, own, pending):
        self.n, self.me, self.axis = n, me, axis
        self.src, self.dst, self.send, self.recv, self.own = src, dst, send, recv, own
        self.pending = pending

    def copy(self, peer, slot):
        return pltpu.make_async_remote_copy(
            src_ref=self.src.at[peer],
            dst_ref=self.dst.at[slot],
            send_sem=self.send.at[peer],
            recv_sem=self.recv.at[slot],
            device_id={self.axis: peer},
            device_id_type=MESH,
        )

    def start(self, peer):
        copy = self.copy(peer, self.me)
        copy.start()
        self.pending.append(copy)

    def group(self, g, j, size):
        if j:
            for e in range(size):
                self.start(g * size + e)
            return
        for e in range(1, size):
            self.start(g * size + lax.rem(lax.rem(self.me, size) + e, size))
        self.local = pltpu.make_async_copy(
            self.src.at[self.me], self.dst.at[self.me], self.own
        )
        self.local.start()

    def arrive(self):
        self.local.wait()
        for k in range(1, self.n):
            origin = lax.rem(self.me + k, self.n)
            self.copy(origin, origin).wait_recv()


ORDER = (2, 1, 3, 0)


def modes_factor(row, col):
    kx = lanes((64, GRID), 0) + col * 64
    ky = lanes((64, GRID), 1)
    kx = jnp.where(kx <= GRID // 2, kx, kx - GRID // 2).astype(F32) * (2.0 * math.pi / GRID)
    ky = jnp.where(ky <= GRID // 2, ky, ky - GRID // 2).astype(F32) * (2.0 * math.pi / GRID)
    kz = jnp.where(row <= NZ // 2, row, row - NZ // 2)
    kz = jnp.full((64, GRID), kz, jnp.int32).astype(F32) * (2.0 * math.pi / NZ)
    square = kx * kx + ky * ky + kz * kz
    return jnp.where(square > 0, -1.0 / jnp.where(square > 0, square, 1.0), 0.0)


def solve(place, buffers, semaphores, held, factor, out, pending, fill=(None,) * 4):
    row, col = place
    mo, r1, pk, r2, zb, r3, xb, r4 = buffers
    s1, q1, s2, q2, s3, q3, s4, q4, own = semaphores
    fxh, fxl, fyh, fyl, gyh, gyl, gxh, gxl, hxh, hxl = held
    def groups(me, size):
        return [(lax.rem(lax.div(me, size) + j, 4), j) for j in ORDER]

    swap = Exchange(NROW, row, "row", mo, r1, s1, q1, own.at[0], pending)
    for g, j in groups(row, 4):
        swap.group(g, j, 4)
    if fill[0]:
        fill[0]()
    swap.arrive()

    swap = Exchange(NCOL, col, "col", pk, r2, s2, q2, own.at[1], pending)
    pair, last = left_terms(r1[...].reshape(256, 128))
    low_half = lanes((64, 128)) < 64
    for g, j in groups(col, 2):
        rows = pl.ds(pl.multiple_of(256 * g, 256), 256)
        t = left_product(fxh[rows, :], fxl[rows, :], pair, last)
        packed = jnp.where(low_half, t[:64], t[64:128]) + roll(
            jnp.where(low_half, t[128:192], t[192:]), 64, 1
        )
        pk[pl.ds(2 * g, 2)] = packed.reshape(2, 32, 128)
        swap.group(g, j, 2)
    if fill[1]:
        fill[1]()
    swap.arrive()

    half = lanes((32, 128)) < 64
    top, bottom = [], []
    for p in range(4):
        a, b = r2[2 * p], r2[2 * p + 1]
        top.append(jnp.where(half, a, roll(b, 64, 1)))
        bottom.append(jnp.where(half, roll(a, 64, 1), b))
    full = jnp.concatenate(
        [jnp.concatenate(top, axis=1), jnp.concatenate(bottom, axis=1)], axis=0
    )
    modes = right_product(full, fyh[...], fyl[...]) * factor[...]
    swap = Exchange(NCOL, col, "col", zb, r3, s3, q3, own.at[2], pending)
    pair = jnp.concatenate(split_3(modes), axis=0)
    for g, j in groups(col, 2) if out is None else ():
        rows = pl.ds(pl.multiple_of(128 * g, 128), 128)
        t = dot_turned(pair, fyh[rows, :])
        u = dot_turned(pair[:128], fyl[rows, :])
        back = t[:64] + ((t[64:128] + u[:64]) + (u[64:] + t[128:]))
        a, b = back[:32], back[32:]
        zb[2 * g] = jnp.where(half, a, roll(b, 64, 1))
        zb[2 * g + 1] = jnp.where(half, roll(a, 64, 1), b)
        swap.group(g, j, 2)
    for g, j in groups(col, 2) if out is not None else ():
        lane = pl.ds(pl.multiple_of(256 * g, 256), 256)
        t = dot(pair, gyh[:, lane])
        u = dot(pair[:128], gyl[:, lane])
        back = t[:64] + ((t[64:128] + u[:64]) + (u[64:] + t[128:]))
        zb[2 * g] = back[:, :128]
        zb[2 * g + 1] = back[:, 128:]
        swap.group(g, j, 2)
    if fill[2]:
        fill[2]()
    swap.arrive()

    swap = Exchange(NROW, row, "row", xb, r4, s4, q4, own.at[3], pending)
    pair, last = left_terms(r3[...].reshape(-1, 128))
    for g, j in groups(row, 4) if out is None else ():
        rows = pl.ds(pl.multiple_of(256 * g, 256), 256)
        t = left_product(hxh[rows, :], hxl[rows, :], pair, last)
        packed = jnp.where(low_half, t[:64], t[64:128]) + roll(
            jnp.where(low_half, t[128:192], t[192:]), 64, 1
        )
        xb[pl.ds(4 * g, 4)] = packed.reshape(4, 16, 128)
        swap.group(g, j, 4)
    for g, j in groups(row, 4) if out is not None else ():
        rows = pl.ds(pl.multiple_of(4 * XH * g, 4 * XH), 4 * XH)
        t = left_product(gxh[rows, :], gxl[rows, :], pair, last)
        xb[pl.ds(4 * g, 4)] = t.reshape(4, XH, 128)
        swap.group(g, j, 4)
    if fill[3]:
        fill[3]()
    swap.arrive()
    for s in range(5 if out is not None else 0):
        rows = pl.ds(8 * s, 8)
        for z, value in enumerate(inverse_z([r4[m, rows, :] for m in range(16)])):
            out[z, rows, :] = value


def to_modes(src, mo):
    for s in range(2):
        rows = pl.ds(8 * s, 8)
        for m, value in enumerate(forward_z([src[z, rows, :] for z in range(16)])):
            mo[m, rows, :] = value


def delta_modes(delta, tzh, tzl, mo):
    d = delta[...]
    t = right_product(
        jnp.concatenate([d[:, 256 * q : 256 * (q + 1)] for q in range(4)], axis=0),
        tzh[...],
        tzl[...],
    )
    slot = lanes((16, 128)) // 16
    for m in range(16):
        part = 128 * (m // 8)
        value = None
        for h in range(2):
            for q in range(4):
                piece = t[32 * q + 16 * h : 32 * q + 16 * h + 16, part : part + 128]
                piece = roll(piece, 16 * (4 * h + q - m % 8), 1)
                value = piece if value is None else jnp.where(slot == 4 * h + q, piece, value)
        mo[m] = value


class Handover:
    def __init__(self, row, col, src, dst, sems):
        self.me, self.col = row * NCOL + col, col
        self.src, self.dst = src, dst
        self.send, self.recv, self.own = sems

    def groups(self):
        return [(lax.rem(lax.div(self.me, 32) + j, 4), j) for j in ORDER]

    def group(self, g, j):
        @pl.loop(0 if j else 1, 32)
        def _(k):
            peer = 32 * g + lax.rem(lax.rem(self.me, 32) + k, 32)
            pltpu.make_async_remote_copy(
                src_ref=self.src.at[peer],
                dst_ref=self.dst.at[self.me],
                send_sem=self.send,
                recv_sem=self.recv,
                device_id={"row": lax.div(peer, NCOL), "col": lax.rem(peer, NCOL)},
                device_id_type=MESH,
            ).start()

        if j == 0:
            self.local = pltpu.make_async_copy(
                self.src.at[self.me], self.dst.at[self.me], self.own
            )
            self.local.start()

    def arrive(self, pending):
        self.local.wait()
        all_of_them = pltpu.make_async_remote_copy(
            src_ref=self.src.at[pl.ds(0, 127)],
            dst_ref=self.dst.at[pl.ds(0, 127)],
            send_sem=self.send,
            recv_sem=self.recv,
            device_id={"col": lax.rem(self.col + 1, NCOL)},
            device_id_type=MESH,
        )
        all_of_them.wait_recv()
        pending.append(all_of_them)


def start_edges(row, col, axis, field, low, high, sems):
    if axis == 0:
        n, me, name, last, first = NROW, row, "row", field.at[3], field.at[0]
    else:
        n, me, name = NCOL, col, "col"
        last, first = field.at[:, pl.ds(56, 8)], field.at[:, pl.ds(0, 8)]
    copies = []
    for i, (step, src, dst) in enumerate(((1, last, low), (n - 1, first, high))):
        copy = pltpu.make_async_remote_copy(
            src_ref=src,
            dst_ref=dst,
            send_sem=sems.at[0, 2 * axis + i],
            recv_sem=sems.at[1, 2 * axis + i],
            device_id={name: lax.rem(me + step, n)},
            device_id_type=MESH,
        )
        copy.start()
        copies.append(copy)
    return copies


VM = pl.BlockSpec(memory_space=pltpu.VMEM)
ANY = pl.BlockSpec(memory_space=pl.ANY)


def pack(f):
    return jnp.where(lanes((16, 128)) < 64, f[0:16], roll(f[16:32], 64, 1))


def curvatures(below, here, above):
    xx = up(here, 0) - 2.0 * here + down(here, 0)
    yy = up(here, 1) - 2.0 * here + down(here, 1)
    zz = above - 2.0 * here + below
    dx = up(here, 0) - down(here, 0)
    dz = above - below
    xy = (up(dx, 1) - down(dx, 1)) * 0.25
    xz = (up(dz, 0) - down(dz, 0)) * 0.25
    yz = (up(dz, 1) - down(dz, 1)) * 0.25
    return xx, yy, zz, xy, xz, yz


def source(first, out):
    for z in range(NZ):
        xx, yy, zz, xy, xz, yz = curvatures(
            first[(z + 15) % 16], first[z], first[(z + 1) % 16]
        )
        out[z] = pack(xx * (yy + zz) + yy * zz - (xy * xy + xz * xz + yz * yz))


def keep_curvatures(first, kept, zs):
    for z in zs:
        xx, yy, zz, xy, xz, yz = curvatures(
            first[(z + 15) % 16], first[z], first[(z + 1) % 16]
        )
        for i, value in enumerate((yy + zz, xx + zz, xx + yy, -2.0 * xy, -2.0 * xz, -2.0 * yz)):
            kept[i, z] = value


def group_roll(x, s):
    z = lanes(x.shape) % 16
    return jnp.where(z >= s, roll(x, s, 1), roll(x, s - 16, 1))


def barrel(x, amount):
    for bit in (1, 2, 4, 8):
        x = jnp.where((amount & bit) > 0, group_roll(x, bit), x)
    return x


def barrel_16(x, amount):
    for bit in (1, 2, 4):
        x = jnp.where((amount & bit) > 0, roll(x, 16 * bit, 1), x)
    return x


def slots(owner_row, owner_col):
    device = lanes((128, 256), 0)
    chosen_t = jnp.where(device == owner_row, 1.0, 0.0)
    order = jnp.where(lanes((256, 256), 0) < lanes((256, 256), 1), 1.0, 0.0)
    earlier_t = dot(chosen_t.astype(BF16), order.astype(BF16))
    along = jnp.sum(earlier_t * chosen_t, axis=0, keepdims=True)
    along = owner_row * 8 + along.astype(jnp.int32)
    chosen = jnp.where(lanes((256, 128)) == owner_col, 1.0, 0.0)
    order = jnp.where(lanes((256, 256), 0) > lanes((256, 256), 1), 1.0, 0.0)
    earlier = dot(order.astype(BF16), chosen.astype(BF16))
    down_ = jnp.sum(earlier * chosen, axis=1, keepdims=True)
    down_ = owner_col * 8 + down_.astype(jnp.int32)
    return along, down_


def place_tables(along, down_rows, to_slot, from_slot):
    target = jnp.concatenate([along, along + 4], axis=1)
    for i in range(4):
        rows = lanes((256, 512), 0) + 256 * i
        to_slot[pl.ds(256 * i, 256), :] = jnp.where(rows == target, 1.0, 0.0).astype(BF16)
    for i in range(2):
        table = jnp.where(lanes((256, 1024)) == down_rows + 4 * i, 1.0, 0.0)
        from_slot[pl.ds(256 * i, 256), :] = table.astype(BF16)


def paint(first, second, to_slot, ax, ay, az, spread, out, total, fracs, tz, tt, hand):
    piece = lanes((16, 128)) // 32
    for z in range(NZ):
        total[z] = first[z] + SECOND_ORDER * second[z]
    for axis in range(3):
        for z in range(NZ):
            if axis == 2:
                slope = total[(z + 1) % 16, 0:32, :] - total[(z + 15) % 16, 0:32, :]
            elif axis == 1:
                here = total[z, 0:32, :]
                slope = up(here, 1) - down(here, 1)
            else:
                here = total[z]
                slope = (up(here, 0) - down(here, 0))[0:32]
            tz[pl.ds(z, 32, stride=16), :] = 0.5 - 0.5 * slope
        for q in range(4):
            tt[q] = jnp.transpose(tz[pl.ds(128 * q, 128), :])[0:64]
        for q in range(4):
            quarter = [tt[q, pl.ds(v, 16, stride=4), :] for v in range(4)]
            for k in range(4):
                block = roll(quarter[0], -32 * k, 1)
                for v in range(1, 4):
                    block = jnp.where(piece == v, roll(quarter[v], 32 * (v - k), 1), block)
                fracs[axis, pl.ds(16 * (4 * q + k), 16), :] = block
    fx, fy, fz = fracs[0], fracs[1], fracs[2]
    fields = []
    for wx in (1.0 - fx, fx):
        for wy in (1.0 - fy, fy):
            q = wx * wy
            upper = q * fz
            fields.append(q - upper + group_roll(upper, 1))
    box = exact_right(jnp.concatenate(fields, axis=1), spread[...])
    box_0, box_1 = barrel(box[:, :128], az), barrel(box[:, 128:], az)
    lane = lanes((256, 128))
    box_1 = jnp.where(lane == 112, ax.astype(F32), box_1)
    box_1 = jnp.where(lane == 113, ay.astype(F32), box_1)
    stacked = jnp.concatenate([box_0, box_1], axis=0)
    pair = jnp.concatenate(split(stacked), axis=1)
    for g, j in hand.groups():
        t = dot(to_slot[pl.ds(pl.multiple_of(256 * g, 256), 256), :], pair)
        out[pl.ds(32 * g, 32)] = (t[:, :128] + t[:, 128:]).reshape(32, 8, 128)
        hand.group(g, j)


def weigh_counts(bias, counts, weighted):
    for j in range(8):
        value = None
        for b in range(NBIN):
            term = bias[b] * counts[b, :, pl.ds(128 * j, 128)].astype(F32)
            value = term if value is None else value + term
        weighted[pl.ds(32 * j, 32), :] = value


def geometry(data):
    n = data.shape[0]
    second = lanes((n, 128), 0) // 4 % 2

    def both(lane):
        column = jnp.broadcast_to(data[:, lane : lane + 1], (n, 128))
        return jnp.where(second == 1, column, roll(column, -4, 0)).astype(jnp.int32)

    ax, ay = both(112), both(113)
    step = ay & 7
    return (
        second,
        (ay >> 3) * 32 + ax,
        step,
        (3 * second + 3 + ay) & 7,
        lanes((n, 128)) >= step * 16,
    )


def own_cells(nbar, bias, arrived, weighted, density, back, dens, pulls, hand):
    data = arrived[...].reshape(1024, 128)
    second, base, step, side_step, stay = geometry(data)
    flipped = jnp.concatenate(
        [jnp.transpose(data[128 * i : 128 * (i + 1)]) for i in range(8)], axis=1
    )
    second_row = lanes((1, 1024)) // 4 % 2

    def both_row(lane):
        line = flipped[lane : lane + 1]
        line = jnp.where(second_row == 1, line, roll(line, -4, 1))
        return line.astype(jnp.int32)

    ax_row, ay_row = both_row(112), both_row(113)
    base_row = (ay_row >> 3) * 32 + ax_row
    lane = lanes((1024, 128))
    main = barrel_16(jnp.where(lane < 80, data, 0.0), step)
    side_mask = (lane >= 80) & (lane < 112 + 16 * (1 - second))
    side = barrel_16(jnp.where(side_mask, data, 0.0), side_step)
    total = None
    for part, offset in ((main, 2 * second_row), (side, 1)):
        table = jnp.where(lanes((256, 1024), 0) == base_row + offset, 1.0, 0.0).astype(BF16)
        near = split(jnp.where(stay, part, 0.0))
        far = split(jnp.where(stay, 0.0, part))
        t = dot(table, jnp.concatenate([*near, *far], axis=1))
        total = t if total is None else total + t
    near = total[:, :128] + total[:, 128:256]
    far = total[:, 256:384] + total[:, 384:]
    dens[...] = near + jnp.where(lanes((256, 128), 0) >= 32, roll(far, 32, 0), 0.0)
    for j in range(8):
        here = dens[pl.ds(32 * j, 32), :]
        density[:, pl.ds(128 * j, 128)] = here
        contrast = here - 1.0
        pull = weighted[pl.ds(32 * j, 32), :]
        for b in range(NBIN):
            pull = pull - (bias[b] * nbar[b]) * jnp.exp(bias[b] * contrast)
        pulls[pl.ds(32 * j, 32), :] = pull
    pull = pulls[...]
    ahead = jnp.where(lanes((256, 128), 0) < 224, roll(pull, -32, 0), 0.0)
    both_pulls = jnp.concatenate([*split(pull), *split(ahead)], axis=1)

    lane = lanes((256, 128))
    row_of = lanes((256, 256))
    for g, j in hand.groups():
        data = arrived[pl.ds(32 * g, 32)].reshape(256, 128)
        second, base, step, side_step, stay = geometry(data)
        parts = []
        for offset, amount in ((2 * second, step), (1, side_step)):
            wide = base + offset
            table = jnp.where(row_of == jnp.concatenate([wide, wide], axis=1), 1.0, 0.0)
            t = dot(table.astype(BF16), both_pulls)
            value = jnp.where(stay, t[:, :128] + t[:, 128:256], t[:, 256:384] + t[:, 384:])
            parts.append(barrel_16(value, (8 - amount) & 7))
        back[pl.ds(32 * g, 32)] = jnp.where(lane < 80, *parts).reshape(32, 8, 128)
        hand.group(g, j)


def forces(returned, from_slot, az, spread_t, fracs, outs, after):
    t = exact_left(from_slot[...], returned[...].reshape(1024, 128))
    amount = (16 - az) & 15
    box = jnp.concatenate([barrel(t[:256], amount), barrel(t[256:], amount)], axis=1)
    corner = exact_right(box, spread_t[...])
    fx, fy, fz = fracs[0], fracs[1], fracs[2]
    along, across = [], []
    for d in range(4):
        here = corner[:, 128 * d : 128 * (d + 1)]
        change = group_roll(here, 15) - here
        along.append(here + fz * change)
        across.append(change)
    force_x = (1.0 - fy) * (along[2] - along[0]) + fy * (along[3] - along[1])
    force_y = (1.0 - fx) * (along[1] - along[0]) + fx * (along[3] - along[2])
    force_z = (1.0 - fx) * ((1.0 - fy) * across[0] + fy * across[1]) + fx * (
        (1.0 - fy) * across[2] + fy * across[3]
    )
    piece = lanes((16, 128)) // 32
    for axis, (force, out) in enumerate(zip((force_x, force_y, force_z), outs)):
        for q in range(4):
            group = [force[16 * (4 * q + k) : 16 * (4 * q + k) + 16] for k in range(4)]
            for v in range(4):
                value = roll(group[0], -32 * v, 1)
                for k in range(1, 4):
                    value = jnp.where(piece == k, roll(group[k], 32 * (k - v), 1), value)
                out[q, pl.ds(v, 16, stride=4), :] = value
        after[axis]()


def divergence(fx, fy, fz, x_low, x_high, y_low, y_high, out, tz):
    def wide(ref):
        return jnp.concatenate([ref[q] for q in range(4)], axis=1)

    def four(value):
        return jnp.concatenate([value] * 4, axis=1)

    def edge(ref, i):
        return jnp.concatenate([ref[q, i : i + 1, :] for q in range(4)], axis=1)

    f = wide(fx)
    lane = lanes((64, 512))
    before = jnp.where(lane < 16, four(roll(x_low[...], 16, 1)), roll(f, 16, 1))
    after = jnp.where(lane >= 496, four(roll(x_high[...], 112, 1)), roll(f, -16, 1))
    total = after - before
    g = wide(fy)
    line = lanes((64, 512), 0)
    before = jnp.where(line == 0, edge(y_low, 7), roll(g, 1, 0))
    after = jnp.where(line == 63, edge(y_high, 0), roll(g, -1, 0))
    total = total + (after - before)
    h = wide(fz)
    z = lane % 16
    after = jnp.where(z == 15, roll(h, 15, 1), roll(h, -1, 1))
    before = jnp.where(z == 0, roll(h, -15, 1), roll(h, 1, 1))
    total = (total + (after - before)) * (0.5 * SECOND_ORDER)
    total = jnp.concatenate([total, jnp.zeros_like(total)], axis=0)
    for q in range(4):
        tz[pl.ds(128 * q, 128), :] = jnp.transpose(total[:, 128 * q : 128 * (q + 1)])
    for z in range(NZ):
        value = tz[pl.ds(z, 32, stride=16), :]
        out[z] = jnp.where(
            lanes((16, 128)) < 64, value[0:16], roll(value[16:32], 64, 1)
        )


def weights(kept, pulled, out, wzz, wxz, wyz):
    for z in range(NZ):
        g = pulled[z]
        wzz[z] = g * kept[2, z]
        wxz[z] = g * kept[4, z]
        wyz[z] = g * kept[5, z]
    for z in range(NZ):
        a, b = (z + 1) % 16, (z + 15) % 16
        g = pulled[z]
        wx, wy, wxy = g * kept[0, z], g * kept[1, z], g * kept[3, z]
        dx = 0.25 * (wxz[a] - wxz[b])
        dy = 0.25 * ((wyz[a] - wyz[b]) + (up(wxy, 0) - down(wxy, 0)))
        along_x = up(wx + dx, 0) + down(wx - dx, 0)
        along_y = up(wy + dy, 1) + down(wy - dy, 1)
        along_z = wzz[a] + wzz[b]
        out[z] = pack(along_x + along_y + along_z - 2.0 * (wx + wy + wzz[z]))


def finish(pulled_modes, last_modes, sums, tzh, tzl, gradient):
    slot = lanes((32, 128)) // 16
    for m in range(16):
        here = last_modes[m]
        whole = jnp.concatenate([here, roll(here, 64, 1)], axis=0)
        sums[m, 0:32, :] = pulled_modes[m, 0:32, :] * (1.0 / SECOND_ORDER) + whole
    quarters = []
    for q in range(4):
        parts = []
        for p in range(2):
            value = None
            for k in range(8):
                piece = roll(sums[8 * p + k, 0:32, :], 16 * (k - q), 1)
                value = piece if value is None else jnp.where(slot == k, piece, value)
            parts.append(value)
        quarters.append(jnp.concatenate(parts, axis=1))
    t = right_product(jnp.concatenate(quarters, axis=0), tzh[...], tzl[...])
    for q in range(4):
        gradient[:, pl.ds(256 * q, 256)] = t[32 * q : 32 * q + 32]


def columns(rows):
    stack = jnp.concatenate([r.astype(F32) for r in rows] + [jnp.zeros((124, 256), F32)], axis=0)
    turned = jnp.concatenate([jnp.transpose(stack[:, :128]), jnp.transpose(stack[:, 128:])], axis=0)
    return [turned[:, i : i + 1].astype(jnp.int32) for i in range(len(rows))]


N_TABLES = 16


def whole_kernel(nbar, bias, delta, owner, anchor_x, anchor_y, anchor_z, *refs):
    counts_far, tables = refs[0], refs[1 : 1 + N_TABLES]
    gradient, density = refs[1 + N_TABLES : 3 + N_TABLES]
    rest = list(refs[3 + N_TABLES :])

    def take(n):
        taken, rest[:] = rest[:n], rest[n:]
        return taken

    held, (counts,) = take(N_TABLES), take(1)
    buffers = [take(8) for _ in range(4)]
    first, second, pulled, total, wzz, wxz, wyz, kept = take(8)
    src, factor, fracs, tz, tt = take(5)
    payload, arrived, back, returned, dens, pulls, weighted = take(7)
    to_slot, from_slot = take(2)
    fx, fy, fz, x_low, x_high, y_low, y_high = take(7)
    table_sem, *exchange_sems, own, hand_sem, edge_sem = rest
    row, col = lax.axis_index("row"), lax.axis_index("col")
    me = row * NCOL + col
    pending = []

    def semaphores(i):
        return [s.at[i] for s in exchange_sems] + [own.at[i]]

    barrier = pltpu.get_barrier_semaphore()

    for n, here, axis in ((NROW, row, "row"), (NCOL, col, "col")):
        for k in range(1, n):
            pl.semaphore_signal(
                barrier,
                inc=1,
                device_id={axis: lax.rem(here + k, n)},
                device_id_type=MESH,
            )

    loads = [
        pltpu.make_async_copy(t, h, table_sem.at[i])
        for i, (t, h) in enumerate(zip((*tables, counts_far), (*held, counts)))
    ]
    for load in loads[:4]:
        load.start()
    tzh, tzl, *main, spread, spread_t, bzh, bzl = held
    loads[0].wait()
    loads[1].wait()
    delta_modes(delta, tzh, tzl, buffers[0][0])
    for load in loads[4:]:
        load.start()
    pl.semaphore_wait(barrier, NROW + NCOL - 2)

    owner_row = owner[...]
    owner_col, ax, ay, az = columns((owner_row, anchor_x[...], anchor_y[...], anchor_z[...]))

    def loaded(first_load, end):
        for load in loads[first_load:end]:
            load.wait()

    def fill_0():
        factor[...] = modes_factor(row, col)
        loaded(2, 4)

    def fill_2():
        place_tables(*slots(owner_row, owner_col), to_slot, from_slot)
        loaded(8, 10)

    place = (row, col)
    fill = (fill_0, lambda: loaded(4, 8), fill_2, lambda: loaded(10, None))
    solve(place, buffers[0], semaphores(0), main, factor, first, pending, fill)
    source(first, src)
    to_modes(src, buffers[1][0])
    fill = (
        lambda: keep_curvatures(first, kept, range(8)),
        lambda: weigh_counts(bias, counts, weighted),
        None,
        lambda: keep_curvatures(first, kept, range(8, 16)),
    )
    solve(place, buffers[1], semaphores(1), main, factor, second, pending, fill)
    hand = Handover(row, col, payload, arrived, [hand_sem.at[i] for i in range(3)])
    paint(first, second, to_slot, ax, ay, az, spread, payload, total, fracs, tz, tt, hand)
    hand.arrive(pending)
    hand = Handover(row, col, back, returned, [hand_sem.at[i] for i in range(3, 6)])
    own_cells(nbar, bias, arrived, weighted, density, back, dens, pulls, hand)
    hand.arrive(pending)
    edges = []
    after = (
        lambda: edges.extend(start_edges(row, col, 0, fx, x_low, x_high, edge_sem)),
        lambda: edges.extend(start_edges(row, col, 1, fy, y_low, y_high, edge_sem)),
        lambda: None,
    )
    forces(returned, from_slot, az, spread_t, fracs, (fx, fy, fz), after)
    for copy in edges:
        copy.wait_recv()
    pending.extend(edges)
    divergence(fx, fy, fz, x_low, x_high, y_low, y_high, src, tz)
    to_modes(src, buffers[2][0])
    solve(place, buffers[2], semaphores(2), main, factor, pulled, pending)
    weights(kept, pulled, src, wzz, wxz, wyz)
    to_modes(src, buffers[3][0])
    solve(place, buffers[3], semaphores(3), main, factor, None, pending)
    finish(buffers[2][7], buffers[3][7], total, bzh, bzl, gradient)
    for copy in pending:
        copy.wait_send()


def delta_table():
    t = np.zeros((16, 16, 16, 16))
    for y in range(16):
        t[y, :, :, y] = ZB.T
    return t.reshape(256, 256)


def spread_tables():
    spread = make_spread()
    return [spread.astype(jnp.bfloat16), spread.T.copy().astype(jnp.bfloat16)]


TABLES = [
    *two_terms(delta_table()),
    *make_tables(),
    *spread_tables(),
    *two_terms(delta_table().T.copy()),
]


def on_device(delta, counts, nbar, bias, owner, anchor_x, anchor_y, anchor_z):
    tables = [jnp.asarray(t) for t in TABLES]
    flat = [a.reshape(1, 256) for a in (owner, anchor_x, anchor_y, anchor_z)]
    field = pltpu.VMEM((NZ, XH, 128), F32)
    hand = pltpu.VMEM((128, 8, 128), F32)
    scratch = [pltpu.VMEM(t.shape, BF16) for t in tables] + [pltpu.VMEM(counts.shape, jnp.int32)]
    for i in range(4):
        deep, tall = (64, XH) if i < 3 else (32, 16)
        for s in ((NROW, 16, 128), (NCOL, 32, 128), (NCOL, deep, 128), (NROW, tall, 128)):
            scratch += [pltpu.VMEM(s, F32), pltpu.VMEM(s, F32)]
    scratch += [field] * 7 + [pltpu.VMEM((6, NZ, XH, 128), F32)]
    scratch += [pltpu.VMEM((NZ, 16, 128), F32), pltpu.VMEM((64, GRID), F32)]
    scratch += [pltpu.VMEM((3, 256, 128), F32), pltpu.VMEM((512, 128), F32)]
    scratch += [pltpu.VMEM((4, 64, 128), F32)]
    scratch += [hand] * 4 + [pltpu.VMEM((256, 128), F32)] * 3
    scratch += [pltpu.VMEM((1024, 512), BF16), pltpu.VMEM((512, 1024), BF16)]
    scratch += [pltpu.VMEM((4, 64, 128), F32)] * 3
    scratch += [pltpu.VMEM((64, 128), F32)] * 2 + [pltpu.VMEM((4, 8, 128), F32)] * 2
    scratch += [pltpu.SemaphoreType.DMA((len(tables) + 1,))]
    for n in (NROW, NCOL, NCOL, NROW):
        scratch += [pltpu.SemaphoreType.DMA((4, n)), pltpu.SemaphoreType.DMA((4, n))]
    scratch += [
        pltpu.SemaphoreType.DMA((4, 4)),
        pltpu.SemaphoreType.DMA((6,)),
        pltpu.SemaphoreType.DMA((2, 4)),
    ]
    smem = pl.BlockSpec(memory_space=pltpu.SMEM)
    return pl.pallas_call(
        whole_kernel,
        out_shape=[
            jax.ShapeDtypeStruct((CX, CY * NZ), F32),
            jax.ShapeDtypeStruct((CX, CY * NZ), F32),
        ],
        in_specs=[smem] * 2 + [VM] * 5 + [ANY] * (1 + len(tables)),
        out_specs=[VM, VM],
        scratch_shapes=scratch,
        compiler_params=pltpu.CompilerParams(
            collective_id=0, has_side_effects=True, vmem_limit_bytes=60 << 20
        ),
        name="whole",
    )(nbar, bias, delta, *flat, counts, *tables)


def solution(mesh):
    return jax.shard_map(
        on_device,
        mesh=mesh,
        in_specs=(
            P("row", "col"),
            P(None, "row", "col"),
            P(),
            P(),
            P(("row", "col"), None),
            P(("row", "col")),
            P(("row", "col")),
            P(("row", "col")),
        ),
        out_specs=(P("row", "col"), P("row", "col")),
        check_vma=False,
    )
```

```python
import functools
import math

import jax
import jax.numpy as jnp
import numpy as np
from jax import lax
from jax.experimental import pallas as pl
from jax.experimental.pallas import tpu as pltpu
from jax.sharding import PartitionSpec as P

GRID, NZ = 512, 16
NROW, NCOL = 16, 8
CX, CY = 32, 64
NBIN = 8
XH = 40
SECOND_ORDER = 3.0 / 7.0
F32, BF16 = jnp.float32, jnp.bfloat16
MESH = pl.DeviceIdType.MESH


def real_basis(n):
    k = np.arange(n)
    rows = []
    for m in range(n):
        if m == 0:
            rows.append(np.full(n, 1.0 / math.sqrt(n)))
        elif m < n // 2:
            rows.append(math.sqrt(2.0 / n) * np.cos(2 * np.pi * (m * k % n) / n))
        elif m == n // 2:
            rows.append((1.0 - 2.0 * (k % 2)) / math.sqrt(n))
        else:
            rows.append(math.sqrt(2.0 / n) * np.sin(2 * np.pi * ((m - n // 2) * k % n) / n))
    return np.stack(rows)


def two_terms(table):
    table = table.astype(np.float32)
    high = table.astype(jnp.bfloat16)
    low = (table - high.astype(np.float32)).astype(jnp.bfloat16)
    return high, low


def make_tables():
    basis = real_basis(GRID)
    r, i = np.divmod(np.arange(256), 16)
    first, second = 32 * r + i, 32 * r + 16 + i
    c, k = np.divmod(np.arange(256), 32)
    low, high = 64 * c + k, 64 * c + 32 + k
    fx = np.stack(
        [
            basis[low][:, first],
            basis[high][:, second],
            basis[high][:, first],
            basis[low][:, second],
        ]
    )
    fx = fx.reshape(4, 4, 64, 256).transpose(1, 0, 2, 3).reshape(1024, 256)
    hx = np.stack(
        [
            basis[low][:, first].T,
            basis[high][:, second].T,
            basis[low][:, second].T,
            basis[high][:, first].T,
        ]
    )
    hx = hx.reshape(4, 4, 64, 256).transpose(1, 0, 2, 3).reshape(1024, 256)
    fy = basis.T
    gy = np.zeros((GRID, NCOL, 128))
    for c in range(NCOL):
        for y in range(-2, CY + 2):
            gy[:, c, y % 128] = basis[:, (CY * c + y) % GRID]
    gx = np.zeros((NROW, XH, GRID))
    for r in range(NROW):
        for x in range(-2, CX + 2):
            gx[r, x % XH] = basis[:, (CX * r + x) % GRID]
    tables = []
    for t in (fx, fy, gy.reshape(GRID, NCOL * 128), gx.reshape(NROW * XH, GRID), hx):
        tables.extend(two_terms(t))
    return tables


ZB = real_basis(NZ)


def box_lane(a, b, z):
    if a == 0:
        return b * 16 + z
    if a == 2:
        return 128 + b * 16 + z
    return 80 + b * 16 + z if b < 3 else 208 + (b - 3) * 16 + z


def make_spread():
    e = np.zeros((4, 128, 256), np.float32)
    for dx in range(2):
        for dy in range(2):
            for v in range(4):
                for u in range(2):
                    for z in range(16):
                        e[dx * 2 + dy, 32 * v + 16 * u + z, box_lane(u + dx, v + dy, z)] = 1.0
    return e.reshape(512, 256)


def dot(a, b):
    return lax.dot_general(a, b, (((1,), (0,)), ((), ())), preferred_element_type=F32)


def dot_turned(a, b):
    return lax.dot_general(a, b, (((1,), (1,)), ((), ())), preferred_element_type=F32)


def split(x):
    high = x.astype(BF16)
    return high, (x - high.astype(F32)).astype(BF16)


def split_3(x):
    high = x.astype(BF16)
    rest = x - high.astype(F32)
    middle = rest.astype(BF16)
    return high, middle, (rest - middle.astype(F32)).astype(BF16)


def left_product(high, low, pair, last):
    m, n = high.shape[0], last.shape[1]
    t = dot(jnp.concatenate([high, low], axis=0), pair)
    u = t[m:]
    t = t[:m]
    return t[:, :n] + ((t[:, n:] + u[:, :n]) + (u[:, n:] + dot(high, last)))


def left_terms(b):
    b0, b1, b2 = split_3(b)
    return jnp.concatenate([b0, b1], axis=1), b2


def right_product(a, high, low):
    m = a.shape[0]
    a0, a1, a2 = split_3(a)
    pair = jnp.concatenate([a0, a1], axis=0)
    t = dot(jnp.concatenate([pair, a2], axis=0), high)
    s = dot(pair, low)
    return t[:m] + ((t[m : 2 * m] + s[:m]) + (s[m:] + t[2 * m :]))


def exact_left(zero_one, b):
    n = b.shape[1]
    t = dot(zero_one, jnp.concatenate(split(b), axis=1))
    return t[:, :n] + t[:, n:]


def exact_right(a, zero_one):
    m = a.shape[0]
    t = dot(jnp.concatenate(split(a), axis=0), zero_one)
    return t[:m] + t[m:]


def lanes(shape, axis=1):
    return lax.broadcasted_iota(jnp.int32, shape, axis)


def roll(x, shift, axis):
    shift = shift % x.shape[axis]
    return x if shift == 0 else pltpu.roll(x, shift, axis)


def up(x, axis):
    return roll(x, -1, axis)


def down(x, axis):
    return roll(x, 1, axis)


def forward_z(v):
    even = [v[0]] + [v[z] + v[16 - z] for z in range(1, 8)] + [v[8]]
    odd = [None] + [v[z] - v[16 - z] for z in range(1, 8)]
    out = []
    for m in range(9):
        s = even[0] * float(ZB[m, 0])
        for z in range(1, 9):
            s = s + even[z] * float(ZB[m, z])
        out.append(s)
    for m in range(9, 16):
        s = odd[1] * float(ZB[m, 1])
        for z in range(2, 8):
            s = s + odd[z] * float(ZB[m, z])
        out.append(s)
    return out


def inverse_z(v):
    out = [None] * 16
    for z in range(9):
        even = v[0] * float(ZB[0, z])
        for m in range(1, 9):
            even = even + v[m] * float(ZB[m, z])
        if z in (0, 8):
            out[z] = even
            continue
        odd = v[9] * float(ZB[9, z])
        for m in range(10, 16):
            odd = odd + v[m] * float(ZB[m, z])
        out[z] = even + odd
        out[16 - z] = even - odd
    return out


class Exchange:
    def __init__(self, n, me, axis, src, dst, send, recv, own, pending):
        self.n, self.me, self.axis = n, me, axis
        self.src, self.dst, self.send, self.recv, self.own = src, dst, send, recv, own
        self.pending = pending

    def copy(self, peer, slot):
        return pltpu.make_async_remote_copy(
            src_ref=self.src.at[peer],
            dst_ref=self.dst.at[slot],
            send_sem=self.send.at[peer],
            recv_sem=self.recv.at[slot],
            device_id={self.axis: peer},
            device_id_type=MESH,
        )

    def start(self, peer):
        copy = self.copy(peer, self.me)
        copy.start()
        self.pending.append(copy)

    def group(self, g, j, size):
        if j:
            for e in range(size):
                self.start(g * size + e)
            return
        for e in range(1, size):
            self.start(g * size + lax.rem(lax.rem(self.me, size) + e, size))
        self.local = pltpu.make_async_copy(
            self.src.at[self.me], self.dst.at[self.me], self.own
        )
        self.local.start()

    def arrive(self):
        self.local.wait()
        for k in range(1, self.n):
            origin = lax.rem(self.me + k, self.n)
            self.copy(origin, origin).wait_recv()


ORDER = (2, 1, 3, 0)


def modes_factor(row, col):
    kx = lanes((64, GRID), 0) + col * 64
    ky = lanes((64, GRID), 1)
    kx = jnp.where(kx <= GRID // 2, kx, kx - GRID // 2).astype(F32) * (2.0 * math.pi / GRID)
    ky = jnp.where(ky <= GRID // 2, ky, ky - GRID // 2).astype(F32) * (2.0 * math.pi / GRID)
    kz = jnp.where(row <= NZ // 2, row, row - NZ // 2)
    kz = jnp.full((64, GRID), kz, jnp.int32).astype(F32) * (2.0 * math.pi / NZ)
    square = kx * kx + ky * ky + kz * kz
    return jnp.where(square > 0, -1.0 / jnp.where(square > 0, square, 1.0), 0.0)


def solve(place, buffers, semaphores, held, factor, out, pending, fill=(None,) * 4):
    row, col = place
    mo, r1, pk, r2, zb, r3, xb, r4 = buffers
    s1, q1, s2, q2, s3, q3, s4, q4, own = semaphores
    fxh, fxl, fyh, fyl, gyh, gyl, gxh, gxl, hxh, hxl = held
    def groups(me, size):
        return [(lax.rem(lax.div(me, size) + j, 4), j) for j in ORDER]

    swap = Exchange(NROW, row, "row", mo, r1, s1, q1, own.at[0], pending)
    for g, j in groups(row, 4):
        swap.group(g, j, 4)
    if fill[0]:
        fill[0]()
    swap.arrive()

    swap = Exchange(NCOL, col, "col", pk, r2, s2, q2, own.at[1], pending)
    pair, last = left_terms(r1[...].reshape(256, 128))
    low_half = lanes((64, 128)) < 64
    for g, j in groups(col, 2):
        rows = pl.ds(pl.multiple_of(256 * g, 256), 256)
        t = left_product(fxh[rows, :], fxl[rows, :], pair, last)
        packed = jnp.where(low_half, t[:64], t[64:128]) + roll(
            jnp.where(low_half, t[128:192], t[192:]), 64, 1
        )
        pk[pl.ds(2 * g, 2)] = packed.reshape(2, 32, 128)
        swap.group(g, j, 2)
    if fill[1]:
        fill[1]()
    swap.arrive()

    half = lanes((32, 128)) < 64
    top, bottom = [], []
    for p in range(4):
        a, b = r2[2 * p], r2[2 * p + 1]
        top.append(jnp.where(half, a, roll(b, 64, 1)))
        bottom.append(jnp.where(half, roll(a, 64, 1), b))
    full = jnp.concatenate(
        [jnp.concatenate(top, axis=1), jnp.concatenate(bottom, axis=1)], axis=0
    )
    modes = right_product(full, fyh[...], fyl[...]) * factor[...]
    swap = Exchange(NCOL, col, "col", zb, r3, s3, q3, own.at[2], pending)
    pair = jnp.concatenate(split_3(modes), axis=0)
    for g, j in groups(col, 2) if out is None else ():
        rows = pl.ds(pl.multiple_of(128 * g, 128), 128)
        t = dot_turned(pair, fyh[rows, :])
        u = dot_turned(pair[:128], fyl[rows, :])
        back = t[:64] + ((t[64:128] + u[:64]) + (u[64:] + t[128:]))
        a, b = back[:32], back[32:]
        zb[2 * g] = jnp.where(half, a, roll(b, 64, 1))
        zb[2 * g + 1] = jnp.where(half, roll(a, 64, 1), b)
        swap.group(g, j, 2)
    for g, j in groups(col, 2) if out is not None else ():
        lane = pl.ds(pl.multiple_of(256 * g, 256), 256)
        t = dot(pair, gyh[:, lane])
        u = dot(pair[:128], gyl[:, lane])
        back = t[:64] + ((t[64:128] + u[:64]) + (u[64:] + t[128:]))
        zb[2 * g] = back[:, :128]
        zb[2 * g + 1] = back[:, 128:]
        swap.group(g, j, 2)
    if fill[2]:
        fill[2]()
    swap.arrive()

    swap = Exchange(NROW, row, "row", xb, r4, s4, q4, own.at[3], pending)
    pair, last = left_terms(r3[...].reshape(-1, 128))
    for g, j in groups(row, 4) if out is None else ():
        rows = pl.ds(pl.multiple_of(256 * g, 256), 256)
        t = left_product(hxh[rows, :], hxl[rows, :], pair, last)
        packed = jnp.where(low_half, t[:64], t[64:128]) + roll(
            jnp.where(low_half, t[128:192], t[192:]), 64, 1
        )
        xb[pl.ds(4 * g, 4)] = packed.reshape(4, 16, 128)
        swap.group(g, j, 4)
    for g, j in groups(row, 4) if out is not None else ():
        rows = pl.ds(pl.multiple_of(4 * XH * g, 4 * XH), 4 * XH)
        t = left_product(gxh[rows, :], gxl[rows, :], pair, last)
        xb[pl.ds(4 * g, 4)] = t.reshape(4, XH, 128)
        swap.group(g, j, 4)
    if fill[3]:
        fill[3]()
    swap.arrive()
    for s in range(5 if out is not None else 0):
        rows = pl.ds(8 * s, 8)
        for z, value in enumerate(inverse_z([r4[m, rows, :] for m in range(16)])):
            out[z, rows, :] = value


def to_modes(src, mo):
    for s in range(2):
        rows = pl.ds(8 * s, 8)
        for m, value in enumerate(forward_z([src[z, rows, :] for z in range(16)])):
            mo[m, rows, :] = value


def delta_modes(delta, tzh, tzl, mo):
    d = delta[...]
    t = right_product(
        jnp.concatenate([d[:, 256 * q : 256 * (q + 1)] for q in range(4)], axis=0),
        tzh[...],
        tzl[...],
    )
    slot = lanes((16, 128)) // 16
    for m in range(16):
        part = 128 * (m // 8)
        value = None
        for h in range(2):
            for q in range(4):
                piece = t[32 * q + 16 * h : 32 * q + 16 * h + 16, part : part + 128]
                piece = roll(piece, 16 * (4 * h + q - m % 8), 1)
                value = piece if value is None else jnp.where(slot == 4 * h + q, piece, value)
        mo[m] = value


class Handover:
    def __init__(self, row, col, src, dst, sems):
        self.me, self.col = row * NCOL + col, col
        self.src, self.dst = src, dst
        self.send, self.recv, self.own = sems

    def groups(self):
        return [(lax.rem(lax.div(self.me, 32) + j, 4), j) for j in ORDER]

    def group(self, g, j):
        @pl.loop(0 if j else 1, 32)
        def _(k):
            peer = 32 * g + lax.rem(lax.rem(self.me, 32) + k, 32)
            pltpu.make_async_remote_copy(
                src_ref=self.src.at[peer],
                dst_ref=self.dst.at[self.me],
                send_sem=self.send,
                recv_sem=self.recv,
                device_id={"row": lax.div(peer, NCOL), "col": lax.rem(peer, NCOL)},
                device_id_type=MESH,
            ).start()

        if j == 0:
            self.local = pltpu.make_async_copy(
                self.src.at[self.me], self.dst.at[self.me], self.own
            )
            self.local.start()

    def arrive(self, pending):
        self.local.wait()
        all_of_them = pltpu.make_async_remote_copy(
            src_ref=self.src.at[pl.ds(0, 127)],
            dst_ref=self.dst.at[pl.ds(0, 127)],
            send_sem=self.send,
            recv_sem=self.recv,
            device_id={"col": lax.rem(self.col + 1, NCOL)},
            device_id_type=MESH,
        )
        all_of_them.wait_recv()
        pending.append(all_of_them)


def start_edges(row, col, axis, field, low, high, sems):
    if axis == 0:
        n, me, name, last, first = NROW, row, "row", field.at[3], field.at[0]
    else:
        n, me, name = NCOL, col, "col"
        last, first = field.at[:, pl.ds(56, 8)], field.at[:, pl.ds(0, 8)]
    copies = []
    for i, (step, src, dst) in enumerate(((1, last, low), (n - 1, first, high))):
        copy = pltpu.make_async_remote_copy(
            src_ref=src,
            dst_ref=dst,
            send_sem=sems.at[0, 2 * axis + i],
            recv_sem=sems.at[1, 2 * axis + i],
            device_id={name: lax.rem(me + step, n)},
            device_id_type=MESH,
        )
        copy.start()
        copies.append(copy)
    return copies


VM = pl.BlockSpec(memory_space=pltpu.VMEM)
ANY = pl.BlockSpec(memory_space=pl.ANY)


def pack(f):
    return jnp.where(lanes((16, 128)) < 64, f[0:16], roll(f[16:32], 64, 1))


def curvatures(below, here, above):
    xx = up(here, 0) - 2.0 * here + down(here, 0)
    yy = up(here, 1) - 2.0 * here + down(here, 1)
    zz = above - 2.0 * here + below
    dx = up(here, 0) - down(here, 0)
    dz = above - below
    xy = (up(dx, 1) - down(dx, 1)) * 0.25
    xz = (up(dz, 0) - down(dz, 0)) * 0.25
    yz = (up(dz, 1) - down(dz, 1)) * 0.25
    return xx, yy, zz, xy, xz, yz


def source(first, out):
    for z in range(NZ):
        xx, yy, zz, xy, xz, yz = curvatures(
            first[(z + 15) % 16], first[z], first[(z + 1) % 16]
        )
        out[z] = pack(xx * (yy + zz) + yy * zz - (xy * xy + xz * xz + yz * yz))


def keep_curvatures(first, kept, zs):
    for z in zs:
        xx, yy, zz, xy, xz, yz = curvatures(
            first[(z + 15) % 16], first[z], first[(z + 1) % 16]
        )
        for i, value in enumerate((yy + zz, xx + zz, xx + yy, -2.0 * xy, -2.0 * xz, -2.0 * yz)):
            kept[i, z] = value


def group_roll(x, s):
    z = lanes(x.shape) % 16
    return jnp.where(z >= s, roll(x, s, 1), roll(x, s - 16, 1))


def barrel(x, amount):
    for bit in (1, 2, 4, 8):
        x = jnp.where((amount & bit) > 0, group_roll(x, bit), x)
    return x


def barrel_16(x, amount):
    for bit in (1, 2, 4):
        x = jnp.where((amount & bit) > 0, roll(x, 16 * bit, 1), x)
    return x


def slots(owner_row, owner_col):
    device = lanes((128, 256), 0)
    chosen_t = jnp.where(device == owner_row, 1.0, 0.0)
    order = jnp.where(lanes((256, 256), 0) < lanes((256, 256), 1), 1.0, 0.0)
    earlier_t = dot(chosen_t.astype(BF16), order.astype(BF16))
    along = jnp.sum(earlier_t * chosen_t, axis=0, keepdims=True)
    along = owner_row * 8 + along.astype(jnp.int32)
    chosen = jnp.where(lanes((256, 128)) == owner_col, 1.0, 0.0)
    order = jnp.where(lanes((256, 256), 0) > lanes((256, 256), 1), 1.0, 0.0)
    earlier = dot(order.astype(BF16), chosen.astype(BF16))
    down_ = jnp.sum(earlier * chosen, axis=1, keepdims=True)
    down_ = owner_col * 8 + down_.astype(jnp.int32)
    return along, down_


def place_tables(along, down_rows, to_slot, from_slot):
    target = jnp.concatenate([along, along + 4], axis=1)
    for i in range(4):
        rows = lanes((256, 512), 0) + 256 * i
        to_slot[pl.ds(256 * i, 256), :] = jnp.where(rows == target, 1.0, 0.0).astype(BF16)
    for i in range(2):
        table = jnp.where(lanes((256, 1024)) == down_rows + 4 * i, 1.0, 0.0)
        from_slot[pl.ds(256 * i, 256), :] = table.astype(BF16)


def paint(first, second, to_slot, ax, ay, az, spread, out, total, fracs, tz, tt, hand):
    piece = lanes((16, 128)) // 32
    for z in range(NZ):
        total[z] = first[z] + SECOND_ORDER * second[z]
    for axis in range(3):
        for z in range(NZ):
            if axis == 2:
                slope = total[(z + 1) % 16, 0:32, :] - total[(z + 15) % 16, 0:32, :]
            elif axis == 1:
                here = total[z, 0:32, :]
                slope = up(here, 1) - down(here, 1)
            else:
                here = total[z]
                slope = (up(here, 0) - down(here, 0))[0:32]
            tz[pl.ds(z, 32, stride=16), :] = 0.5 - 0.5 * slope
        for q in range(4):
            tt[q] = jnp.transpose(tz[pl.ds(128 * q, 128), :])[0:64]
        for q in range(4):
            quarter = [tt[q, pl.ds(v, 16, stride=4), :] for v in range(4)]
            for k in range(4):
                block = roll(quarter[0], -32 * k, 1)
                for v in range(1, 4):
                    block = jnp.where(piece == v, roll(quarter[v], 32 * (v - k), 1), block)
                fracs[axis, pl.ds(16 * (4 * q + k), 16), :] = block
    fx, fy, fz = fracs[0], fracs[1], fracs[2]
    fields = []
    for wx in (1.0 - fx, fx):
        for wy in (1.0 - fy, fy):
            q = wx * wy
            upper = q * fz
            fields.append(q - upper + group_roll(upper, 1))
    box = exact_right(jnp.concatenate(fields, axis=1), spread[...])
    box_0, box_1 = barrel(box[:, :128], az), barrel(box[:, 128:], az)
    lane = lanes((256, 128))
    box_1 = jnp.where(lane == 112, ax.astype(F32), box_1)
    box_1 = jnp.where(lane == 113, ay.astype(F32), box_1)
    stacked = jnp.concatenate([box_0, box_1], axis=0)
    pair = jnp.concatenate(split(stacked), axis=1)
    for g, j in hand.groups():
        t = dot(to_slot[pl.ds(pl.multiple_of(256 * g, 256), 256), :], pair)
        out[pl.ds(32 * g, 32)] = (t[:, :128] + t[:, 128:]).reshape(32, 8, 128)
        hand.group(g, j)


def weigh_counts(bias, counts, weighted):
    for j in range(8):
        value = None
        for b in range(NBIN):
            term = bias[b] * counts[b, :, pl.ds(128 * j, 128)].astype(F32)
            value = term if value is None else value + term
        weighted[pl.ds(32 * j, 32), :] = value


def geometry(data):
    n = data.shape[0]
    second = lanes((n, 128), 0) // 4 % 2

    def both(lane):
        column = jnp.broadcast_to(data[:, lane : lane + 1], (n, 128))
        return jnp.where(second == 1, column, roll(column, -4, 0)).astype(jnp.int32)

    ax, ay = both(112), both(113)
    step = ay & 7
    return (
        second,
        (ay >> 3) * 32 + ax,
        step,
        (3 * second + 3 + ay) & 7,
        lanes((n, 128)) >= step * 16,
    )


def own_cells(nbar, bias, arrived, weighted, density, back, dens, pulls, hand):
    data = arrived[...].reshape(1024, 128)
    second, base, step, side_step, stay = geometry(data)
    flipped = jnp.concatenate(
        [jnp.transpose(data[128 * i : 128 * (i + 1)]) for i in range(8)], axis=1
    )
    second_row = lanes((1, 1024)) // 4 % 2

    def both_row(lane):
        line = flipped[lane : lane + 1]
        line = jnp.where(second_row == 1, line, roll(line, -4, 1))
        return line.astype(jnp.int32)

    ax_row, ay_row = both_row(112), both_row(113)
    base_row = (ay_row >> 3) * 32 + ax_row
    lane = lanes((1024, 128))
    main = barrel_16(jnp.where(lane < 80, data, 0.0), step)
    side_mask = (lane >= 80) & (lane < 112 + 16 * (1 - second))
    side = barrel_16(jnp.where(side_mask, data, 0.0), side_step)
    total = None
    for part, offset in ((main, 2 * second_row), (side, 1)):
        table = jnp.where(lanes((256, 1024), 0) == base_row + offset, 1.0, 0.0).astype(BF16)
        near = split(jnp.where(stay, part, 0.0))
        far = split(jnp.where(stay, 0.0, part))
        t = dot(table, jnp.concatenate([*near, *far], axis=1))
        total = t if total is None else total + t
    near = total[:, :128] + total[:, 128:256]
    far = total[:, 256:384] + total[:, 384:]
    dens[...] = near + jnp.where(lanes((256, 128), 0) >= 32, roll(far, 32, 0), 0.0)
    for j in range(8):
        here = dens[pl.ds(32 * j, 32), :]
        density[:, pl.ds(128 * j, 128)] = here
        contrast = here - 1.0
        pull = weighted[pl.ds(32 * j, 32), :]
        for b in range(NBIN):
            pull = pull - (bias[b] * nbar[b]) * jnp.exp(bias[b] * contrast)
        pulls[pl.ds(32 * j, 32), :] = pull
    pull = pulls[...]
    ahead = jnp.where(lanes((256, 128), 0) < 224, roll(pull, -32, 0), 0.0)
    both_pulls = jnp.concatenate([*split(pull), *split(ahead)], axis=1)

    lane = lanes((256, 128))
    row_of = lanes((256, 256))
    for g, j in hand.groups():
        data = arrived[pl.ds(32 * g, 32)].reshape(256, 128)
        second, base, step, side_step, stay = geometry(data)
        parts = []
        for offset, amount in ((2 * second, step), (1, side_step)):
            wide = base + offset
            table = jnp.where(row_of == jnp.concatenate([wide, wide], axis=1), 1.0, 0.0)
            t = dot(table.astype(BF16), both_pulls)
            value = jnp.where(stay, t[:, :128] + t[:, 128:256], t[:, 256:384] + t[:, 384:])
            parts.append(barrel_16(value, (8 - amount) & 7))
        back[pl.ds(32 * g, 32)] = jnp.where(lane < 80, *parts).reshape(32, 8, 128)
        hand.group(g, j)


def forces(returned, from_slot, az, spread_t, fracs, outs, after):
    t = exact_left(from_slot[...], returned[...].reshape(1024, 128))
    amount = (16 - az) & 15
    box = jnp.concatenate([barrel(t[:256], amount), barrel(t[256:], amount)], axis=1)
    corner = exact_right(box, spread_t[...])
    fx, fy, fz = fracs[0], fracs[1], fracs[2]
    along, across = [], []
    for d in range(4):
        here = corner[:, 128 * d : 128 * (d + 1)]
        change = group_roll(here, 15) - here
        along.append(here + fz * change)
        across.append(change)
    force_x = (1.0 - fy) * (along[2] - along[0]) + fy * (along[3] - along[1])
    force_y = (1.0 - fx) * (along[1] - along[0]) + fx * (along[3] - along[2])
    force_z = (1.0 - fx) * ((1.0 - fy) * across[0] + fy * across[1]) + fx * (
        (1.0 - fy) * across[2] + fy * across[3]
    )
    piece = lanes((16, 128)) // 32
    for axis, (force, out) in enumerate(zip((force_x, force_y, force_z), outs)):
        for q in range(4):
            group = [force[16 * (4 * q + k) : 16 * (4 * q + k) + 16] for k in range(4)]
            for v in range(4):
                value = roll(group[0], -32 * v, 1)
                for k in range(1, 4):
                    value = jnp.where(piece == k, roll(group[k], 32 * (k - v), 1), value)
                out[q, pl.ds(v, 16, stride=4), :] = value
        after[axis]()


def divergence(fx, fy, fz, x_low, x_high, y_low, y_high, out, tz):
    def wide(ref):
        return jnp.concatenate([ref[q] for q in range(4)], axis=1)

    def four(value):
        return jnp.concatenate([value] * 4, axis=1)

    def edge(ref, i):
        return jnp.concatenate([ref[q, i : i + 1, :] for q in range(4)], axis=1)

    f = wide(fx)
    lane = lanes((64, 512))
    before = jnp.where(lane < 16, four(roll(x_low[...], 16, 1)), roll(f, 16, 1))
    after = jnp.where(lane >= 496, four(roll(x_high[...], 112, 1)), roll(f, -16, 1))
    total = after - before
    g = wide(fy)
    line = lanes((64, 512), 0)
    before = jnp.where(line == 0, edge(y_low, 7), roll(g, 1, 0))
    after = jnp.where(line == 63, edge(y_high, 0), roll(g, -1, 0))
    total = total + (after - before)
    h = wide(fz)
    z = lane % 16
    after = jnp.where(z == 15, roll(h, 15, 1), roll(h, -1, 1))
    before = jnp.where(z == 0, roll(h, -15, 1), roll(h, 1, 1))
    total = (total + (after - before)) * (0.5 * SECOND_ORDER)
    total = jnp.concatenate([total, jnp.zeros_like(total)], axis=0)
    for q in range(4):
        tz[pl.ds(128 * q, 128), :] = jnp.transpose(total[:, 128 * q : 128 * (q + 1)])
    for z in range(NZ):
        value = tz[pl.ds(z, 32, stride=16), :]
        out[z] = jnp.where(
            lanes((16, 128)) < 64, value[0:16], roll(value[16:32], 64, 1)
        )


def weights(kept, pulled, out, wzz, wxz, wyz):
    for z in range(NZ):
        g = pulled[z]
        wzz[z] = g * kept[2, z]
        wxz[z] = g * kept[4, z]
        wyz[z] = g * kept[5, z]
    for z in range(NZ):
        a, b = (z + 1) % 16, (z + 15) % 16
        g = pulled[z]
        wx, wy, wxy = g * kept[0, z], g * kept[1, z], g * kept[3, z]
        dx = 0.25 * (wxz[a] - wxz[b])
        dy = 0.25 * ((wyz[a] - wyz[b]) + (up(wxy, 0) - down(wxy, 0)))
        along_x = up(wx + dx, 0) + down(wx - dx, 0)
        along_y = up(wy + dy, 1) + down(wy - dy, 1)
        along_z = wzz[a] + wzz[b]
        out[z] = pack(along_x + along_y + along_z - 2.0 * (wx + wy + wzz[z]))


def finish(pulled_modes, last_modes, sums, tzh, tzl, gradient):
    slot = lanes((32, 128)) // 16
    for m in range(16):
        here = last_modes[m]
        whole = jnp.concatenate([here, roll(here, 64, 1)], axis=0)
        sums[m, 0:32, :] = pulled_modes[m, 0:32, :] * (1.0 / SECOND_ORDER) + whole
    quarters = []
    for q in range(4):
        parts = []
        for p in range(2):
            value = None
            for k in range(8):
                piece = roll(sums[8 * p + k, 0:32, :], 16 * (k - q), 1)
                value = piece if value is None else jnp.where(slot == k, piece, value)
            parts.append(value)
        quarters.append(jnp.concatenate(parts, axis=1))
    t = right_product(jnp.concatenate(quarters, axis=0), tzh[...], tzl[...])
    for q in range(4):
        gradient[:, pl.ds(256 * q, 256)] = t[32 * q : 32 * q + 32]


def columns(rows):
    stack = jnp.concatenate([r.astype(F32) for r in rows] + [jnp.zeros((124, 256), F32)], axis=0)
    turned = jnp.concatenate([jnp.transpose(stack[:, :128]), jnp.transpose(stack[:, 128:])], axis=0)
    return [turned[:, i : i + 1].astype(jnp.int32) for i in range(len(rows))]


N_TABLES = 16


def whole_kernel(nbar, bias, delta, owner, anchor_x, anchor_y, anchor_z, *refs):
    counts_far, tables = refs[0], refs[1 : 1 + N_TABLES]
    gradient, density = refs[1 + N_TABLES : 3 + N_TABLES]
    rest = list(refs[3 + N_TABLES :])

    def take(n):
        taken, rest[:] = rest[:n], rest[n:]
        return taken

    held, (counts,) = take(N_TABLES), take(1)
    buffers = [take(8) for _ in range(4)]
    first, second, pulled, total, wzz, wxz, wyz, kept = take(8)
    src, factor, fracs, tz, tt = take(5)
    payload, arrived, back, returned, dens, pulls, weighted = take(7)
    to_slot, from_slot = take(2)
    fx, fy, fz, x_low, x_high, y_low, y_high = take(7)
    table_sem, *exchange_sems, own, hand_sem, edge_sem = rest
    row, col = lax.axis_index("row"), lax.axis_index("col")
    me = row * NCOL + col
    pending = []

    def semaphores(i):
        return [s.at[i] for s in exchange_sems] + [own.at[i]]

    barrier = pltpu.get_barrier_semaphore()

    for n, here, axis in ((NROW, row, "row"), (NCOL, col, "col")):
        for k in range(1, n):
            pl.semaphore_signal(
                barrier,
                inc=1,
                device_id={axis: lax.rem(here + k, n)},
                device_id_type=MESH,
            )

    loads = [
        pltpu.make_async_copy(t, h, table_sem.at[i])
        for i, (t, h) in enumerate(zip((*tables, counts_far), (*held, counts)))
    ]
    for load in loads[:4]:
        load.start()
    tzh, tzl, *main, spread, spread_t, bzh, bzl = held
    loads[0].wait()
    loads[1].wait()
    delta_modes(delta, tzh, tzl, buffers[0][0])
    for load in loads[4:]:
        load.start()
    pl.semaphore_wait(barrier, NROW + NCOL - 2)

    owner_row = owner[...]
    owner_col, ax, ay, az = columns((owner_row, anchor_x[...], anchor_y[...], anchor_z[...]))

    def loaded(first_load, end):
        for load in loads[first_load:end]:
            load.wait()

    def fill_0():
        factor[...] = modes_factor(row, col)
        loaded(2, 4)

    def fill_2():
        place_tables(*slots(owner_row, owner_col), to_slot, from_slot)
        loaded(8, 10)

    place = (row, col)
    fill = (fill_0, lambda: loaded(4, 8), fill_2, lambda: loaded(10, None))
    solve(place, buffers[0], semaphores(0), main, factor, first, pending, fill)
    source(first, src)
    to_modes(src, buffers[1][0])
    solve(place, buffers[1], semaphores(1), main, factor, second, pending)
    hand = Handover(row, col, payload, arrived, [hand_sem.at[i] for i in range(3)])
    paint(first, second, to_slot, ax, ay, az, spread, payload, total, fracs, tz, tt, hand)
    weigh_counts(bias, counts, weighted)
    hand.arrive(pending)
    hand = Handover(row, col, back, returned, [hand_sem.at[i] for i in range(3, 6)])
    own_cells(nbar, bias, arrived, weighted, density, back, dens, pulls, hand)
    keep_curvatures(first, kept, range(NZ))
    hand.arrive(pending)
    edges = []
    after = (
        lambda: edges.extend(start_edges(row, col, 0, fx, x_low, x_high, edge_sem)),
        lambda: edges.extend(start_edges(row, col, 1, fy, y_low, y_high, edge_sem)),
        lambda: None,
    )
    forces(returned, from_slot, az, spread_t, fracs, (fx, fy, fz), after)
    for copy in edges:
        copy.wait_recv()
    pending.extend(edges)
    divergence(fx, fy, fz, x_low, x_high, y_low, y_high, src, tz)
    to_modes(src, buffers[2][0])
    solve(place, buffers[2], semaphores(2), main, factor, pulled, pending)
    weights(kept, pulled, src, wzz, wxz, wyz)
    to_modes(src, buffers[3][0])
    solve(place, buffers[3], semaphores(3), main, factor, None, pending)
    finish(buffers[2][7], buffers[3][7], total, bzh, bzl, gradient)
    for copy in pending:
        copy.wait_send()


def delta_table():
    t = np.zeros((16, 16, 16, 16))
    for y in range(16):
        t[y, :, :, y] = ZB.T
    return t.reshape(256, 256)


def spread_tables():
    spread = make_spread()
    return [spread.astype(jnp.bfloat16), spread.T.copy().astype(jnp.bfloat16)]


TABLES = [
    *two_terms(delta_table()),
    *make_tables(),
    *spread_tables(),
    *two_terms(delta_table().T.copy()),
]


def on_device(delta, counts, nbar, bias, owner, anchor_x, anchor_y, anchor_z):
    tables = [jnp.asarray(t) for t in TABLES]
    flat = [a.reshape(1, 256) for a in (owner, anchor_x, anchor_y, anchor_z)]
    field = pltpu.VMEM((NZ, XH, 128), F32)
    hand = pltpu.VMEM((128, 8, 128), F32)
    scratch = [pltpu.VMEM(t.shape, BF16) for t in tables] + [pltpu.VMEM(counts.shape, jnp.int32)]
    for i in range(4):
        deep, tall = (64, XH) if i < 3 else (32, 16)
        for s in ((NROW, 16, 128), (NCOL, 32, 128), (NCOL, deep, 128), (NROW, tall, 128)):
            scratch += [pltpu.VMEM(s, F32), pltpu.VMEM(s, F32)]
    scratch += [field] * 7 + [pltpu.VMEM((6, NZ, XH, 128), F32)]
    scratch += [pltpu.VMEM((NZ, 16, 128), F32), pltpu.VMEM((64, GRID), F32)]
    scratch += [pltpu.VMEM((3, 256, 128), F32), pltpu.VMEM((512, 128), F32)]
    scratch += [pltpu.VMEM((4, 64, 128), F32)]
    scratch += [hand] * 4 + [pltpu.VMEM((256, 128), F32)] * 3
    scratch += [pltpu.VMEM((1024, 512), BF16), pltpu.VMEM((512, 1024), BF16)]
    scratch += [pltpu.VMEM((4, 64, 128), F32)] * 3
    scratch += [pltpu.VMEM((64, 128), F32)] * 2 + [pltpu.VMEM((4, 8, 128), F32)] * 2
    scratch += [pltpu.SemaphoreType.DMA((len(tables) + 1,))]
    for n in (NROW, NCOL, NCOL, NROW):
        scratch += [pltpu.SemaphoreType.DMA((4, n)), pltpu.SemaphoreType.DMA((4, n))]
    scratch += [
        pltpu.SemaphoreType.DMA((4, 4)),
        pltpu.SemaphoreType.DMA((6,)),
        pltpu.SemaphoreType.DMA((2, 4)),
    ]
    smem = pl.BlockSpec(memory_space=pltpu.SMEM)
    return pl.pallas_call(
        whole_kernel,
        out_shape=[
            jax.ShapeDtypeStruct((CX, CY * NZ), F32),
            jax.ShapeDtypeStruct((CX, CY * NZ), F32),
        ],
        in_specs=[smem] * 2 + [VM] * 5 + [ANY] * (1 + len(tables)),
        out_specs=[VM, VM],
        scratch_shapes=scratch,
        compiler_params=pltpu.CompilerParams(
            collective_id=0, has_side_effects=True, vmem_limit_bytes=60 << 20
        ),
        name="whole",
    )(nbar, bias, delta, *flat, counts, *tables)


def solution(mesh):
    return jax.shard_map(
        on_device,
        mesh=mesh,
        in_specs=(
            P("row", "col"),
            P(None, "row", "col"),
            P(),
            P(),
            P(("row", "col"), None),
            P(("row", "col")),
            P(("row", "col")),
            P(("row", "col")),
        ),
        out_specs=(P("row", "col"), P("row", "col")),
        check_vma=False,
    )
```
